32 devices in a mesh: groups: 2 (over y), state: 4 (over z), type: 4 (over x, core).
Axes of the slice: x: 2, y: 2, z: 4, core: 2. Of those that a mesh axis runs over, the one named last changes fastest.
Arguments:
- value_in: bfloat16 [16384, 2048], P(('groups', 'state'), 'type'), parts along dimension 0, may hold values from -7.5 to 7.5
- cotangent: bfloat16 [16384, 2048], P(('groups', 'state'), 'type'), parts along dimension 0, may hold values from -100 to 100
- state_util: float32 [2, 16384], P(None, ('groups', 'state')), parts along dimension 1, may hold values from -300 to 300
- taste: float32 [2, 4096], P(None, ('groups', 'type')), parts along dimension 1, may hold values from -6 to 6
- tiles: bfloat16 [128, 2, 6, 128, 128], P(('groups', 'state')), parts along dimension 0, may hold values from 0 to 0.0051879883
- dest_block: int32 [128, 2, 6], P(('groups', 'state')), parts along dimension 0, may hold values from 0 to 63, as said below
- counts: int32 [128, 2], P(('groups', 'state')), parts along dimension 0, may hold values from 1 to 6
Outputs:
- value_out: float32 [16384, 2048], P(('groups', 'state'), 'type'), parts along dimension 0
- adjoint: float32 [16384, 2048], P(('groups', 'state'), 'type'), parts along dimension 0
- grad_util: float32 [2, 16384], P(None, ('groups', 'state')), parts along dimension 1
- grad_taste: float32 [2, 4096], P(None, ('groups', 'type')), parts along dimension 1
The draws below stay inside these ranges and needn't reach their ends.
There are 2 independent parts, one for each index of `groups`. The reference program is written for one: setup_inputs(seed, part) draws one part's arguments, and reference() takes and returns one part's arrays. A program takes and returns all parts, laid end to end along the dimension named above; each array names one. Nothing has to cross between parts.
Inputs may be any that keep to these rules, and one draw needn't show every extreme that they name: `dest_block`: entries at or beyond a list's count name blocks of the list's own run of 16 blocks. In each run of 16 blocks exactly 16 used entries name blocks outside the run, at most 6 of them in any one other run, and exactly 6 in some other run.
All inputs are finite; a program needn't handle non-finite values.
Results may differ from the reference program's by a relative error of at most 0.0012.
Values may be sent and summed in bfloat16 or wider, within the bound.
A program may use at most 192 MiB of HBM per device.

```python
import math
import jax
import jax.numpy as jnp
from jax import lax

B_DEV = 16
M = 6
TILE = 128
K = 2048
NB = 64
S = 8192
REMOTE = 16
CAP = 6


def integer_lists(key):
    device_count = NB // B_DEV
    entry_total = B_DEV * 2 * M
    list_total = B_DEV * 2
    count_draw = jax.random.randint(jax.random.fold_in(key, 11), (device_count * list_total,), 1, M + 1)
    high_spot = jax.random.randint(jax.random.fold_in(key, 12), (), 0, NB * 2)
    low_spot = (high_spot + 1 + jax.random.randint(jax.random.fold_in(key, 13), (), 0, NB * 2 - 1)) % (NB * 2)
    count_draw = count_draw.at[high_spot].set(M).at[low_spot].set(1)
    count_grid = count_draw.reshape(device_count, list_total)
    entry_pos = jnp.arange(entry_total, dtype=jnp.int32) % M
    list_pos = jnp.arange(entry_total, dtype=jnp.int32) // M
    used = entry_pos[None, :] < count_grid[:, list_pos]
    keys_one = jax.random.split(jax.random.fold_in(key, 14), device_count)
    ranks = jax.vmap(lambda subkey: jax.random.permutation(subkey, entry_total))(keys_one)
    score = ranks + entry_total * (1 - used.astype(jnp.int32))
    chosen = jnp.argsort(score, axis=1, stable=True)[:, :REMOTE]
    pair_total = (device_count - 1) * CAP
    hot_offset = jax.random.randint(jax.random.fold_in(key, 15), (device_count, 1), 1, device_count)
    keys_two = jax.random.split(jax.random.fold_in(key, 16), device_count)
    pair_rank = jax.vmap(lambda subkey: jax.random.permutation(subkey, pair_total))(keys_two)
    offset_of = 1 + jnp.arange(pair_total, dtype=jnp.int32) // CAP
    priority = pair_rank + pair_total * (offset_of[None, :] != hot_offset).astype(jnp.int32)
    pair_pick = jnp.argsort(priority, axis=1, stable=True)[:, :REMOTE]
    device_ids = jnp.arange(device_count, dtype=jnp.int32)[:, None]
    far_owner = (device_ids + 1 + pair_pick // CAP) % device_count
    owners = jnp.broadcast_to(device_ids, (device_count, entry_total))
    rows = jnp.broadcast_to(device_ids, (device_count, REMOTE))
    owners = owners.at[rows, chosen].set(far_owner)
    inner = jax.random.randint(jax.random.fold_in(key, 17), (device_count, entry_total), 0, B_DEV)
    dest = (owners * B_DEV + inner).reshape(NB, 2, M)
    return (dest.astype(jnp.int32), count_grid.reshape(NB, 2).astype(jnp.int32))


def draw_dest_block(key, part):
    return integer_lists(key)[0]


def draw_counts(key, part):
    return integer_lists(key)[1]


def draw_value_in(key, part):
    noise = jnp.clip(jax.random.normal(jax.random.fold_in(key, 1), (S, K), jnp.float32), -6.0, 6.0)
    offset = jax.random.uniform(jax.random.fold_in(key, 2), (NB, 1, 1), jnp.float32, -1.5, 1.5)
    value = (noise.reshape(NB, TILE, K) + offset).reshape(S, K)
    return value.astype(jnp.bfloat16)


def draw_cotangent(key, part):
    offset = jax.random.uniform(jax.random.fold_in(key, 2), (NB, 1, 1), jnp.float32, -1.5, 1.5)
    noise = jnp.clip(jax.random.normal(jax.random.fold_in(key, 1), (S, K), jnp.float32), -6.0, 6.0)
    base = (noise.reshape(NB, TILE, K) + offset).reshape(S, K)
    row_scale = jnp.exp(jax.random.uniform(jax.random.fold_in(key, 4), (S, 1), jnp.float32, 0.0, math.log(10.0)))
    col_scale = jnp.exp(jax.random.uniform(jax.random.fold_in(key, 5), (1, K), jnp.float32, 0.0, math.log(10.0)))
    return (0.1 * base * row_scale * col_scale).astype(jnp.bfloat16)


def draw_state_util(key, part):
    return jnp.clip(jax.random.normal(jax.random.fold_in(key, 1), (2, S), jnp.float32), -6.0, 6.0)


def shard_levels(stream_key, extent, pieces, low, high):
    factor_of = 1.0
    for position, parts in pieces:
        steps = jax.random.uniform(jax.random.fold_in(jax.random.fold_in(stream_key, 6), position), (parts,), jnp.float32, low / len(pieces), high / len(pieces))
        factor_of = factor_of * jnp.repeat(jnp.exp(steps), extent[position] // parts).reshape((-1,) + (1,) * (len(extent) - 1 - position))
    return factor_of


def bell_draw(rng, shape, width, reach, cuts=(), kind=jnp.bfloat16):
    array = jax.random.normal(rng, shape, jnp.float32) * width
    if len(cuts) > 0:
        array = shard_levels(rng, shape, cuts, -0.22, 0.18) * array
    return jnp.clip(array, min=-reach, max=reach).astype(kind)


def setup_inputs(seed: int = 0, part: int = 0) -> dict:
    arg_keys = jax.random.split(jax.random.key(seed), 8)
    part_splits = jax.random.split(jax.random.fold_in(arg_keys[7], part), 8)
    return {
        "value_in": draw_value_in(jax.random.fold_in(jax.random.fold_in(arg_keys[7], part), 71), part),
        "cotangent": draw_cotangent(jax.random.fold_in(jax.random.fold_in(arg_keys[7], part), 71), part),
        "state_util": draw_state_util(jax.random.fold_in(jax.random.fold_in(arg_keys[7], part), 71), part),
        "taste": bell_draw(part_splits[3], (2, K), 1.0, 6.0, ((1, 4),), jnp.float32),
        "tiles": jnp.clip(0.0051879883 * jax.random.uniform(part_splits[4], (NB, 2, M, TILE, TILE), jnp.float32) ** shard_levels(part_splits[4], (NB, 2, M, TILE, TILE), ((0, 4),), -0.2, 0.2), 0.0, 0.0051879883).astype(jnp.bfloat16),
        "dest_block": draw_dest_block(jax.random.fold_in(jax.random.fold_in(arg_keys[7], part), 71), part),
        "counts": draw_counts(jax.random.fold_in(jax.random.fold_in(arg_keys[7], part), 71), part),
    }


def reference(value_in, cotangent, state_util, taste, tiles, dest_block, counts):
    block_count = tiles.shape[0]
    entry_count = tiles.shape[2]
    tile_rows = tiles.shape[3]
    type_width = value_in.shape[1]
    state_count = value_in.shape[0]
    value_blocks = value_in.reshape(block_count, tile_rows, type_width)
    cot_blocks = cotangent.reshape(block_count, tile_rows, type_width)
    util_blocks = state_util.reshape(2, block_count, tile_rows)

    def sweep(carry, block):
        adjoint, taste_total = carry
        tile_here = tiles[block].astype(jnp.float32)
        dest_here = dest_block[block]
        used = jnp.arange(entry_count, dtype=jnp.int32)[None, :] < counts[block][:, None]
        picked = value_blocks[dest_here].astype(jnp.float32) * used[:, :, None, None].astype(jnp.float32)
        cont = jnp.einsum("amij,amjk->aik", tile_here, picked)
        util_here = lax.dynamic_index_in_dim(util_blocks, block, 1, keepdims=False)
        scores = util_here[:, :, None] + taste[:, None, :] + 0.95 * cont
        largest = jnp.max(scores, axis=0)
        value = largest + jnp.log(jnp.sum(jnp.exp(scores - largest[None]), axis=0))
        prob = jnp.exp(scores - value[None])
        grad_q = cot_blocks[block].astype(jnp.float32)[None] * prob
        grad_u = jnp.sum(grad_q, axis=2) / type_width
        scaled = lax.optimization_barrier((0.95 * grad_q).astype(jnp.bfloat16)).astype(jnp.float32)
        contrib = jnp.einsum("amij,aik->amjk", tile_here, scaled)
        contrib = contrib * used[:, :, None, None].astype(jnp.float32)
        remote = (dest_here // B_DEV) != (block // B_DEV)
        rounded = lax.optimization_barrier(contrib.astype(jnp.bfloat16)).astype(jnp.float32)
        contrib = jnp.where(remote[:, :, None, None], rounded, contrib)
        adjoint = adjoint.at[dest_here.reshape(-1)].add(contrib.reshape(-1, tile_rows, type_width))
        taste_total = taste_total + jnp.sum(grad_q, axis=1)
        return (adjoint, taste_total), (value, grad_u)

    start = (jnp.zeros((block_count, tile_rows, type_width), jnp.float32), jnp.zeros((2, type_width), jnp.float32))
    (adjoint, taste_total), (values, grad_units) = lax.scan(sweep, start, jnp.arange(block_count, dtype=jnp.int32))
    value_out = values.reshape(state_count, type_width)
    grad_util = grad_units.transpose(1, 0, 2).reshape(2, state_count)
    grad_taste = taste_total / state_count
    return value_out, adjoint.reshape(state_count, type_width), grad_util, grad_taste
```

```python
import functools

import jax
import jax.numpy as jnp
from jax import lax
from jax.experimental import pallas as pl
from jax.experimental.pallas import tpu as pltpu
from jax.sharding import PartitionSpec as P

VMEM = pltpu.VMEM
SMEM = pltpu.SMEM
MESH = pl.DeviceIdType.MESH


def smem():
    return pl.BlockSpec(memory_space=SMEM)


def whole(shape):
    return pl.BlockSpec(shape, lambda *g: (0,) * len(shape))


def plan_kernel(dims, me_ref, dest_ref, count_ref, req_ref, look_ref, from_ref, fill):
    B, A, M, D, cap = dims
    me = me_ref[0]

    def clear(p, carry):
        fill[p] = 0
        for s in range(cap):
            req_ref[p, 0, s] = -1
            from_ref[p * cap + s] = 0
        return carry

    lax.fori_loop(0, D, clear, 0)

    def lists(i, carry):
        for a in range(A):
            count = count_ref[a, i]
            for n in range(M):
                e = (i * A + a) * M + n
                dest = dest_ref[n, a, i]
                owner = lax.div(dest, B)
                block = dest - owner * B
                used = n < count
                look_ref[e] = jnp.where(used & (owner == me), block, -1)

                @pl.when(used & (owner != me))
                def _():
                    s = fill[owner]
                    fill[owner] = s + 1
                    req_ref[owner, 0, s] = block
                    from_ref[owner * cap + s] = e
                    look_ref[e] = B + owner * cap + s

        return carry

    lax.fori_loop(0, B, lists, 0)


def greet(axis, others):
    barrier = pltpu.get_barrier_semaphore()
    for ids in others:
        pl.semaphore_signal(barrier, inc=1, device_id=ids, device_id_type=MESH)
    pl.semaphore_wait(barrier, len(others))


def request_kernel(D, req_ref, out_ref, land, send, recv):
    me = lax.axis_index("state")
    peers = [{"state": lax.rem(me + k, D)} for k in range(1, D)]
    greet("state", peers)
    copies = []
    for k in range(1, D):
        c = pltpu.make_async_remote_copy(
            src_ref=req_ref.at[lax.rem(me + k, D)],
            dst_ref=land.at[k],
            send_sem=send.at[k],
            recv_sem=recv.at[k],
            device_id={"state": lax.rem(me + k, D)},
            device_id_type=MESH,
        )
        c.start()
        copies.append(c)
    for c in copies:
        c.wait()
    out_ref[me] = req_ref[me]
    for k in range(1, D):
        out_ref[lax.rem(me - k + D, D)] = land[k]


def gather_kernel(D, cap, half, want_ref, val_ref, *rest):
    outs, sem = rest[:-1], rest[-1]

    def run(h, act):
        def peer(p, carry):
            for s in range(cap):
                w = jnp.maximum(want_ref[p, 0, s], 0)
                act(
                    pltpu.make_async_copy(
                        val_ref.at[w, :, pl.ds(h * half, half)],
                        outs[h].at[p * cap + s],
                        sem.at[h, p * cap + s],
                    )
                )
            return carry

        lax.fori_loop(0, D, peer, 0)

    for h in range(len(outs)):
        run(h, lambda c: c.start())
    for h in range(len(outs)):
        run(h, lambda c: c.wait())


def transposed_dot(tile, right):
    return lax.dot_general(tile, right, (((0,), (0,)), ((), ())), preferred_element_type=jnp.float32)


def continuation(M, first, look_ref, table, tiles):
    weights, values = [], []
    for n in range(M):
        row = look_ref[first + n]
        keep = jnp.where(row >= 0, 1.0, 0.0).astype(jnp.float32)
        tile = tiles(n)
        weights.append(tile * jnp.full(tile.shape, keep, jnp.float32).astype(jnp.bfloat16))
        values.append(table[jnp.maximum(row, 0)])
    return jnp.dot(
        jnp.concatenate(weights, axis=1), jnp.concatenate(values, axis=0), preferred_element_type=jnp.float32
    )


def fetch_value_kernel(G, rows, D, look_ref, from_ref, val_ref, *rest):
    H = (len(rest) - 14) // 2
    outs, rest = rest[:H], rest[H:]
    body, lands = rest[:9], rest[9 : 9 + H - 1]
    acc, table, kept, sem, send, recv = rest[9 + H - 1 :]
    step = pl.program_id(0)
    B, C, V = val_ref.shape[0], outs[0].shape[0], outs[0].shape[2]
    cap = C // D
    me = lax.axis_index("state")

    def copy(h, k):
        to = lax.rem(me + k, D)
        land = table.at[pl.ds(B + me * cap, cap)] if h == 0 else lands[h - 1].at[pl.ds(me * cap, cap)]
        return pltpu.make_async_remote_copy(
            src_ref=outs[h].at[pl.ds(to * cap, cap)],
            dst_ref=land,
            send_sem=send.at[h, k],
            recv_sem=recv.at[h, k],
            device_id={"state": to},
            device_id_type=MESH,
        )

    @pl.when(step == 0)
    def _():
        greet("state", [{"state": lax.rem(me + k, D)} for k in range(1, D)])
        for h in range(H):
            for k in range(1, D):
                copy(h, k).start()
        own = pltpu.make_async_copy(val_ref.at[:, :, pl.ds(0, V)], table.at[pl.ds(0, B)], sem.at[0])
        mine = pltpu.make_async_copy(
            outs[0].at[pl.ds(me * cap, cap)], table.at[pl.ds(B + me * cap, cap)], sem.at[1]
        )
        own.start()
        mine.start()
        own.wait()
        mine.wait()
        for k in range(1, D):
            copy(0, k).wait()

    work(G, rows, look_ref, from_ref, *body, acc, table, kept)

    @pl.when(step == pl.num_programs(0) - 1)
    def _():
        for h in range(1, H):
            for k in range(1, D):
                copy(h, k).wait()


def value_kernel(
    G, rows, col, look_ref, from_ref, val_ref, inc_ref, tiles_ref, cot_ref, util_ref, taste_ref, *rest
):
    before_ref = rest[0]
    value_ref, scaled_ref, out_ref, gu_ref, gt_ref, acc, table, kept, sem = rest[-9:]
    step = pl.program_id(0)
    B, C, V = val_ref.shape[0], inc_ref.shape[0], inc_ref.shape[2]

    @pl.when(step == 0)
    def _():
        own = pltpu.make_async_copy(val_ref.at[:, :, pl.ds(col, V)], table.at[pl.ds(0, B)], sem.at[0])
        far = pltpu.make_async_copy(inc_ref, table.at[pl.ds(B, C)], sem.at[1])
        own.start()
        far.start()
        own.wait()
        far.wait()

    value_ref[:, :col] = before_ref[...]
    work(
        G, rows, look_ref, from_ref, tiles_ref, cot_ref, util_ref, taste_ref,
        value_ref.at[:, col:], scaled_ref, out_ref, gu_ref, gt_ref, acc, table, kept,
    )


def work(
    G, rows, look_ref, from_ref, tiles_ref, cot_ref, util_ref, taste_ref,
    value_ref, scaled_ref, out_ref, gu_ref, gt_ref, acc, table, kept,
):
    step = pl.program_id(0)
    _, A, M, R, _ = tiles_ref.shape
    C = out_ref.shape[0]

    @pl.when(step == 0)
    def _():
        gt_ref[...] = jnp.zeros_like(gt_ref)

    t0, t1 = taste_ref[0:1, :], taste_ref[1:2, :]
    for g in range(G):
        i = step * G + g
        for a in range(A):
            acc[g, a] = continuation(M, (i * A + a) * M, look_ref, table, lambda n: tiles_ref[i, a, n])
    for g in range(G):
        g0 = g1 = 0.0
        cols = [
            jnp.transpose(jnp.broadcast_to(util_ref[a : a + 1, g * R : (g + 1) * R], (R, R))) for a in range(A)
        ]
        for c in range(0, R, rows):
            at = slice(c, c + rows)
            here = slice(g * R + c, g * R + c + rows)
            q0 = cols[0][at, 0:1] + t0 + 0.95 * acc[g, 0, at, :]
            q1 = cols[1][at, 0:1] + t1 + 0.95 * acc[g, 1, at, :]
            gap = q1 - q0
            small = jnp.exp(-jnp.abs(gap))
            total = 1.0 + small
            value_ref[here, :] = jnp.maximum(q0, q1) + jnp.log(total)
            big = cot_ref[here, :].astype(jnp.float32) / total
            little = big * small
            first_wins = gap <= 0.0
            h0 = jnp.where(first_wins, big, little)
            h1 = jnp.where(first_wins, little, big)
            scaled_ref[g, 0, at, :] = (0.95 * h0).astype(jnp.bfloat16)
            scaled_ref[g, 1, at, :] = (0.95 * h1).astype(jnp.bfloat16)
            gu_ref[g, at, 0:1] = jnp.sum(h0, axis=1, keepdims=True)
            gu_ref[g, at, 1:2] = jnp.sum(h1, axis=1, keepdims=True)
            g0, g1 = g0 + h0, g1 + h1
        gt_ref[0:1, :] += jnp.sum(g0, axis=0, keepdims=True)
        gt_ref[1:2, :] += jnp.sum(g1, axis=0, keepdims=True)
    kept[pl.ds(step * G, G)] = scaled_ref[...]

    @pl.when(step == pl.num_programs(0) - 1)
    def _():
        def back(q, carry):
            for u in range(2):
                slot = q * 2 + u
                e = from_ref[slot]
                pair = lax.div(e, M)
                i = lax.div(pair, A)
                a = pair - i * A
                out_ref[slot] = transposed_dot(tiles_ref[i, a, e - pair * M], kept[i, a]).astype(jnp.bfloat16)
            return carry

        lax.fori_loop(0, C // 2, back, 0)


def back_kernel(G, A, M, look_ref, tiles_ref, scaled_ref, adj_ref):
    spare = adj_ref.shape[0] - 1
    step = pl.program_id(0)

    @pl.when(step == 0)
    def _():
        adj_ref[...] = jnp.zeros_like(adj_ref)

    for g in range(G):
        i = step * G + g
        for a in range(A):
            for n in range(M):
                block = look_ref[(i * A + a) * M + n]
                here = jnp.where((block >= 0) & (block < spare), block, spare)
                adj_ref[here] += transposed_dot(tiles_ref[g, a, n], scaled_ref[g, a])


def sums_kernel(D, T, gu_ref, gt_ref, token_ref, after_ref, ou_ref, ot_ref, lu, lt, us, ur, ts, tr):
    ms, mt = lax.axis_index("state"), lax.axis_index("type")
    peers = [{"state": lax.rem(ms + k, D)} for k in range(1, D)]
    peers += [{"type": lax.rem(mt + k, T)} for k in range(1, T)]
    greet("state", peers)
    copies = []
    for k in range(1, T):
        copies.append(
            pltpu.make_async_remote_copy(
                src_ref=gu_ref, dst_ref=lu.at[k], send_sem=us.at[k], recv_sem=ur.at[k],
                device_id={"type": lax.rem(mt + k, T)}, device_id_type=MESH,
            )
        )
    for k in range(1, D):
        copies.append(
            pltpu.make_async_remote_copy(
                src_ref=gt_ref, dst_ref=lt.at[k], send_sem=ts.at[k], recv_sem=tr.at[k],
                device_id={"state": lax.rem(ms + k, D)}, device_id_type=MESH,
            )
        )
    for c in copies:
        c.start()
    for c in copies:
        c.wait()
    lu[0] = gu_ref[...]
    lt[0] = gt_ref[...]
    u = lu[lax.rem(mt, T)]
    for j in range(1, T):
        u = u + lu[lax.rem(mt - j + T, T)]
    t = lt[lax.rem(ms, D)]
    for j in range(1, D):
        t = t + lt[lax.rem(ms - j + D, D)]
    ou_ref[...] = u
    ot_ref[...] = t


def land_kernel(D, cap, want_ref, adj_ref, ret_ref, *rest):
    out_ref, done_ref = rest[-2:]
    done_ref[0] = 0
    out_ref[...] = adj_ref[...]

    def peer(p, carry):
        for s in range(cap):
            w = want_ref[p, 0, s]

            @pl.when(w >= 0)
            def _():
                out_ref[w] += ret_ref[p * cap + s].astype(jnp.float32)

        return carry

    lax.fori_loop(0, D, peer, 0)


def local(value_in, cotangent, state_util, taste, tiles, dest_block, counts):
    B, A, M, R, _ = tiles.shape
    W = value_in.shape[1]
    D = lax.axis_size("state")
    T = lax.axis_size("type")
    cap = max(2, (B + D - 2) // (D - 1))
    E, C = B * A * M, D * cap
    f32, bf16, i32 = jnp.float32, jnp.bfloat16, jnp.int32
    shape = jax.ShapeDtypeStruct
    values = value_in.reshape(B, R, W)

    req, look, origin = pl.pallas_call(
        functools.partial(plan_kernel, (B, A, M, D, cap)),
        out_shape=(shape((D, 1, 128), i32), shape((E,), i32), shape((C,), i32)),
        in_specs=[smem()] * 3,
        out_specs=[smem()] * 3,
        scratch_shapes=[SMEM((D,), i32)],
        name="plan",
    )(lax.axis_index("state").reshape(1).astype(i32), dest_block.transpose(2, 1, 0), counts.T)

    wanted = pl.pallas_call(
        functools.partial(request_kernel, D),
        out_shape=shape((D, 1, 128), i32),
        in_specs=[pl.BlockSpec(memory_space=VMEM)],
        out_specs=pl.BlockSpec(memory_space=VMEM),
        scratch_shapes=[VMEM((D, 1, 128), i32), pltpu.SemaphoreType.DMA((D,)), pltpu.SemaphoreType.DMA((D,))],
        compiler_params=pltpu.CompilerParams(collective_id=0, has_side_effects=True),
        name="request",
    )(req)

    H = 2 if W % 256 == 0 else 1
    V = W // H
    G = 4 if B % 4 == 0 else 1
    outgoing = pl.pallas_call(
        functools.partial(gather_kernel, D, cap, V),
        out_shape=tuple(shape((C, R, V), bf16) for h in range(H)),
        in_specs=[smem(), pl.BlockSpec(memory_space=VMEM)],
        out_specs=[pl.BlockSpec(memory_space=pl.ANY)] * H,
        scratch_shapes=[pltpu.SemaphoreType.DMA((H, C))],
        name="gather",
    )(wanted, values)

    def exchange(x):
        return lax.all_to_all(
            x.reshape(D, cap, R, V), "state", split_axis=0, concat_axis=0, tiled=True
        ).reshape(C, R, V)

    incoming = []

    flops = 2 * E * R * R * W
    value = None
    gus, gts, outbound, scaleds = [], [], [], []
    any_spec = pl.BlockSpec(memory_space=pl.ANY)
    for h in range(H):
        wide = V * (h + 1)
        ins = [
            whole((B, A, M, R, R)),
            pl.BlockSpec((G * R, V), lambda i, h=h: (i, h)),
            pl.BlockSpec((A, G * R), lambda i: (0, i)),
            pl.BlockSpec((A, V), lambda i, h=h: (0, h)),
        ]
        out_shape = [
            shape((B * R, wide), f32), shape((B, A, R, V), bf16), shape((C, R, V), bf16),
            shape((B, R, A), f32), shape((A, V), f32),
        ]
        out_specs = [
            pl.BlockSpec((G * R, wide), lambda i: (i, 0)),
            pl.BlockSpec((G, A, R, V), lambda i: (i, 0, 0, 0)),
            whole((C, R, V)),
            pl.BlockSpec((G, R, A), lambda i: (i, 0, 0)),
            whole((A, V)),
        ]
        scratch = [
            VMEM((G, A, R, V), f32), VMEM((B + C, R, V), bf16), VMEM((B, A, R, V), bf16),
            pltpu.SemaphoreType.DMA((2,)),
        ]
        cost = pl.CostEstimate(flops=flops // H, bytes_accessed=(24 << 20) // H, transcendentals=3 * B * R * V)
        if h == 0:
            value, scaled, out, gu, gt, *incoming = pl.pallas_call(
                functools.partial(fetch_value_kernel, G, 32, D),
                grid=(B // G,),
                out_shape=out_shape + [shape((C, R, V), bf16)] * (H - 1),
                in_specs=[smem(), smem(), any_spec] + [any_spec] * H + ins,
                out_specs=out_specs + [any_spec] * (H - 1),
                scratch_shapes=scratch + [pltpu.SemaphoreType.DMA((H, D)), pltpu.SemaphoreType.DMA((H, D))],
                compiler_params=pltpu.CompilerParams(collective_id=2, has_side_effects=True),
                cost_estimate=cost,
                name="fetch",
            )(look, origin, values, *outgoing, tiles, cotangent, state_util, taste)
        else:
            value, scaled, out, gu, gt = pl.pallas_call(
                functools.partial(value_kernel, G, 32, h * V),
                grid=(B // G,),
                out_shape=out_shape,
                in_specs=[smem(), smem(), any_spec, any_spec] + ins
                + [pl.BlockSpec((G * R, h * V), lambda i: (i, 0))],
                out_specs=out_specs,
                scratch_shapes=scratch,
                cost_estimate=cost,
                name="value",
            )(look, origin, values, incoming[h - 1], tiles, cotangent, state_util, taste, value)
        outbound.append(out)
        scaleds.append(scaled)
        gus.append(gu)
        gts.append(gt)

    adjs = [
        pl.pallas_call(
            functools.partial(back_kernel, G, A, M),
            grid=(B // G,),
            out_shape=shape((B + 1, R, V), f32),
            in_specs=[
                smem(),
                pl.BlockSpec((G, A, M, R, R), lambda i: (i, 0, 0, 0, 0)),
                pl.BlockSpec((G, A, R, V), lambda i: (i, 0, 0, 0)),
            ],
            out_specs=whole((B + 1, R, V)),
            cost_estimate=pl.CostEstimate(flops=flops // H, bytes_accessed=(14 << 20) // H, transcendentals=0),
            name="back",
        )(look, tiles, x)
        for x in scaleds
    ]

    returned = []
    for h in range(H):
        if h > 0:
            outbound[h], adjs[h - 1] = lax.optimization_barrier((outbound[h], adjs[h - 1]))
        returned.append(exchange(outbound[h]))

    adjoint, tokens = None, []
    gu_rows = sum(gus).transpose(2, 0, 1).reshape(A, B * R) / (W * T)
    for h in range(H):
        held = [] if h == 0 else [adjoint]
        adjoint, token = pl.pallas_call(
            functools.partial(land_kernel, D, cap),
            grid=(1,),
            out_shape=(shape((B, R, W), f32), shape((1,), i32)),
            in_specs=[smem(), whole((B, R, V)), whole((C, R, V))]
            + [pl.BlockSpec(memory_space=pl.ANY)] * len(held),
            out_specs=[pl.BlockSpec((B, R, V), lambda j, h=h: (0, 0, h)), smem()],
            input_output_aliases={3 + k: k for k in range(len(held))},
            name="land",
        )(wanted, adjs[h], returned[h], *held)
        tokens.append(token)
    grad_util, grad_taste = pl.pallas_call(
        functools.partial(sums_kernel, D, T),
        out_shape=(shape((A, B * R), f32), shape((A, W), f32)),
        in_specs=[pl.BlockSpec(memory_space=VMEM)] * 2 + [smem(), pl.BlockSpec(memory_space=pl.ANY)],
        out_specs=[pl.BlockSpec(memory_space=VMEM)] * 2,
        scratch_shapes=[
            VMEM((T, A, B * R), f32), VMEM((D, A, W), f32),
            pltpu.SemaphoreType.DMA((T,)), pltpu.SemaphoreType.DMA((T,)),
            pltpu.SemaphoreType.DMA((D,)), pltpu.SemaphoreType.DMA((D,)),
        ],
        compiler_params=pltpu.CompilerParams(collective_id=1, has_side_effects=True),
        cost_estimate=pl.CostEstimate(flops=0, bytes_accessed=8 << 20, transcendentals=0),
        name="sums",
    )(gu_rows, jnp.concatenate(gts, axis=1) / (B * R * D), tokens[0], adjs[-1])

    return value, adjoint.reshape(B * R, W), grad_util, grad_taste


def meet_kernel(dims, dest_ref, count_ref, plan_ref, send_ref, mine, land, oh, ssem, rsem):
    B, A, M, D, cap, Q = dims
    f32 = jnp.float32
    y, z = lax.axis_index("groups"), lax.axis_index("state")
    q = y * D + z
    E2 = oh.shape[0]
    mine[...] = jnp.full(mine.shape, -1.0, f32)
    for n in range(M):
        mine[n * A : (n + 1) * A, 0:B] = jnp.where(n < count_ref[...], dest_ref[n], -1).astype(f32)
    land[0] = jnp.transpose(mine[...])[0:B, :]

    def member(k):
        p = lax.rem(q + k, Q)
        return {"groups": lax.div(p, D), "state": lax.rem(p, D)}

    greet("state", [member(k) for k in range(1, Q)])
    copies = [
        pltpu.make_async_remote_copy(
            src_ref=land.at[0], dst_ref=land.at[k], send_sem=ssem.at[k], recv_sem=rsem.at[k],
            device_id=member(k), device_id_type=MESH,
        )
        for k in range(1, Q)
    ]
    for c in copies:
        c.start()

    lane = lax.broadcasted_iota(jnp.int32, (B, 128), 1).astype(f32)
    oh[...] = jnp.zeros(oh.shape, f32)
    own = land[0]
    for c in range(A * M):
        oh[c * B : (c + 1) * B, :] = jnp.where(own[:, c : c + 1] == lane, 1.0, 0.0)
    for c in copies:
        c.wait()

    def need_of(table):
        total = jnp.zeros((B, 128), f32)
        for c in range(A * M):
            total = jnp.maximum(total, jnp.where(table[:, c : c + 1] == lane, 1.0, 0.0))
        return jnp.max(total, axis=0, keepdims=True)

    seg = lax.div(lax.broadcasted_iota(jnp.int32, (1, 128), 1), B)
    b = lax.broadcasted_iota(jnp.int32, (1, 128), 1).astype(f32)
    half = D // 2
    rows, needs = [], []
    for u in range(Q // D):
        g = lax.rem(y + u, Q // D)
        need = [need_of(land[lax.rem(q - (g * D + r) + Q, Q)]) for r in range(D)]
        end = jnp.where(seg < half, need[D - 1], need[0])
        gate = jnp.where(seg < half, need[half], need[half - 1]) * (1.0 - end)
        rows += [end, gate]
        if u == 0:
            needs = need
    peer = 2 * lax.div(z, 2) + 1 - lax.rem(z, 2)
    mine_need = sum(jnp.where(z == r, needs[r], 0.0) for r in range(D))
    peer_need = sum(jnp.where(peer == r, needs[r], 0.0) for r in range(D))
    at = len(rows)
    rows += [mine_need, peer_need]
    stack = jnp.concatenate(rows + [jnp.zeros((8 - len(rows), 128), f32)], axis=0)
    one = lax.broadcasted_iota(jnp.int32, (128, 128), 0)
    two = lax.broadcasted_iota(jnp.int32, (128, 128), 1)
    same = jnp.where(lax.div(one, B) == lax.div(two, B), 1.0, 0.0)
    below = jnp.where(one < two, same, 0.0)
    rank = jnp.dot(stack, below, preferred_element_type=f32)
    size = jnp.dot(stack, same, preferred_element_type=f32)
    far_any = rows[0] + rows[1]
    far_rank = jnp.where(rows[0] > 0, rank[0:1], size[0:1] + rank[1:2])
    most = size[0:1] + size[1:2]
    for u in range(1, Q // D):
        most = jnp.maximum(most, size[2 * u : 2 * u + 1] + size[2 * u + 1 : 2 * u + 2])
    near_rank, give_rank = rank[at : at + 1], rank[at + 1 : at + 2]
    first = (z * B).astype(f32)
    FX = 2 * cap
    row_of = 1.0 + jnp.where(
        seg == z,
        b - first,
        jnp.where(
            lax.div(seg, 2) == lax.div(z, 2), B + near_rank, B + cap + lax.rem(seg, 2).astype(f32) * FX + far_rank
        ),
    )

    def as_row(col):
        full = jnp.broadcast_to(col, (E2, 128))
        return jnp.concatenate(
            [jnp.transpose(full[k : k + 128, :])[0:1, :] for k in range(0, E2, 128)], axis=1
        )

    row = jnp.sum(oh[...] * row_of, axis=1, keepdims=True)
    key = jnp.where(row == 0, 200.0, jnp.where(row > B, row, row + 100.0))
    iq = lax.broadcasted_iota(jnp.int32, (E2, 1), 0)
    order = key * E2 + iq.astype(f32)
    order_row, key_row = as_row(order), as_row(key)
    pos = jnp.sum(jnp.where(order_row < order, 1.0, 0.0), axis=1, keepdims=True)
    less = jnp.sum(jnp.where(key_row < key, 1.0, 0.0), axis=1, keepdims=True)
    wide = lax.broadcasted_iota(jnp.int32, (E2, E2), 1).astype(f32)
    c = lax.div(iq, B)
    entry = ((lax.rem(iq, B) * A + lax.rem(c, A)) * M + lax.div(c, A)).astype(f32)
    move = jnp.where(pos == wide, 1.0, 0.0)
    sort_row = jnp.sum(move * entry, axis=0, keepdims=True)
    prev_row = jnp.sum(move * jnp.where(pos == less, 0.0, pos), axis=0, keepdims=True)
    look_row = jnp.sum(jnp.where(entry == wide, row, 0.0), axis=0, keepdims=True)
    row_key = jnp.where(b >= B, b + 1.0, b + 101.0)
    last = jnp.sum(jnp.where(key <= row_key, 1.0, 0.0), axis=0, keepdims=True)
    used = jnp.max(jnp.where(key == row_key, 1.0, 0.0), axis=0, keepdims=True)
    put = lambda k, v: plan_ref.__setitem__((slice(k, k + 1), slice(0, v.shape[1])), v.astype(jnp.int32))
    plan_ref[...] = jnp.zeros(plan_ref.shape, jnp.int32)
    put(0, look_row)
    put(1, sort_row)
    put(2, prev_row)
    put(3, last * used)
    put(4, jnp.where((peer_need > 0) & (seg == z), give_rank + 1.0, 0.0))
    put(5, jnp.where((far_any > 0) & (seg == z), far_rank + 1.0, 0.0))
    put(6, jnp.broadcast_to(jnp.max(most, axis=1, keepdims=True), (1, 128)))
    slot = lax.broadcasted_iota(jnp.int32, (16, 128), 0).astype(f32)
    here = jnp.where(seg == z, b - first, 0.0)
    near = jnp.sum(
        jnp.where(give_rank == slot, jnp.where(peer_need > 0, here, 0.0), 0.0), axis=1, keepdims=True
    )
    far = jnp.sum(jnp.where(far_rank == slot, jnp.where(far_any > 0, here, 0.0), 0.0), axis=1, keepdims=True)
    send_ref[0:16, :] = jnp.broadcast_to(near, (16, 128)).astype(jnp.int32)
    send_ref[16:32, :] = jnp.broadcast_to(far, (16, 128)).astype(jnp.int32)


def sweep_kernel(dims, plan, send, val, cot_hbm, tiles_hbm, util, taste, value_hbm, adj_hbm, gu_ref, gt_ref, *rest):
    B, A, M, R, V, H, D, T, cap, FX, F, G, rows = dims
    f32, bf16 = jnp.float32, jnp.bfloat16
    E, C, CH = B * A * M, cap // 2, 2
    tables, retn, retf, rest = rest[:H], rest[H : 2 * H], rest[2 * H : 3 * H], rest[3 * H :]
    (own, stn, stx, tiles, cot, vout, scaled, P, bst, rel, adj, acc, fold, gacc, gtac, lu, lt,
     lsem, vsem, asem, sn, rn, sx, rx, sf, bsn, brn, bsx, brel, brx, usem, ursem, tsem, trsem) = rest
    z, t = lax.axis_index("state"), lax.axis_index("type")
    side = lax.div(z, 2)
    spot = lax.rem(z, 2)
    peer = 2 * side + 1 - spot
    gate_to = D // 2 - side
    is_gate = (z == D // 2 - 1) | (z == D // 2)
    is_end = jnp.logical_not(is_gate)
    far0 = 2 * (1 - side)
    tail = [C] if F > cap else []

    def span(c):
        return pl.ds(cap, F - cap) if isinstance(c, int) and c == C else pl.ds(c * CH, CH)

    def remote(src, dst, s, r, device):
        return pltpu.make_async_remote_copy(
            src_ref=src, dst_ref=dst, send_sem=s, recv_sem=r, device_id={"state": device}, device_id_type=MESH
        )

    def shift(c, base):
        s = span(c)
        return pl.ds(base + s.start, s.size)

    def fwd_near(h):
        return remote(stn.at[h], tables[h].at[pl.ds(B, cap)], sn.at[h], rn.at[h], peer)

    def fwd_far(h, c, x):
        return remote(
            stx.at[h, span(c)], tables[h].at[shift(c, B + cap + x * FX)], sx.at[h, c], rx.at[h, x, c], gate_to
        )

    def fwd_pass(h, x, c):
        part = tables[h].at[shift(c, B + cap + x * FX)]
        return remote(part, part, sf.at[h, x, c], rx.at[h, x, c], peer)

    def bwd_near(h):
        return remote(bst.at[h, pl.ds(0, cap)], retn[h], bsn.at[h], brn.at[h], peer)

    def bwd_far(h, x, c):
        return remote(
            bst.at[h, shift(c, cap + x * FX)], retf[h].at[span(c)], bsx.at[h, x, c], brx.at[h, c], far0 + x
        )

    def bwd_end(h, x, c):
        return remote(
            bst.at[h, shift(c, cap + x * FX)], rel.at[h, x, span(c)], bsx.at[h, x, c], brel.at[h, x, c], peer
        )

    def cols(h):
        return pl.ds(h * V, V)

    own_copy = pltpu.make_async_copy(val, own, lsem.at[0])
    own_copy.start()
    fills = [
        pltpu.make_async_copy(val.at[:, :, cols(h)], tables[h].at[pl.ds(0, B)], lsem.at[1 + h]) for h in range(H)
    ]
    fills[0].start()
    tile_copy = pltpu.make_async_copy(tiles_hbm, tiles, lsem.at[1 + H])
    cot_copy = pltpu.make_async_copy(cot_hbm, cot, lsem.at[2 + H])
    greet(
        "state",
        [{"state": lax.rem(z + k, D)} for k in range(1, D)] + [{"type": lax.rem(t + k, T)} for k in range(1, T)],
    )
    own_copy.wait()
    for h in range(H):
        for s in range(F):
            stx[h, s] = own[send[16 + s, 0], :, h * V : (h + 1) * V]
            if s >= 2 and s % CH == 1 and s - CH < cap:
                fwd_far(h, s // CH - 1, spot).start()
        for s in range(cap):
            stn[h, s] = own[send[s, 0], :, h * V : (h + 1) * V]
        if F <= cap + 1:
            fwd_far(h, C - 1, spot).start()
        for c in tail:
            fwd_far(h, c, spot).start()
        fwd_near(h).start()
        if h == 0:
            tile_copy.start()
            cot_copy.start()
            for f in fills[1:]:
                f.start()
    P[0] = jnp.zeros((R, V), f32)
    gtac[...] = jnp.zeros(gtac.shape, f32)

    def pass_on(h, c):
        @pl.when(is_gate)
        def _():
            for x in range(2):
                fwd_far(h, c, x).wait_recv()
                fwd_pass(h, x, c).start()

    def arrived(h):
        fwd_near(h).wait_recv()

        @pl.when(is_gate)
        def _():
            for x in range(2):
                for c in tail:
                    fwd_far(h, c, x).wait_recv()

        @pl.when(is_end)
        def _():
            for x in range(2):
                for c in range(C):
                    fwd_far(h, c, x).wait_recv()

    def values(h, hook):
        t0, t1 = taste[0:1, h * V : (h + 1) * V], taste[1:2, h * V : (h + 1) * V]

        def step(k, carry):
            for g in range(G):
                i = k * G + g
                for a in range(A):
                    weights, blocks = [], []
                    for n in range(M):
                        e = (i * A + a) * M + n
                        row = plan[0, e]
                        keep = jnp.where(row > 0, 1.0, 0.0).astype(f32)
                        tile = tiles[e]
                        weights.append(tile * jnp.full(tile.shape, keep, f32).astype(bf16))
                        blocks.append(tables[h][jnp.maximum(row - 1, 0)])
                    acc[g, a] = jnp.dot(
                        jnp.concatenate(weights, axis=1), jnp.concatenate(blocks, axis=0),
                        preferred_element_type=f32,
                    )
            for g in range(G):
                i = k * G + g
                lanes = pl.ds(pl.multiple_of(i * R, R), R)
                base = [jnp.transpose(jnp.broadcast_to(util[a : a + 1, lanes], (R, R))) for a in range(A)]
                g0 = g1 = 0.0
                for c in range(0, R, rows):
                    at = slice(c, c + rows)
                    here = pl.ds(pl.multiple_of(i * R + c, rows), rows)
                    q0 = base[0][at, 0:1] + t0 + 0.95 * acc[g, 0, at, :]
                    q1 = base[1][at, 0:1] + t1 + 0.95 * acc[g, 1, at, :]
                    gap = q1 - q0
                    small = jnp.exp(-jnp.abs(gap))
                    total = 1.0 + small
                    vout[here, :] = jnp.maximum(q0, q1) + jnp.log(total)
                    big = cot[here, h * V : (h + 1) * V].astype(f32) / total
                    little = big * small
                    first_wins = gap <= 0.0
                    h0 = jnp.where(first_wins, big, little)
                    h1 = jnp.where(first_wins, little, big)
                    scaled[i * A, at, :] = (0.95 * h0).astype(bf16)
                    scaled[i * A + 1, at, :] = (0.95 * h1).astype(bf16)
                    fold[0, at, :] = sum(h0[:, w : w + 128] for w in range(0, V, 128))
                    fold[1, at, :] = sum(h1[:, w : w + 128] for w in range(0, V, 128))
                    g0, g1 = g0 + h0, g1 + h1
                for a in range(A):
                    line = jnp.sum(jnp.transpose(fold[a]), axis=0, keepdims=True)
                    gacc[a : a + 1, lanes] = line if h == 0 else gacc[a : a + 1, lanes] + line
                gtac[0:1, h * V : (h + 1) * V] += jnp.sum(g0, axis=0, keepdims=True)
                gtac[1:2, h * V : (h + 1) * V] += jnp.sum(g1, axis=0, keepdims=True)
            part = pl.ds(k * G * R, G * R)
            pltpu.make_async_copy(vout.at[part], value_hbm.at[part, cols(h)], vsem.at[k]).start()
            hook(k)
            return carry

        lax.fori_loop(0, B // G, step, 0)

    def value_done(h):
        for k in range(B // G):
            part = pl.ds(k * G * R, G * R)
            pltpu.make_async_copy(vout.at[part], value_hbm.at[part, cols(h)], vsem.at[k]).wait()

    def back(lo, hi):
        def step(k, carry):
            for u in range(B):
                e = plan[1, k * B + u]
                P[k * B + u + 1] = P[plan[2, k * B + u]] + transposed_dot(tiles[e], scaled[lax.div(e, M)])
            return carry

        lax.fori_loop(lo, hi, step, 0)

    def stage(h, s):
        bst[h, s] = P[plan[3, B + s]].astype(bf16)

    def give(h):
        @pl.when(is_end)
        def _():
            for c in range(C):
                for x in range(2):
                    for s in range(c * CH, (c + 1) * CH):
                        stage(h, cap + x * FX + s)
                if c > 0:
                    for x in range(2):
                        bwd_end(h, x, c - 1).start()

        @pl.when(is_gate)
        def _():
            for x in range(2):
                for s in range(cap, F):
                    stage(h, cap + x * FX + s)

        for s in range(cap):
            stage(h, s)

        @pl.when(is_end)
        def _():
            for x in range(2):
                bwd_end(h, x, C - 1).start()

        @pl.when(is_gate)
        def _():
            for x in range(2):
                for c in tail:
                    bwd_far(h, x, c).start()

        bwd_near(h).start()

    def add_on(h, c):
        @pl.when(is_gate)
        def _():
            for x in range(2):
                bwd_end(h, x, c).wait_recv()
                for s in range(CH):
                    u = c * CH + s
                    term = P[plan[3, B + cap + x * FX + u]] + rel[h, x, u].astype(f32)
                    bst[h, cap + x * FX + u] = term.astype(bf16)
            for x in range(2):
                bwd_far(h, x, c).start()

    def keep(h):
        def step(j, carry):
            adj[h, j] = P[plan[3, j]]
            return carry

        lax.fori_loop(0, B, step, 0)

    def adj_out(h, k):
        part = pl.ds(k * G, G)
        return pltpu.make_async_copy(adj.at[h, part], adj_hbm.at[part, :, cols(h)], asem.at[h, k])

    def land(h):
        bwd_near(h).wait_recv()
        for c in list(range(C)) + tail:
            bwd_far(h, 0, c).wait_recv()

        def step(k, carry):
            for g in range(G):
                j = k * G + g
                near, far = plan[4, z * B + j], plan[5, z * B + j]
                add = jnp.where(near > 0, retn[h][jnp.maximum(near - 1, 0)].astype(f32), 0.0)
                add += jnp.where(far > 0, retf[h][jnp.maximum(far - 1, 0)].astype(f32), 0.0)
                adj[h, j] = (adj[h, j] if h < H - 1 else P[plan[3, j]]) + add
            adj_out(h, k).start()
            return carry

        lax.fori_loop(0, B // G, step, 0)

    def sums():
        out = []
        for k in range(1, T):
            out.append(
                pltpu.make_async_remote_copy(
                    src_ref=gacc, dst_ref=lu.at[k], send_sem=usem.at[k], recv_sem=ursem.at[k],
                    device_id={"type": lax.rem(t + k, T)}, device_id_type=MESH,
                )
            )
        for k in range(1, D):
            out.append(remote(gtac, lt.at[k], tsem.at[k], trsem.at[k], lax.rem(z + k, D)))
        return out

    for c in range(C):
        pass_on(0, c)
    fills[0].wait()
    arrived(0)
    tile_copy.wait()
    cot_copy.wait()
    for h in range(H):
        steps = B // G

        def hook(k, h=h):
            @pl.when(k < C)
            def _():
                if h + 1 < H:
                    pass_on(h + 1, k)
                if h > 0:
                    add_on(h - 1, k)

        if h > 0:
            fills[h].wait()
            arrived(h)
            value_done(h - 1)
        values(h, hook)
        back(0, 1)
        give(h)
        if h == H - 1:
            for c in sums():
                c.start()
        back(1, E // B)
        if h < H - 1:
            keep(h)
        if h > 0:
            land(h - 1)
    for c in range(C):
        add_on(H - 1, c)
    for c in sums():
        c.wait()
    lu[0] = gacc[...]
    lt[0] = gtac[...]
    u = lu[lax.rem(t, T)]
    for j in range(1, T):
        u = u + lu[lax.rem(t - j + T, T)]
    w = lt[lax.rem(z, D)]
    for j in range(1, D):
        w = w + lt[lax.rem(z - j + D, D)]
    gu_ref[...] = u / (H * V * T)
    gt_ref[...] = w / (B * R * D)
    land(H - 1)
    value_done(H - 1)
    for h in range(H):
        for k in range(B // G):
            adj_out(h, k).wait()
        fwd_near(h).wait_send()
        bwd_near(h).wait_send()
        for c in list(range(C)) + tail:
            fwd_far(h, c, spot).wait_send()

        @pl.when(is_gate)
        def _(h=h):
            for x in range(2):
                for c in range(C):
                    fwd_pass(h, x, c).wait_send()
                for c in list(range(C)) + tail:
                    bwd_far(h, x, c).wait_send()

        @pl.when(is_end)
        def _(h=h):
            for x in range(2):
                for c in range(C):
                    bwd_end(h, x, c).wait_send()


def folded(value_in, cotangent, state_util, taste, tiles, dest_block, counts):
    B, A, M, R, _ = tiles.shape
    W = value_in.shape[1]
    D, T = lax.axis_size("state"), lax.axis_size("type")
    Q = lax.axis_size("groups") * D
    cap = (B + D - 2) // (D - 1)
    E, FX, H, G = B * A * M, 2 * cap, 2, 4
    V = W // H
    f32, bf16, i32 = jnp.float32, jnp.bfloat16, jnp.int32
    shape, DMA = jax.ShapeDtypeStruct, pltpu.SemaphoreType.DMA
    vmem = pl.BlockSpec(memory_space=VMEM)
    hbm = pl.BlockSpec(memory_space=pl.ANY)

    plan, send = pl.pallas_call(
        functools.partial(meet_kernel, (B, A, M, D, cap, Q)),
        out_shape=(shape((8, 256), i32), shape((32, 128), i32)),
        in_specs=[vmem] * 2,
        out_specs=[vmem] * 2,
        scratch_shapes=[VMEM((128, 128), f32), VMEM((Q, B, 128), f32), VMEM((256, 128), f32), DMA((Q,)), DMA((Q,))],
        compiler_params=pltpu.CompilerParams(collective_id=0, has_side_effects=True),
        name="meet",
    )(dest_block.transpose(2, 1, 0), counts.T)

    def sweep(F, ident):
        dims = (B, A, M, R, V, H, D, T, cap, FX, F, G, 32)
        C = cap // 2
        return pl.pallas_call(
            functools.partial(sweep_kernel, dims),
            out_shape=(
                shape((B * R, W), f32), shape((B, R, W), f32), shape((A, B * R), f32), shape((A, W), f32),
            ),
            in_specs=[smem(), smem(), hbm, hbm, hbm, vmem, vmem],
            out_specs=[hbm, hbm, vmem, vmem],
            scratch_shapes=[VMEM((B + cap + 2 * FX, R, V), bf16)] * H
            + [VMEM((cap, R, V), bf16)] * H
            + [VMEM((FX, R, V), bf16)] * H
            + [
                VMEM((B, R, W), bf16), VMEM((H, cap, R, V), bf16), VMEM((H, FX, R, V), bf16),
                VMEM((E, R, R), bf16), VMEM((B * R, W), bf16), VMEM((B * R, V), f32),
                VMEM((B * A, R, V), bf16), VMEM((E + 1, R, V), f32), VMEM((H, cap + 2 * FX, R, V), bf16),
                VMEM((H, 2, cap, R, V), bf16), VMEM((H, B, R, V), f32), VMEM((G, A, R, V), f32),
                VMEM((A, R, 128), f32), VMEM((A, B * R), f32), VMEM((A, W), f32),
                VMEM((T, A, B * R), f32), VMEM((D, A, W), f32),
                DMA((3 + H,)), DMA((B // G,)), DMA((H, B // G)), DMA((H,)), DMA((H,)),
                DMA((H, C + 1)), DMA((H, 2, C + 1)), DMA((H, 2, C)), DMA((H,)), DMA((H,)),
                DMA((H, 2, C + 1)), DMA((H, 2, C)), DMA((H, C + 1)),
                DMA((T,)), DMA((T,)), DMA((D,)), DMA((D,)),
            ],
            compiler_params=pltpu.CompilerParams(
                collective_id=ident, has_side_effects=True, vmem_limit_bytes=66_000_000
            ),
            cost_estimate=pl.CostEstimate(flops=4 * E * R * R * W, bytes_accessed=20 << 20, transcendentals=3 * B * R * W),
            name="sweep",
        )

    value, adjoint, grad_util, grad_taste = sweep(FX, 1)(
        plan, send, value_in.reshape(B, R, W), cotangent, tiles.reshape(E, R, R), state_util, taste
    )
    return value, adjoint.reshape(B * R, W), grad_util, grad_taste


def choose(*args):
    B, A, M, R, _ = args[4].shape
    D = lax.axis_size("state")
    cap = (B + D - 2) // (D - 1)
    fits = D * B <= 128 and 128 < B * A * M <= 256 and cap % 2 == 0 and B % 4 == 0 and R == 128
    if D == 4 and fits and args[0].shape[1] % 256 == 0:
        return folded(*args)
    return local(*args)


def solution(mesh):
    rows = ("groups", "state")
    return jax.shard_map(
        choose,
        mesh=mesh,
        in_specs=(
            P(rows, "type"),
            P(rows, "type"),
            P(None, rows),
            P(None, ("groups", "type")),
            P(rows, None, None, None, None),
            P(rows, None, None),
            P(rows, None),
        ),
        out_specs=(P(rows, "type"), P(rows, "type"), P(None, rows), P(None, ("groups", "type"))),
        check_vma=False,
    )
```

```python
import functools

import jax
import jax.numpy as jnp
from jax import lax
from jax.experimental import pallas as pl
from jax.experimental.pallas import tpu as pltpu
from jax.sharding import PartitionSpec as P

VMEM = pltpu.VMEM
SMEM = pltpu.SMEM
MESH = pl.DeviceIdType.MESH


def smem():
    return pl.BlockSpec(memory_space=SMEM)


def whole(shape):
    return pl.BlockSpec(shape, lambda *g: (0,) * len(shape))


def plan_kernel(dims, me_ref, dest_ref, count_ref, req_ref, look_ref, from_ref, fill):
    B, A, M, D, cap = dims
    me = me_ref[0]

    def clear(p, carry):
        fill[p] = 0
        for s in range(cap):
            req_ref[p, 0, s] = -1
            from_ref[p * cap + s] = 0
        return carry

    lax.fori_loop(0, D, clear, 0)

    def lists(i, carry):
        for a in range(A):
            count = count_ref[a, i]
            for n in range(M):
                e = (i * A + a) * M + n
                dest = dest_ref[n, a, i]
                owner = lax.div(dest, B)
                block = dest - owner * B
                used = n < count
                look_ref[e] = jnp.where(used & (owner == me), block, -1)

                @pl.when(used & (owner != me))
                def _():
                    s = fill[owner]
                    fill[owner] = s + 1
                    req_ref[owner, 0, s] = block
                    from_ref[owner * cap + s] = e
                    look_ref[e] = B + owner * cap + s

        return carry

    lax.fori_loop(0, B, lists, 0)


def greet(axis, others):
    barrier = pltpu.get_barrier_semaphore()
    for ids in others:
        pl.semaphore_signal(barrier, inc=1, device_id=ids, device_id_type=MESH)
    pl.semaphore_wait(barrier, len(others))


def request_kernel(D, req_ref, out_ref, land, send, recv):
    me = lax.axis_index("state")
    peers = [{"state": lax.rem(me + k, D)} for k in range(1, D)]
    greet("state", peers)
    copies = []
    for k in range(1, D):
        c = pltpu.make_async_remote_copy(
            src_ref=req_ref.at[lax.rem(me + k, D)],
            dst_ref=land.at[k],
            send_sem=send.at[k],
            recv_sem=recv.at[k],
            device_id={"state": lax.rem(me + k, D)},
            device_id_type=MESH,
        )
        c.start()
        copies.append(c)
    for c in copies:
        c.wait()
    out_ref[me] = req_ref[me]
    for k in range(1, D):
        out_ref[lax.rem(me - k + D, D)] = land[k]


def gather_kernel(D, cap, half, want_ref, val_ref, *rest):
    outs, sem = rest[:-1], rest[-1]

    def run(h, act):
        def peer(p, carry):
            for s in range(cap):
                w = jnp.maximum(want_ref[p, 0, s], 0)
                act(
                    pltpu.make_async_copy(
                        val_ref.at[w, :, pl.ds(h * half, half)],
                        outs[h].at[p * cap + s],
                        sem.at[h, p * cap + s],
                    )
                )
            return carry

        lax.fori_loop(0, D, peer, 0)

    for h in range(len(outs)):
        run(h, lambda c: c.start())
    for h in range(len(outs)):
        run(h, lambda c: c.wait())


def transposed_dot(tile, right):
    return lax.dot_general(tile, right, (((0,), (0,)), ((), ())), preferred_element_type=jnp.float32)


def continuation(M, first, look_ref, table, tiles):
    weights, values = [], []
    for n in range(M):
        row = look_ref[first + n]
        keep = jnp.where(row >= 0, 1.0, 0.0).astype(jnp.float32)
        tile = tiles(n)
        weights.append(tile * jnp.full(tile.shape, keep, jnp.float32).astype(jnp.bfloat16))
        values.append(table[jnp.maximum(row, 0)])
    return jnp.dot(
        jnp.concatenate(weights, axis=1), jnp.concatenate(values, axis=0), preferred_element_type=jnp.float32
    )


def fetch_value_kernel(G, rows, D, look_ref, from_ref, val_ref, *rest):
    H = (len(rest) - 14) // 2
    outs, rest = rest[:H], rest[H:]
    body, lands = rest[:9], rest[9 : 9 + H - 1]
    acc, table, kept, sem, send, recv = rest[9 + H - 1 :]
    step = pl.program_id(0)
    B, C, V = val_ref.shape[0], outs[0].shape[0], outs[0].shape[2]
    cap = C // D
    me = lax.axis_index("state")

    def copy(h, k):
        to = lax.rem(me + k, D)
        land = table.at[pl.ds(B + me * cap, cap)] if h == 0 else lands[h - 1].at[pl.ds(me * cap, cap)]
        return pltpu.make_async_remote_copy(
            src_ref=outs[h].at[pl.ds(to * cap, cap)],
            dst_ref=land,
            send_sem=send.at[h, k],
            recv_sem=recv.at[h, k],
            device_id={"state": to},
            device_id_type=MESH,
        )

    @pl.when(step == 0)
    def _():
        greet("state", [{"state": lax.rem(me + k, D)} for k in range(1, D)])
        for h in range(H):
            for k in range(1, D):
                copy(h, k).start()
        own = pltpu.make_async_copy(val_ref.at[:, :, pl.ds(0, V)], table.at[pl.ds(0, B)], sem.at[0])
        mine = pltpu.make_async_copy(
            outs[0].at[pl.ds(me * cap, cap)], table.at[pl.ds(B + me * cap, cap)], sem.at[1]
        )
        own.start()
        mine.start()
        own.wait()
        mine.wait()
        for k in range(1, D):
            copy(0, k).wait()

    work(G, rows, look_ref, from_ref, *body, acc, table, kept)

    @pl.when(step == pl.num_programs(0) - 1)
    def _():
        for h in range(1, H):
            for k in range(1, D):
                copy(h, k).wait()


def value_kernel(
    G, rows, col, look_ref, from_ref, val_ref, inc_ref, tiles_ref, cot_ref, util_ref, taste_ref, *rest
):
    before_ref = rest[0]
    value_ref, scaled_ref, out_ref, gu_ref, gt_ref, acc, table, kept, sem = rest[-9:]
    step = pl.program_id(0)
    B, C, V = val_ref.shape[0], inc_ref.shape[0], inc_ref.shape[2]

    @pl.when(step == 0)
    def _():
        own = pltpu.make_async_copy(val_ref.at[:, :, pl.ds(col, V)], table.at[pl.ds(0, B)], sem.at[0])
        far = pltpu.make_async_copy(inc_ref, table.at[pl.ds(B, C)], sem.at[1])
        own.start()
        far.start()
        own.wait()
        far.wait()

    value_ref[:, :col] = before_ref[...]
    work(
        G, rows, look_ref, from_ref, tiles_ref, cot_ref, util_ref, taste_ref,
        value_ref.at[:, col:], scaled_ref, out_ref, gu_ref, gt_ref, acc, table, kept,
    )


def work(
    G, rows, look_ref, from_ref, tiles_ref, cot_ref, util_ref, taste_ref,
    value_ref, scaled_ref, out_ref, gu_ref, gt_ref, acc, table, kept,
):
    step = pl.program_id(0)
    _, A, M, R, _ = tiles_ref.shape
    C = out_ref.shape[0]

    @pl.when(step == 0)
    def _():
        gt_ref[...] = jnp.zeros_like(gt_ref)

    t0, t1 = taste_ref[0:1, :], taste_ref[1:2, :]
    for g in range(G):
        i = step * G + g
        for a in range(A):
            acc[g, a] = continuation(M, (i * A + a) * M, look_ref, table, lambda n: tiles_ref[i, a, n])
    for g in range(G):
        g0 = g1 = 0.0
        cols = [
            jnp.transpose(jnp.broadcast_to(util_ref[a : a + 1, g * R : (g + 1) * R], (R, R))) for a in range(A)
        ]
        for c in range(0, R, rows):
            at = slice(c, c + rows)
            here = slice(g * R + c, g * R + c + rows)
            q0 = cols[0][at, 0:1] + t0 + 0.95 * acc[g, 0, at, :]
            q1 = cols[1][at, 0:1] + t1 + 0.95 * acc[g, 1, at, :]
            gap = q1 - q0
            small = jnp.exp(-jnp.abs(gap))
            total = 1.0 + small
            value_ref[here, :] = jnp.maximum(q0, q1) + jnp.log(total)
            big = cot_ref[here, :].astype(jnp.float32) / total
            little = big * small
            first_wins = gap <= 0.0
            h0 = jnp.where(first_wins, big, little)
            h1 = jnp.where(first_wins, little, big)
            scaled_ref[g, 0, at, :] = (0.95 * h0).astype(jnp.bfloat16)
            scaled_ref[g, 1, at, :] = (0.95 * h1).astype(jnp.bfloat16)
            gu_ref[g, at, 0:1] = jnp.sum(h0, axis=1, keepdims=True)
            gu_ref[g, at, 1:2] = jnp.sum(h1, axis=1, keepdims=True)
            g0, g1 = g0 + h0, g1 + h1
        gt_ref[0:1, :] += jnp.sum(g0, axis=0, keepdims=True)
        gt_ref[1:2, :] += jnp.sum(g1, axis=0, keepdims=True)
    kept[pl.ds(step * G, G)] = scaled_ref[...]

    @pl.when(step == pl.num_programs(0) - 1)
    def _():
        def back(q, carry):
            for u in range(2):
                slot = q * 2 + u
                e = from_ref[slot]
                pair = lax.div(e, M)
                i = lax.div(pair, A)
                a = pair - i * A
                out_ref[slot] = transposed_dot(tiles_ref[i, a, e - pair * M], kept[i, a]).astype(jnp.bfloat16)
            return carry

        lax.fori_loop(0, C // 2, back, 0)


def back_kernel(G, A, M, look_ref, tiles_ref, scaled_ref, adj_ref):
    spare = adj_ref.shape[0] - 1
    step = pl.program_id(0)

    @pl.when(step == 0)
    def _():
        adj_ref[...] = jnp.zeros_like(adj_ref)

    for g in range(G):
        i = step * G + g
        for a in range(A):
            for n in range(M):
                block = look_ref[(i * A + a) * M + n]
                here = jnp.where((block >= 0) & (block < spare), block, spare)
                adj_ref[here] += transposed_dot(tiles_ref[g, a, n], scaled_ref[g, a])


def sums_kernel(D, T, gu_ref, gt_ref, token_ref, after_ref, ou_ref, ot_ref, lu, lt, us, ur, ts, tr):
    ms, mt = lax.axis_index("state"), lax.axis_index("type")
    peers = [{"state": lax.rem(ms + k, D)} for k in range(1, D)]
    peers += [{"type": lax.rem(mt + k, T)} for k in range(1, T)]
    greet("state", peers)
    copies = []
    for k in range(1, T):
        copies.append(
            pltpu.make_async_remote_copy(
                src_ref=gu_ref, dst_ref=lu.at[k], send_sem=us.at[k], recv_sem=ur.at[k],
                device_id={"type": lax.rem(mt + k, T)}, device_id_type=MESH,
            )
        )
    for k in range(1, D):
        copies.append(
            pltpu.make_async_remote_copy(
                src_ref=gt_ref, dst_ref=lt.at[k], send_sem=ts.at[k], recv_sem=tr.at[k],
                device_id={"state": lax.rem(ms + k, D)}, device_id_type=MESH,
            )
        )
    for c in copies:
        c.start()
    for c in copies:
        c.wait()
    lu[0] = gu_ref[...]
    lt[0] = gt_ref[...]
    u = lu[lax.rem(mt, T)]
    for j in range(1, T):
        u = u + lu[lax.rem(mt - j + T, T)]
    t = lt[lax.rem(ms, D)]
    for j in range(1, D):
        t = t + lt[lax.rem(ms - j + D, D)]
    ou_ref[...] = u
    ot_ref[...] = t


def land_kernel(D, cap, want_ref, adj_ref, ret_ref, *rest):
    out_ref, done_ref = rest[-2:]
    done_ref[0] = 0
    out_ref[...] = adj_ref[...]

    def peer(p, carry):
        for s in range(cap):
            w = want_ref[p, 0, s]

            @pl.when(w >= 0)
            def _():
                out_ref[w] += ret_ref[p * cap + s].astype(jnp.float32)

        return carry

    lax.fori_loop(0, D, peer, 0)


def local(value_in, cotangent, state_util, taste, tiles, dest_block, counts):
    B, A, M, R, _ = tiles.shape
    W = value_in.shape[1]
    D = lax.axis_size("state")
    T = lax.axis_size("type")
    cap = max(2, (B + D - 2) // (D - 1))
    E, C = B * A * M, D * cap
    f32, bf16, i32 = jnp.float32, jnp.bfloat16, jnp.int32
    shape = jax.ShapeDtypeStruct
    values = value_in.reshape(B, R, W)

    req, look, origin = pl.pallas_call(
        functools.partial(plan_kernel, (B, A, M, D, cap)),
        out_shape=(shape((D, 1, 128), i32), shape((E,), i32), shape((C,), i32)),
        in_specs=[smem()] * 3,
        out_specs=[smem()] * 3,
        scratch_shapes=[SMEM((D,), i32)],
        name="plan",
    )(lax.axis_index("state").reshape(1).astype(i32), dest_block.transpose(2, 1, 0), counts.T)

    wanted = pl.pallas_call(
        functools.partial(request_kernel, D),
        out_shape=shape((D, 1, 128), i32),
        in_specs=[pl.BlockSpec(memory_space=VMEM)],
        out_specs=pl.BlockSpec(memory_space=VMEM),
        scratch_shapes=[VMEM((D, 1, 128), i32), pltpu.SemaphoreType.DMA((D,)), pltpu.SemaphoreType.DMA((D,))],
        compiler_params=pltpu.CompilerParams(collective_id=0, has_side_effects=True),
        name="request",
    )(req)

    H = 2 if W % 256 == 0 else 1
    V = W // H
    G = 4 if B % 4 == 0 else 1
    outgoing = pl.pallas_call(
        functools.partial(gather_kernel, D, cap, V),
        out_shape=tuple(shape((C, R, V), bf16) for h in range(H)),
        in_specs=[smem(), pl.BlockSpec(memory_space=VMEM)],
        out_specs=[pl.BlockSpec(memory_space=pl.ANY)] * H,
        scratch_shapes=[pltpu.SemaphoreType.DMA((H, C))],
        name="gather",
    )(wanted, values)

    def exchange(x):
        return lax.all_to_all(
            x.reshape(D, cap, R, V), "state", split_axis=0, concat_axis=0, tiled=True
        ).reshape(C, R, V)

    incoming = []

    flops = 2 * E * R * R * W
    value = None
    gus, gts, outbound, scaleds = [], [], [], []
    any_spec = pl.BlockSpec(memory_space=pl.ANY)
    for h in range(H):
        wide = V * (h + 1)
        ins = [
            whole((B, A, M, R, R)),
            pl.BlockSpec((G * R, V), lambda i, h=h: (i, h)),
            pl.BlockSpec((A, G * R), lambda i: (0, i)),
            pl.BlockSpec((A, V), lambda i, h=h: (0, h)),
        ]
        out_shape = [
            shape((B * R, wide), f32), shape((B, A, R, V), bf16), shape((C, R, V), bf16),
            shape((B, R, A), f32), shape((A, V), f32),
        ]
        out_specs = [
            pl.BlockSpec((G * R, wide), lambda i: (i, 0)),
            pl.BlockSpec((G, A, R, V), lambda i: (i, 0, 0, 0)),
            whole((C, R, V)),
            pl.BlockSpec((G, R, A), lambda i: (i, 0, 0)),
            whole((A, V)),
        ]
        scratch = [
            VMEM((G, A, R, V), f32), VMEM((B + C, R, V), bf16), VMEM((B, A, R, V), bf16),
            pltpu.SemaphoreType.DMA((2,)),
        ]
        cost = pl.CostEstimate(flops=flops // H, bytes_accessed=(24 << 20) // H, transcendentals=3 * B * R * V)
        if h == 0:
            value, scaled, out, gu, gt, *incoming = pl.pallas_call(
                functools.partial(fetch_value_kernel, G, 32, D),
                grid=(B // G,),
                out_shape=out_shape + [shape((C, R, V), bf16)] * (H - 1),
                in_specs=[smem(), smem(), any_spec] + [any_spec] * H + ins,
                out_specs=out_specs + [any_spec] * (H - 1),
                scratch_shapes=scratch + [pltpu.SemaphoreType.DMA((H, D)), pltpu.SemaphoreType.DMA((H, D))],
                compiler_params=pltpu.CompilerParams(collective_id=2, has_side_effects=True),
                cost_estimate=cost,
                name="fetch",
            )(look, origin, values, *outgoing, tiles, cotangent, state_util, taste)
        else:
            value, scaled, out, gu, gt = pl.pallas_call(
                functools.partial(value_kernel, G, 32, h * V),
                grid=(B // G,),
                out_shape=out_shape,
                in_specs=[smem(), smem(), any_spec, any_spec] + ins
                + [pl.BlockSpec((G * R, h * V), lambda i: (i, 0))],
                out_specs=out_specs,
                scratch_shapes=scratch,
                cost_estimate=cost,
                name="value",
            )(look, origin, values, incoming[h - 1], tiles, cotangent, state_util, taste, value)
        outbound.append(out)
        scaleds.append(scaled)
        gus.append(gu)
        gts.append(gt)

    adjs = [
        pl.pallas_call(
            functools.partial(back_kernel, G, A, M),
            grid=(B // G,),
            out_shape=shape((B + 1, R, V), f32),
            in_specs=[
                smem(),
                pl.BlockSpec((G, A, M, R, R), lambda i: (i, 0, 0, 0, 0)),
                pl.BlockSpec((G, A, R, V), lambda i: (i, 0, 0, 0)),
            ],
            out_specs=whole((B + 1, R, V)),
            cost_estimate=pl.CostEstimate(flops=flops // H, bytes_accessed=(14 << 20) // H, transcendentals=0),
            name="back",
        )(look, tiles, x)
        for x in scaleds
    ]

    returned = []
    for h in range(H):
        if h > 0:
            outbound[h], adjs[h - 1] = lax.optimization_barrier((outbound[h], adjs[h - 1]))
        returned.append(exchange(outbound[h]))

    adjoint, tokens = None, []
    gu_rows = sum(gus).transpose(2, 0, 1).reshape(A, B * R) / (W * T)
    for h in range(H):
        held = [] if h == 0 else [adjoint]
        adjoint, token = pl.pallas_call(
            functools.partial(land_kernel, D, cap),
            grid=(1,),
            out_shape=(shape((B, R, W), f32), shape((1,), i32)),
            in_specs=[smem(), whole((B, R, V)), whole((C, R, V))]
            + [pl.BlockSpec(memory_space=pl.ANY)] * len(held),
            out_specs=[pl.BlockSpec((B, R, V), lambda j, h=h: (0, 0, h)), smem()],
            input_output_aliases={3 + k: k for k in range(len(held))},
            name="land",
        )(wanted, adjs[h], returned[h], *held)
        tokens.append(token)
    grad_util, grad_taste = pl.pallas_call(
        functools.partial(sums_kernel, D, T),
        out_shape=(shape((A, B * R), f32), shape((A, W), f32)),
        in_specs=[pl.BlockSpec(memory_space=VMEM)] * 2 + [smem(), pl.BlockSpec(memory_space=pl.ANY)],
        out_specs=[pl.BlockSpec(memory_space=VMEM)] * 2,
        scratch_shapes=[
            VMEM((T, A, B * R), f32), VMEM((D, A, W), f32),
            pltpu.SemaphoreType.DMA((T,)), pltpu.SemaphoreType.DMA((T,)),
            pltpu.SemaphoreType.DMA((D,)), pltpu.SemaphoreType.DMA((D,)),
        ],
        compiler_params=pltpu.CompilerParams(collective_id=1, has_side_effects=True),
        cost_estimate=pl.CostEstimate(flops=0, bytes_accessed=8 << 20, transcendentals=0),
        name="sums",
    )(gu_rows, jnp.concatenate(gts, axis=1) / (B * R * D), tokens[0], adjs[-1])

    return value, adjoint.reshape(B * R, W), grad_util, grad_taste


def meet_kernel(dims, dest_ref, count_ref, plan_ref, mine, land, oh, ssem, rsem):
    B, A, M, D, cap, Q = dims
    f32 = jnp.float32
    y, z = lax.axis_index("groups"), lax.axis_index("state")
    q = y * D + z
    E2 = oh.shape[0]
    mine[...] = jnp.full(mine.shape, -1.0, f32)
    for n in range(M):
        mine[n * A : (n + 1) * A, 0:B] = jnp.where(n < count_ref[...], dest_ref[n], -1).astype(f32)
    land[0] = jnp.transpose(mine[...])[0:B, :]

    def member(k):
        p = lax.rem(q + k, Q)
        return {"groups": lax.div(p, D), "state": lax.rem(p, D)}

    greet("state", [member(k) for k in range(1, Q)])
    copies = [
        pltpu.make_async_remote_copy(
            src_ref=land.at[0], dst_ref=land.at[k], send_sem=ssem.at[k], recv_sem=rsem.at[k],
            device_id=member(k), device_id_type=MESH,
        )
        for k in range(1, Q)
    ]
    for c in copies:
        c.start()

    lane = lax.broadcasted_iota(jnp.int32, (B, 128), 1).astype(f32)
    oh[...] = jnp.zeros(oh.shape, f32)
    own = land[0]
    for c in range(A * M):
        oh[c * B : (c + 1) * B, :] = jnp.where(own[:, c : c + 1] == lane, 1.0, 0.0)
    seg = lax.div(lax.broadcasted_iota(jnp.int32, (1, 128), 1), B)
    b = lax.broadcasted_iota(jnp.int32, (1, 128), 1).astype(f32)

    def as_row(col):
        full = jnp.broadcast_to(col, (E2, 128))
        return jnp.concatenate(
            [jnp.transpose(full[k : k + 128, :])[0:1, :] for k in range(0, E2, 128)], axis=1
        )

    key_of = b + jnp.where(seg == z, 129.0, 1.0)
    key = jnp.sum(oh[...] * key_of, axis=1, keepdims=True)
    key = jnp.where(key == 0, 300.0, key)
    iq = lax.broadcasted_iota(jnp.int32, (E2, 1), 0)
    order = key * E2 + iq.astype(f32)
    order_row, key_row = as_row(order), as_row(key)
    pos = jnp.sum(jnp.where(order_row < order, 1.0, 0.0), axis=1, keepdims=True)
    less = jnp.sum(jnp.where(key_row < key, 1.0, 0.0), axis=1, keepdims=True)
    wide = lax.broadcasted_iota(jnp.int32, (E2, E2), 1).astype(f32)
    c = lax.div(iq, B)
    entry = ((lax.rem(iq, B) * A + lax.rem(c, A)) * M + lax.div(c, A)).astype(f32)
    move = jnp.where(pos == wide, 1.0, 0.0)
    put = lambda k, v: plan_ref.__setitem__((slice(k, k + 1), slice(0, v.shape[1])), v.astype(jnp.int32))
    plan_ref[...] = jnp.zeros(plan_ref.shape, jnp.int32)
    put(1, jnp.sum(move * entry, axis=0, keepdims=True))
    put(2, jnp.sum(move * jnp.where(pos == less, 0.0, pos), axis=0, keepdims=True))
    last = jnp.sum(jnp.where(key <= key_of, 1.0, 0.0), axis=0, keepdims=True)
    last = last * jnp.max(jnp.where(key == key_of, 1.0, 0.0), axis=0, keepdims=True)
    for k in copies:
        k.wait()

    def need_of(table):
        total = jnp.zeros((B, 128), f32)
        for c in range(A * M):
            total = jnp.maximum(total, jnp.where(table[:, c : c + 1] == lane, 1.0, 0.0))
        return jnp.max(total, axis=0, keepdims=True)

    half = D // 2
    rows, needs = [], []
    for u in range(Q // D):
        g = lax.rem(y + u, Q // D)
        need = [need_of(land[lax.rem(q - (g * D + r) + Q, Q)]) for r in range(D)]
        end = jnp.where(seg < half, need[D - 1], need[0])
        gate = jnp.where(seg < half, need[half], need[half - 1]) * (1.0 - end)
        rows += [end, gate]
        if u == 0:
            needs = need
    peer = 2 * lax.div(z, 2) + 1 - lax.rem(z, 2)
    mine_need = sum(jnp.where(z == r, needs[r], 0.0) for r in range(D))
    peer_need = sum(jnp.where(peer == r, needs[r], 0.0) for r in range(D))
    at = len(rows)
    rows += [mine_need, peer_need]
    stack = jnp.concatenate(rows + [jnp.zeros((8 - len(rows), 128), f32)], axis=0)
    one = lax.broadcasted_iota(jnp.int32, (128, 128), 0)
    two = lax.broadcasted_iota(jnp.int32, (128, 128), 1)
    same = jnp.where(lax.div(one, B) == lax.div(two, B), 1.0, 0.0)
    below = jnp.where(one < two, same, 0.0)
    rank = jnp.dot(stack, below, preferred_element_type=f32)
    size = jnp.dot(stack, same, preferred_element_type=f32)
    far_any = rows[0] + rows[1]
    far_rank = jnp.where(rows[0] > 0, rank[0:1], size[0:1] + rank[1:2])
    most = size[0:1] + size[1:2]
    for u in range(1, Q // D):
        most = jnp.maximum(most, size[2 * u : 2 * u + 1] + size[2 * u + 1 : 2 * u + 2])
    near_rank, give_rank = rank[at : at + 1], rank[at + 1 : at + 2]
    first = (z * B).astype(f32)
    FX = 2 * cap
    row_of = 1.0 + jnp.where(
        seg == z,
        b - first,
        jnp.where(
            lax.div(seg, 2) == lax.div(z, 2), B + near_rank, B + cap + lax.rem(seg, 2).astype(f32) * FX + far_rank
        ),
    )

    row = jnp.sum(oh[...] * row_of, axis=1, keepdims=True)
    put(0, jnp.sum(jnp.where(entry == wide, row, 0.0), axis=0, keepdims=True))
    slot = lax.broadcasted_iota(jnp.int32, (16, 128), 0).astype(f32)
    here = jnp.where(seg == z, b - first, 0.0)
    mine_here = (seg == z) & (b - first == slot)
    goal = lax.broadcasted_iota(jnp.int32, (64, 128), 0).astype(f32)
    known = (mine_need > 0) | (seg == z)
    lists = [
        jnp.where((give_rank == slot) & (peer_need > 0), here, 0.0),
        jnp.where((far_rank == slot) & (far_any > 0), here, 0.0),
        jnp.where(mine_here & (peer_need > 0), give_rank + 1.0, 0.0),
        jnp.where(mine_here & (far_any > 0), far_rank + 1.0, 0.0),
        jnp.where((row_of - 1.0 == goal) & known, last, 0.0),
    ]
    column = jnp.concatenate([jnp.sum(v, axis=1, keepdims=True) for v in lists], axis=0)
    put(3, jnp.transpose(jnp.broadcast_to(column, (128, 128)))[0:1, :])
    put(4, jnp.broadcast_to(jnp.max(most, axis=1, keepdims=True), (1, 128)))


def sweep_kernel(
    dims, plan, val, cot_hbm, tiles_hbm, util, taste, value_hbm, adj_hbm, retn, retf, gu_ref, gt_ref, *rest
):
    B, A, M, R, V, H, D, T, cap, FX, F, G, rows = dims
    f32, bf16 = jnp.float32, jnp.bfloat16
    E, C, CH = B * A * M, cap // 2, 2
    tables, rest = rest[:H], rest[H:]
    (own, stn, stx, tiles, cot, vout, scaled, P, bst, rel, adj, acc, fold, gacc, gtac, lu, lt,
     lsem, vsem, asem, sn, rn, sx, rx, sf, bsn, brn, bsx, brel, brx, usem, ursem, tsem, trsem) = rest
    z, t = lax.axis_index("state"), lax.axis_index("type")
    side = lax.div(z, 2)
    spot = lax.rem(z, 2)
    peer = 2 * side + 1 - spot
    gate_to = D // 2 - side
    is_gate = (z == D // 2 - 1) | (z == D // 2)
    is_end = jnp.logical_not(is_gate)
    far0 = 2 * (1 - side)
    tail = [C] if F > cap else []

    def span(c):
        return pl.ds(cap, F - cap) if isinstance(c, int) and c == C else pl.ds(c * CH, CH)

    def remote(src, dst, s, r, device):
        return pltpu.make_async_remote_copy(
            src_ref=src, dst_ref=dst, send_sem=s, recv_sem=r, device_id={"state": device}, device_id_type=MESH
        )

    def shift(c, base):
        s = span(c)
        return pl.ds(base + s.start, s.size)

    def fwd_near(h):
        return remote(stn.at[h], tables[h].at[pl.ds(B, cap)], sn.at[h], rn.at[h], peer)

    def fwd_far(h, c, x):
        return remote(
            stx.at[h, span(c)], tables[h].at[shift(c, B + cap + x * FX)], sx.at[h, c], rx.at[h, x, c], gate_to
        )

    def fwd_pass(h, x, c):
        part = tables[h].at[shift(c, B + cap + x * FX)]
        return remote(part, part, sf.at[h, x, c], rx.at[h, x, c], peer)

    def bwd_near(h):
        return remote(bst.at[h, pl.ds(0, cap)], retn.at[:, :, cols(h)], bsn.at[h], brn.at[h], peer)

    def bwd_far(h, x, c):
        return remote(
            bst.at[h, shift(c, cap + x * FX)], retf.at[span(c), :, cols(h)], bsx.at[h, x, c], brx.at[h, c], far0 + x
        )

    def bwd_end(h, x, c):
        return remote(
            bst.at[h, shift(c, cap + x * FX)], rel.at[h, x, span(c)], bsx.at[h, x, c], brel.at[h, x, c], peer
        )

    def cols(h):
        return pl.ds(h * V, V)

    own_copy = pltpu.make_async_copy(val, own, lsem.at[0])
    own_copy.start()
    fills = [
        pltpu.make_async_copy(val.at[:, :, cols(h)], tables[h].at[pl.ds(0, B)], lsem.at[1 + h]) for h in range(H)
    ]
    fills[0].start()
    tile_copy = pltpu.make_async_copy(tiles_hbm, tiles, lsem.at[1 + H])
    cot_copy = pltpu.make_async_copy(cot_hbm, cot, lsem.at[2 + H])
    greet(
        "state",
        [{"state": lax.rem(z + k, D)} for k in range(1, D)] + [{"type": lax.rem(t + k, T)} for k in range(1, T)],
    )
    own_copy.wait()
    for h in range(H):
        for s in range(F):
            stx[h, s] = own[plan[3, 16 + s], :, h * V : (h + 1) * V]
            if s >= 2 and s % CH == 1 and s - CH < cap:
                fwd_far(h, s // CH - 1, spot).start()
        for s in range(cap):
            stn[h, s] = own[plan[3, s], :, h * V : (h + 1) * V]
        if F <= cap + 1:
            fwd_far(h, C - 1, spot).start()
        for c in tail:
            fwd_far(h, c, spot).start()
        fwd_near(h).start()
        if h == 0:
            tile_copy.start()
            cot_copy.start()
            for f in fills[1:]:
                f.start()
    P[0] = jnp.zeros((R, V), f32)
    gtac[...] = jnp.zeros(gtac.shape, f32)

    def pass_on(h, c):
        @pl.when(is_gate)
        def _():
            for x in range(2):
                fwd_far(h, c, x).wait_recv()
                fwd_pass(h, x, c).start()

    def arrived(h):
        fwd_near(h).wait_recv()

        @pl.when(is_gate)
        def _():
            for x in range(2):
                for c in tail:
                    fwd_far(h, c, x).wait_recv()

        @pl.when(is_end)
        def _():
            for x in range(2):
                for c in range(C):
                    fwd_far(h, c, x).wait_recv()

    def values(h, hook):
        t0, t1 = taste[0:1, h * V : (h + 1) * V], taste[1:2, h * V : (h + 1) * V]

        def step(k, carry):
            for g in range(G):
                i = k * G + g
                for a in range(A):
                    weights, blocks = [], []
                    for n in range(M):
                        e = (i * A + a) * M + n
                        row = plan[0, e]
                        keep = jnp.where(row > 0, 1.0, 0.0).astype(f32)
                        tile = tiles[e]
                        weights.append(tile * jnp.full(tile.shape, keep, f32).astype(bf16))
                        blocks.append(tables[h][jnp.maximum(row - 1, 0)])
                    acc[g, a] = jnp.dot(
                        jnp.concatenate(weights, axis=1), jnp.concatenate(blocks, axis=0),
                        preferred_element_type=f32,
                    )
            for g in range(G):
                i = k * G + g
                lanes = pl.ds(pl.multiple_of(i * R, R), R)
                base = [jnp.transpose(jnp.broadcast_to(util[a : a + 1, lanes], (R, R))) for a in range(A)]
                g0 = g1 = 0.0
                for c in range(0, R, rows):
                    at = slice(c, c + rows)
                    here = pl.ds(pl.multiple_of(i * R + c, rows), rows)
                    q0 = base[0][at, 0:1] + t0 + 0.95 * acc[g, 0, at, :]
                    q1 = base[1][at, 0:1] + t1 + 0.95 * acc[g, 1, at, :]
                    gap = q1 - q0
                    small = jnp.exp(-jnp.abs(gap))
                    total = 1.0 + small
                    vout[here, :] = jnp.maximum(q0, q1) + jnp.log(total)
                    big = cot[here, h * V : (h + 1) * V].astype(f32) / total
                    little = big * small
                    first_wins = gap <= 0.0
                    h0 = jnp.where(first_wins, big, little)
                    h1 = jnp.where(first_wins, little, big)
                    scaled[i * A, at, :] = (0.95 * h0).astype(bf16)
                    scaled[i * A + 1, at, :] = (0.95 * h1).astype(bf16)
                    fold[0, at, :] = sum(h0[:, w : w + 128] for w in range(0, V, 128))
                    fold[1, at, :] = sum(h1[:, w : w + 128] for w in range(0, V, 128))
                    g0, g1 = g0 + h0, g1 + h1
                for a in range(A):
                    line = jnp.sum(jnp.transpose(fold[a]), axis=0, keepdims=True)
                    gacc[a : a + 1, lanes] = line if h == 0 else gacc[a : a + 1, lanes] + line
                gtac[0:1, h * V : (h + 1) * V] += jnp.sum(g0, axis=0, keepdims=True)
                gtac[1:2, h * V : (h + 1) * V] += jnp.sum(g1, axis=0, keepdims=True)
            part = pl.ds(k * G * R, G * R)
            pltpu.make_async_copy(vout.at[part], value_hbm.at[part, cols(h)], vsem.at[k]).start()
            hook(k)
            return carry

        lax.fori_loop(0, B // G, step, 0)

    def value_done(h):
        for k in range(B // G):
            part = pl.ds(k * G * R, G * R)
            pltpu.make_async_copy(vout.at[part], value_hbm.at[part, cols(h)], vsem.at[k]).wait()

    def back(lo, hi):
        def step(k, carry):
            for u in range(B):
                e = plan[1, k * B + u]
                P[k * B + u + 1] = P[plan[2, k * B + u]] + transposed_dot(tiles[e], scaled[lax.div(e, M)])
            return carry

        lax.fori_loop(lo, hi, step, 0)

    def stage(h, s):
        bst[h, s] = P[plan[3, 64 + B + s]].astype(bf16)

    def give(h):
        @pl.when(is_end)
        def _():
            for c in range(C):
                for x in range(2):
                    for s in range(c * CH, (c + 1) * CH):
                        stage(h, cap + x * FX + s)
                if c > 0:
                    for x in range(2):
                        bwd_end(h, x, c - 1).start()

        @pl.when(is_gate)
        def _():
            for x in range(2):
                for s in range(cap, F):
                    stage(h, cap + x * FX + s)

        for s in range(cap):
            stage(h, s)

        @pl.when(is_end)
        def _():
            for x in range(2):
                bwd_end(h, x, C - 1).start()

        @pl.when(is_gate)
        def _():
            for x in range(2):
                for c in tail:
                    bwd_far(h, x, c).start()

        bwd_near(h).start()

    def add_on(h, c):
        @pl.when(is_gate)
        def _():
            for x in range(2):
                bwd_end(h, x, c).wait_recv()
                for s in range(CH):
                    u = c * CH + s
                    term = P[plan[3, 64 + B + cap + x * FX + u]] + rel[h, x, u].astype(f32)
                    bst[h, cap + x * FX + u] = term.astype(bf16)
            for x in range(2):
                bwd_far(h, x, c).start()

    def adj_out(h, k):
        part = pl.ds(k * G, G)
        return pltpu.make_async_copy(adj.at[h, part], adj_hbm.at[part, :, cols(h)], asem.at[h, k])

    def keep(h):
        def step(k, carry):
            for g in range(G):
                adj[h, k * G + g] = P[plan[3, 64 + k * G + g]]
            adj_out(h, k).start()
            return carry

        lax.fori_loop(0, B // G, step, 0)

    def sums():
        out = []
        for k in range(1, T):
            out.append(
                pltpu.make_async_remote_copy(
                    src_ref=gacc, dst_ref=lu.at[k], send_sem=usem.at[k], recv_sem=ursem.at[k],
                    device_id={"type": lax.rem(t + k, T)}, device_id_type=MESH,
                )
            )
        for k in range(1, D):
            out.append(remote(gtac, lt.at[k], tsem.at[k], trsem.at[k], lax.rem(z + k, D)))
        return out

    for c in range(C):
        pass_on(0, c)
    fills[0].wait()
    arrived(0)
    tile_copy.wait()
    cot_copy.wait()
    for h in range(H):
        steps = B // G

        def hook(k, h=h):
            @pl.when(k < C)
            def _():
                if h + 1 < H:
                    pass_on(h + 1, k)
                if h > 0:
                    add_on(h - 1, k)

        if h > 0:
            fills[h].wait()
            arrived(h)
            value_done(h - 1)
        values(h, hook)
        back(0, 1)
        give(h)
        if h == H - 1:
            for c in sums():
                c.start()
        back(1, E // B)
        keep(h)
    for c in range(C):
        add_on(H - 1, c)
    for c in sums():
        c.wait()
    lu[0] = gacc[...]
    lt[0] = gtac[...]
    u = lu[lax.rem(t, T)]
    for j in range(1, T):
        u = u + lu[lax.rem(t - j + T, T)]
    w = lt[lax.rem(z, D)]
    for j in range(1, D):
        w = w + lt[lax.rem(z - j + D, D)]
    gu_ref[...] = u / (H * V * T)
    gt_ref[...] = w / (B * R * D)
    value_done(H - 1)
    for h in range(H):
        for k in range(B // G):
            adj_out(h, k).wait()
        fwd_near(h).wait_send()
        bwd_near(h).wait()
        for c in list(range(C)) + tail:
            fwd_far(h, c, spot).wait_send()
            bwd_far(h, 0, c).wait_recv()

        @pl.when(is_gate)
        def _(h=h):
            for x in range(2):
                for c in range(C):
                    fwd_pass(h, x, c).wait_send()
                for c in list(range(C)) + tail:
                    bwd_far(h, x, c).wait_send()

        @pl.when(is_end)
        def _(h=h):
            for x in range(2):
                for c in range(C):
                    bwd_end(h, x, c).wait_send()


def folded(value_in, cotangent, state_util, taste, tiles, dest_block, counts):
    B, A, M, R, _ = tiles.shape
    W = value_in.shape[1]
    D, T = lax.axis_size("state"), lax.axis_size("type")
    Q = lax.axis_size("groups") * D
    cap = (B + D - 2) // (D - 1)
    E, FX, H, G = B * A * M, 2 * cap, 2, 4
    V = W // H
    f32, bf16, i32 = jnp.float32, jnp.bfloat16, jnp.int32
    shape, DMA = jax.ShapeDtypeStruct, pltpu.SemaphoreType.DMA
    vmem = pl.BlockSpec(memory_space=VMEM)
    hbm = pl.BlockSpec(memory_space=pl.ANY)

    plan = pl.pallas_call(
        functools.partial(meet_kernel, (B, A, M, D, cap, Q)),
        out_shape=shape((8, 256), i32),
        in_specs=[vmem] * 2,
        out_specs=vmem,
        scratch_shapes=[VMEM((128, 128), f32), VMEM((Q, B, 128), f32), VMEM((256, 128), f32), DMA((Q,)), DMA((Q,))],
        compiler_params=pltpu.CompilerParams(collective_id=0, has_side_effects=True),
        name="meet",
    )(dest_block.transpose(2, 1, 0), counts.T)

    def sweep(F, ident):
        dims = (B, A, M, R, V, H, D, T, cap, FX, F, G, 32)
        C = cap // 2
        return pl.pallas_call(
            functools.partial(sweep_kernel, dims),
            out_shape=(
                shape((B * R, W), f32), shape((B, R, W), f32), shape((cap, R, W), bf16), shape((FX, R, W), bf16),
                shape((A, B * R), f32), shape((A, W), f32),
            ),
            in_specs=[smem(), hbm, hbm, hbm, vmem, vmem],
            out_specs=[hbm, hbm, hbm, hbm, vmem, vmem],
            scratch_shapes=[VMEM((B + cap + 2 * FX, R, V), bf16)] * H
            + [
                VMEM((B, R, W), bf16), VMEM((H, cap, R, V), bf16), VMEM((H, FX, R, V), bf16),
                VMEM((E, R, R), bf16), VMEM((B * R, W), bf16), VMEM((B * R, V), f32),
                VMEM((B * A, R, V), bf16), VMEM((E + 1, R, V), f32), VMEM((H, cap + 2 * FX, R, V), bf16),
                VMEM((H, 2, cap, R, V), bf16), VMEM((H, B, R, V), f32), VMEM((G, A, R, V), f32),
                VMEM((A, R, 128), f32), VMEM((A, B * R), f32), VMEM((A, W), f32),
                VMEM((T, A, B * R), f32), VMEM((D, A, W), f32),
                DMA((3 + H,)), DMA((B // G,)), DMA((H, B // G)), DMA((H,)), DMA((H,)),
                DMA((H, C + 1)), DMA((H, 2, C + 1)), DMA((H, 2, C)), DMA((H,)), DMA((H,)),
                DMA((H, 2, C + 1)), DMA((H, 2, C)), DMA((H, C + 1)),
                DMA((T,)), DMA((T,)), DMA((D,)), DMA((D,)),
            ],
            compiler_params=pltpu.CompilerParams(
                collective_id=ident, has_side_effects=True, vmem_limit_bytes=66_000_000
            ),
            cost_estimate=pl.CostEstimate(flops=4 * E * R * R * W, bytes_accessed=20 << 20, transcendentals=3 * B * R * W),
            name="sweep%d" % F,
        )

    sizes = sorted({cap + (cap + 1) // 2, cap + (2 * cap + 2) // 3, FX})
    most = plan[4, 0]
    pick = sum((most > f).astype(i32) for f in sizes[:-1])
    held = lax.switch(
        pick, [sweep(f, 1 + k) for k, f in enumerate(sizes)],
        plan, value_in.reshape(B, R, W), cotangent, tiles.reshape(E, R, R), state_util, taste,
    )
    slot = lambda at: pl.BlockSpec((1, R, W), lambda j, p: (jnp.maximum(p[3, at + j] - 1, 0), 0, 0))
    block = pl.BlockSpec((1, R, W), lambda j, p: (j, 0, 0))
    line = pl.BlockSpec((R, W), lambda j, p: (j, 0))
    sums = [pl.BlockSpec(v.shape, lambda j, p: (0, 0)) for v in held[4:]]
    value, adjoint, grad_util, grad_taste = pl.pallas_call(
        finish_kernel,
        grid_spec=pltpu.PrefetchScalarGridSpec(
            num_scalar_prefetch=1, grid=(B,), in_specs=[line, block, slot(32), slot(48)] + sums,
            out_specs=[line, block] + sums,
        ),
        out_shape=[shape(held[k].shape, f32) for k in (0, 1, 4, 5)],
        name="finish",
    )(plan, *held)
    return value, adjoint.reshape(B * R, W), grad_util, grad_taste


def finish_kernel(plan, value_ref, part_ref, near_ref, far_ref, gu_ref, gt_ref, value, adjoint, gu, gt):
    j = pl.program_id(0)
    value[...] = value_ref[...]
    total = part_ref[0] + jnp.where(plan[3, 32 + j] > 0, near_ref[0].astype(jnp.float32), 0.0)
    adjoint[0] = total + jnp.where(plan[3, 48 + j] > 0, far_ref[0].astype(jnp.float32), 0.0)
    gu[...] = gu_ref[...]
    gt[...] = gt_ref[...]


def choose(*args):
    B, A, M, R, _ = args[4].shape
    D = lax.axis_size("state")
    cap = (B + D - 2) // (D - 1)
    fits = D * B <= 128 and 128 < B * A * M <= 256 and cap % 2 == 0 and B % 4 == 0 and R == 128
    if D == 4 and fits and args[0].shape[1] % 256 == 0:
        return folded(*args)
    return local(*args)


def solution(mesh):
    rows = ("groups", "state")
    return jax.shard_map(
        choose,
        mesh=mesh,
        in_specs=(
            P(rows, "type"),
            P(rows, "type"),
            P(None, rows),
            P(None, ("groups", "type")),
            P(rows, None, None, None, None),
            P(rows, None, None),
            P(rows, None),
        ),
        out_specs=(P(rows, "type"), P(rows, "type"), P(None, rows), P(None, ("groups", "type"))),
        check_vma=False,
    )
```

```python
import functools

import jax
import jax.numpy as jnp
from jax import lax
from jax.experimental import pallas as pl
from jax.experimental.pallas import tpu as pltpu
from jax.sharding import PartitionSpec as P

VMEM = pltpu.VMEM
SMEM = pltpu.SMEM
MESH = pl.DeviceIdType.MESH


def smem():
    return pl.BlockSpec(memory_space=SMEM)


def whole(shape):
    return pl.BlockSpec(shape, lambda *g: (0,) * len(shape))


def plan_kernel(dims, me_ref, dest_ref, count_ref, req_ref, look_ref, from_ref, fill):
    B, A, M, D, cap = dims
    me = me_ref[0]

    def clear(p, carry):
        fill[p] = 0
        for s in range(cap):
            req_ref[p, 0, s] = -1
            from_ref[p * cap + s] = 0
        return carry

    lax.fori_loop(0, D, clear, 0)

    def lists(i, carry):
        for a in range(A):
            count = count_ref[a, i]
            for n in range(M):
                e = (i * A + a) * M + n
                dest = dest_ref[n, a, i]
                owner = lax.div(dest, B)
                block = dest - owner * B
                used = n < count
                look_ref[e] = jnp.where(used & (owner == me), block, -1)

                @pl.when(used & (owner != me))
                def _():
                    s = fill[owner]
                    fill[owner] = s + 1
                    req_ref[owner, 0, s] = block
                    from_ref[owner * cap + s] = e
                    look_ref[e] = B + owner * cap + s

        return carry

    lax.fori_loop(0, B, lists, 0)


def greet(axis, others):
    barrier = pltpu.get_barrier_semaphore()
    for ids in others:
        pl.semaphore_signal(barrier, inc=1, device_id=ids, device_id_type=MESH)
    pl.semaphore_wait(barrier, len(others))


def request_kernel(D, req_ref, out_ref, land, send, recv):
    me = lax.axis_index("state")
    peers = [{"state": lax.rem(me + k, D)} for k in range(1, D)]
    greet("state", peers)
    copies = []
    for k in range(1, D):
        c = pltpu.make_async_remote_copy(
            src_ref=req_ref.at[lax.rem(me + k, D)],
            dst_ref=land.at[k],
            send_sem=send.at[k],
            recv_sem=recv.at[k],
            device_id={"state": lax.rem(me + k, D)},
            device_id_type=MESH,
        )
        c.start()
        copies.append(c)
    for c in copies:
        c.wait()
    out_ref[me] = req_ref[me]
    for k in range(1, D):
        out_ref[lax.rem(me - k + D, D)] = land[k]


def gather_kernel(D, cap, half, want_ref, val_ref, *rest):
    outs, sem = rest[:-1], rest[-1]

    def run(h, act):
        def peer(p, carry):
            for s in range(cap):
                w = jnp.maximum(want_ref[p, 0, s], 0)
                act(
                    pltpu.make_async_copy(
                        val_ref.at[w, :, pl.ds(h * half, half)],
                        outs[h].at[p * cap + s],
                        sem.at[h, p * cap + s],
                    )
                )
            return carry

        lax.fori_loop(0, D, peer, 0)

    for h in range(len(outs)):
        run(h, lambda c: c.start())
    for h in range(len(outs)):
        run(h, lambda c: c.wait())


def transposed_dot(tile, right):
    return lax.dot_general(tile, right, (((0,), (0,)), ((), ())), preferred_element_type=jnp.float32)


def continuation(M, first, look_ref, table, tiles):
    weights, values = [], []
    for n in range(M):
        row = look_ref[first + n]
        keep = jnp.where(row >= 0, 1.0, 0.0).astype(jnp.float32)
        tile = tiles(n)
        weights.append(tile * jnp.full(tile.shape, keep, jnp.float32).astype(jnp.bfloat16))
        values.append(table[jnp.maximum(row, 0)])
    return jnp.dot(
        jnp.concatenate(weights, axis=1), jnp.concatenate(values, axis=0), preferred_element_type=jnp.float32
    )


def fetch_value_kernel(G, rows, D, look_ref, from_ref, val_ref, *rest):
    H = (len(rest) - 14) // 2
    outs, rest = rest[:H], rest[H:]
    body, lands = rest[:9], rest[9 : 9 + H - 1]
    acc, table, kept, sem, send, recv = rest[9 + H - 1 :]
    step = pl.program_id(0)
    B, C, V = val_ref.shape[0], outs[0].shape[0], outs[0].shape[2]
    cap = C // D
    me = lax.axis_index("state")

    def copy(h, k):
        to = lax.rem(me + k, D)
        land = table.at[pl.ds(B + me * cap, cap)] if h == 0 else lands[h - 1].at[pl.ds(me * cap, cap)]
        return pltpu.make_async_remote_copy(
            src_ref=outs[h].at[pl.ds(to * cap, cap)],
            dst_ref=land,
            send_sem=send.at[h, k],
            recv_sem=recv.at[h, k],
            device_id={"state": to},
            device_id_type=MESH,
        )

    @pl.when(step == 0)
    def _():
        greet("state", [{"state": lax.rem(me + k, D)} for k in range(1, D)])
        for h in range(H):
            for k in range(1, D):
                copy(h, k).start()
        own = pltpu.make_async_copy(val_ref.at[:, :, pl.ds(0, V)], table.at[pl.ds(0, B)], sem.at[0])
        mine = pltpu.make_async_copy(
            outs[0].at[pl.ds(me * cap, cap)], table.at[pl.ds(B + me * cap, cap)], sem.at[1]
        )
        own.start()
        mine.start()
        own.wait()
        mine.wait()
        for k in range(1, D):
            copy(0, k).wait()

    work(G, rows, look_ref, from_ref, *body, acc, table, kept)

    @pl.when(step == pl.num_programs(0) - 1)
    def _():
        for h in range(1, H):
            for k in range(1, D):
                copy(h, k).wait()


def value_kernel(
    G, rows, col, look_ref, from_ref, val_ref, inc_ref, tiles_ref, cot_ref, util_ref, taste_ref, *rest
):
    before_ref = rest[0]
    value_ref, scaled_ref, out_ref, gu_ref, gt_ref, acc, table, kept, sem = rest[-9:]
    step = pl.program_id(0)
    B, C, V = val_ref.shape[0], inc_ref.shape[0], inc_ref.shape[2]

    @pl.when(step == 0)
    def _():
        own = pltpu.make_async_copy(val_ref.at[:, :, pl.ds(col, V)], table.at[pl.ds(0, B)], sem.at[0])
        far = pltpu.make_async_copy(inc_ref, table.at[pl.ds(B, C)], sem.at[1])
        own.start()
        far.start()
        own.wait()
        far.wait()

    value_ref[:, :col] = before_ref[...]
    work(
        G, rows, look_ref, from_ref, tiles_ref, cot_ref, util_ref, taste_ref,
        value_ref.at[:, col:], scaled_ref, out_ref, gu_ref, gt_ref, acc, table, kept,
    )


def work(
    G, rows, look_ref, from_ref, tiles_ref, cot_ref, util_ref, taste_ref,
    value_ref, scaled_ref, out_ref, gu_ref, gt_ref, acc, table, kept,
):
    step = pl.program_id(0)
    _, A, M, R, _ = tiles_ref.shape
    C = out_ref.shape[0]

    @pl.when(step == 0)
    def _():
        gt_ref[...] = jnp.zeros_like(gt_ref)

    t0, t1 = taste_ref[0:1, :], taste_ref[1:2, :]
    for g in range(G):
        i = step * G + g
        for a in range(A):
            acc[g, a] = continuation(M, (i * A + a) * M, look_ref, table, lambda n: tiles_ref[i, a, n])
    for g in range(G):
        g0 = g1 = 0.0
        cols = [
            jnp.transpose(jnp.broadcast_to(util_ref[a : a + 1, g * R : (g + 1) * R], (R, R))) for a in range(A)
        ]
        for c in range(0, R, rows):
            at = slice(c, c + rows)
            here = slice(g * R + c, g * R + c + rows)
            q0 = cols[0][at, 0:1] + t0 + 0.95 * acc[g, 0, at, :]
            q1 = cols[1][at, 0:1] + t1 + 0.95 * acc[g, 1, at, :]
            gap = q1 - q0
            small = jnp.exp(-jnp.abs(gap))
            total = 1.0 + small
            value_ref[here, :] = jnp.maximum(q0, q1) + jnp.log(total)
            big = cot_ref[here, :].astype(jnp.float32) / total
            little = big * small
            first_wins = gap <= 0.0
            h0 = jnp.where(first_wins, big, little)
            h1 = jnp.where(first_wins, little, big)
            scaled_ref[g, 0, at, :] = (0.95 * h0).astype(jnp.bfloat16)
            scaled_ref[g, 1, at, :] = (0.95 * h1).astype(jnp.bfloat16)
            gu_ref[g, at, 0:1] = jnp.sum(h0, axis=1, keepdims=True)
            gu_ref[g, at, 1:2] = jnp.sum(h1, axis=1, keepdims=True)
            g0, g1 = g0 + h0, g1 + h1
        gt_ref[0:1, :] += jnp.sum(g0, axis=0, keepdims=True)
        gt_ref[1:2, :] += jnp.sum(g1, axis=0, keepdims=True)
    kept[pl.ds(step * G, G)] = scaled_ref[...]

    @pl.when(step == pl.num_programs(0) - 1)
    def _():
        def back(q, carry):
            for u in range(2):
                slot = q * 2 + u
                e = from_ref[slot]
                pair = lax.div(e, M)
                i = lax.div(pair, A)
                a = pair - i * A
                out_ref[slot] = transposed_dot(tiles_ref[i, a, e - pair * M], kept[i, a]).astype(jnp.bfloat16)
            return carry

        lax.fori_loop(0, C // 2, back, 0)


def back_kernel(G, A, M, look_ref, tiles_ref, scaled_ref, adj_ref):
    spare = adj_ref.shape[0] - 1
    step = pl.program_id(0)

    @pl.when(step == 0)
    def _():
        adj_ref[...] = jnp.zeros_like(adj_ref)

    for g in range(G):
        i = step * G + g
        for a in range(A):
            for n in range(M):
                block = look_ref[(i * A + a) * M + n]
                here = jnp.where((block >= 0) & (block < spare), block, spare)
                adj_ref[here] += transposed_dot(tiles_ref[g, a, n], scaled_ref[g, a])


def sums_kernel(D, T, gu_ref, gt_ref, token_ref, after_ref, ou_ref, ot_ref, lu, lt, us, ur, ts, tr):
    ms, mt = lax.axis_index("state"), lax.axis_index("type")
    peers = [{"state": lax.rem(ms + k, D)} for k in range(1, D)]
    peers += [{"type": lax.rem(mt + k, T)} for k in range(1, T)]
    greet("state", peers)
    copies = []
    for k in range(1, T):
        copies.append(
            pltpu.make_async_remote_copy(
                src_ref=gu_ref, dst_ref=lu.at[k], send_sem=us.at[k], recv_sem=ur.at[k],
                device_id={"type": lax.rem(mt + k, T)}, device_id_type=MESH,
            )
        )
    for k in range(1, D):
        copies.append(
            pltpu.make_async_remote_copy(
                src_ref=gt_ref, dst_ref=lt.at[k], send_sem=ts.at[k], recv_sem=tr.at[k],
                device_id={"state": lax.rem(ms + k, D)}, device_id_type=MESH,
            )
        )
    for c in copies:
        c.start()
    for c in copies:
        c.wait()
    lu[0] = gu_ref[...]
    lt[0] = gt_ref[...]
    u = lu[lax.rem(mt, T)]
    for j in range(1, T):
        u = u + lu[lax.rem(mt - j + T, T)]
    t = lt[lax.rem(ms, D)]
    for j in range(1, D):
        t = t + lt[lax.rem(ms - j + D, D)]
    ou_ref[...] = u
    ot_ref[...] = t


def land_kernel(D, cap, want_ref, adj_ref, ret_ref, *rest):
    out_ref, done_ref = rest[-2:]
    done_ref[0] = 0
    out_ref[...] = adj_ref[...]

    def peer(p, carry):
        for s in range(cap):
            w = want_ref[p, 0, s]

            @pl.when(w >= 0)
            def _():
                out_ref[w] += ret_ref[p * cap + s].astype(jnp.float32)

        return carry

    lax.fori_loop(0, D, peer, 0)


def local(value_in, cotangent, state_util, taste, tiles, dest_block, counts):
    B, A, M, R, _ = tiles.shape
    W = value_in.shape[1]
    D = lax.axis_size("state")
    T = lax.axis_size("type")
    cap = max(2, (B + D - 2) // (D - 1))
    E, C = B * A * M, D * cap
    f32, bf16, i32 = jnp.float32, jnp.bfloat16, jnp.int32
    shape = jax.ShapeDtypeStruct
    values = value_in.reshape(B, R, W)

    req, look, origin = pl.pallas_call(
        functools.partial(plan_kernel, (B, A, M, D, cap)),
        out_shape=(shape((D, 1, 128), i32), shape((E,), i32), shape((C,), i32)),
        in_specs=[smem()] * 3,
        out_specs=[smem()] * 3,
        scratch_shapes=[SMEM((D,), i32)],
        name="plan",
    )(lax.axis_index("state").reshape(1).astype(i32), dest_block.transpose(2, 1, 0), counts.T)

    wanted = pl.pallas_call(
        functools.partial(request_kernel, D),
        out_shape=shape((D, 1, 128), i32),
        in_specs=[pl.BlockSpec(memory_space=VMEM)],
        out_specs=pl.BlockSpec(memory_space=VMEM),
        scratch_shapes=[VMEM((D, 1, 128), i32), pltpu.SemaphoreType.DMA((D,)), pltpu.SemaphoreType.DMA((D,))],
        compiler_params=pltpu.CompilerParams(collective_id=0, has_side_effects=True),
        name="request",
    )(req)

    H = 2 if W % 256 == 0 else 1
    V = W // H
    G = 4 if B % 4 == 0 else 1
    outgoing = pl.pallas_call(
        functools.partial(gather_kernel, D, cap, V),
        out_shape=tuple(shape((C, R, V), bf16) for h in range(H)),
        in_specs=[smem(), pl.BlockSpec(memory_space=VMEM)],
        out_specs=[pl.BlockSpec(memory_space=pl.ANY)] * H,
        scratch_shapes=[pltpu.SemaphoreType.DMA((H, C))],
        name="gather",
    )(wanted, values)

    def exchange(x):
        return lax.all_to_all(
            x.reshape(D, cap, R, V), "state", split_axis=0, concat_axis=0, tiled=True
        ).reshape(C, R, V)

    incoming = []

    flops = 2 * E * R * R * W
    value = None
    gus, gts, outbound, scaleds = [], [], [], []
    any_spec = pl.BlockSpec(memory_space=pl.ANY)
    for h in range(H):
        wide = V * (h + 1)
        ins = [
            whole((B, A, M, R, R)),
            pl.BlockSpec((G * R, V), lambda i, h=h: (i, h)),
            pl.BlockSpec((A, G * R), lambda i: (0, i)),
            pl.BlockSpec((A, V), lambda i, h=h: (0, h)),
        ]
        out_shape = [
            shape((B * R, wide), f32), shape((B, A, R, V), bf16), shape((C, R, V), bf16),
            shape((B, R, A), f32), shape((A, V), f32),
        ]
        out_specs = [
            pl.BlockSpec((G * R, wide), lambda i: (i, 0)),
            pl.BlockSpec((G, A, R, V), lambda i: (i, 0, 0, 0)),
            whole((C, R, V)),
            pl.BlockSpec((G, R, A), lambda i: (i, 0, 0)),
            whole((A, V)),
        ]
        scratch = [
            VMEM((G, A, R, V), f32), VMEM((B + C, R, V), bf16), VMEM((B, A, R, V), bf16),
            pltpu.SemaphoreType.DMA((2,)),
        ]
        cost = pl.CostEstimate(flops=flops // H, bytes_accessed=(24 << 20) // H, transcendentals=3 * B * R * V)
        if h == 0:
            value, scaled, out, gu, gt, *incoming = pl.pallas_call(
                functools.partial(fetch_value_kernel, G, 32, D),
                grid=(B // G,),
                out_shape=out_shape + [shape((C, R, V), bf16)] * (H - 1),
                in_specs=[smem(), smem(), any_spec] + [any_spec] * H + ins,
                out_specs=out_specs + [any_spec] * (H - 1),
                scratch_shapes=scratch + [pltpu.SemaphoreType.DMA((H, D)), pltpu.SemaphoreType.DMA((H, D))],
                compiler_params=pltpu.CompilerParams(collective_id=2, has_side_effects=True),
                cost_estimate=cost,
                name="fetch",
            )(look, origin, values, *outgoing, tiles, cotangent, state_util, taste)
        else:
            value, scaled, out, gu, gt = pl.pallas_call(
                functools.partial(value_kernel, G, 32, h * V),
                grid=(B // G,),
                out_shape=out_shape,
                in_specs=[smem(), smem(), any_spec, any_spec] + ins
                + [pl.BlockSpec((G * R, h * V), lambda i: (i, 0))],
                out_specs=out_specs,
                scratch_shapes=scratch,
                cost_estimate=cost,
                name="value",
            )(look, origin, values, incoming[h - 1], tiles, cotangent, state_util, taste, value)
        outbound.append(out)
        scaleds.append(scaled)
        gus.append(gu)
        gts.append(gt)

    adjs = [
        pl.pallas_call(
            functools.partial(back_kernel, G, A, M),
            grid=(B // G,),
            out_shape=shape((B + 1, R, V), f32),
            in_specs=[
                smem(),
                pl.BlockSpec((G, A, M, R, R), lambda i: (i, 0, 0, 0, 0)),
                pl.BlockSpec((G, A, R, V), lambda i: (i, 0, 0, 0)),
            ],
            out_specs=whole((B + 1, R, V)),
            cost_estimate=pl.CostEstimate(flops=flops // H, bytes_accessed=(14 << 20) // H, transcendentals=0),
            name="back",
        )(look, tiles, x)
        for x in scaleds
    ]

    returned = []
    for h in range(H):
        if h > 0:
            outbound[h], adjs[h - 1] = lax.optimization_barrier((outbound[h], adjs[h - 1]))
        returned.append(exchange(outbound[h]))

    adjoint, tokens = None, []
    gu_rows = sum(gus).transpose(2, 0, 1).reshape(A, B * R) / (W * T)
    for h in range(H):
        held = [] if h == 0 else [adjoint]
        adjoint, token = pl.pallas_call(
            functools.partial(land_kernel, D, cap),
            grid=(1,),
            out_shape=(shape((B, R, W), f32), shape((1,), i32)),
            in_specs=[smem(), whole((B, R, V)), whole((C, R, V))]
            + [pl.BlockSpec(memory_space=pl.ANY)] * len(held),
            out_specs=[pl.BlockSpec((B, R, V), lambda j, h=h: (0, 0, h)), smem()],
            input_output_aliases={3 + k: k for k in range(len(held))},
            name="land",
        )(wanted, adjs[h], returned[h], *held)
        tokens.append(token)
    grad_util, grad_taste = pl.pallas_call(
        functools.partial(sums_kernel, D, T),
        out_shape=(shape((A, B * R), f32), shape((A, W), f32)),
        in_specs=[pl.BlockSpec(memory_space=VMEM)] * 2 + [smem(), pl.BlockSpec(memory_space=pl.ANY)],
        out_specs=[pl.BlockSpec(memory_space=VMEM)] * 2,
        scratch_shapes=[
            VMEM((T, A, B * R), f32), VMEM((D, A, W), f32),
            pltpu.SemaphoreType.DMA((T,)), pltpu.SemaphoreType.DMA((T,)),
            pltpu.SemaphoreType.DMA((D,)), pltpu.SemaphoreType.DMA((D,)),
        ],
        compiler_params=pltpu.CompilerParams(collective_id=1, has_side_effects=True),
        cost_estimate=pl.CostEstimate(flops=0, bytes_accessed=8 << 20, transcendentals=0),
        name="sums",
    )(gu_rows, jnp.concatenate(gts, axis=1) / (B * R * D), tokens[0], adjs[-1])

    return value, adjoint.reshape(B * R, W), grad_util, grad_taste


def meet_kernel(dims, sizes, dest_ref, count_ref, plan_ref, pick_ref, mine, land, oh, ssem, rsem):
    B, A, M, D, cap, Q = dims
    f32 = jnp.float32
    y, z = lax.axis_index("groups"), lax.axis_index("state")
    q = y * D + z
    E2 = oh.shape[0]
    mine[...] = jnp.full(mine.shape, -1.0, f32)
    for n in range(M):
        mine[n * A : (n + 1) * A, 0:B] = jnp.where(n < count_ref[...], dest_ref[n], -1).astype(f32)
    own = jnp.transpose(mine[...])[0:B, :]
    lane = lax.broadcasted_iota(jnp.int32, (B, 128), 1).astype(f32)
    oh[A * M * B :, :] = jnp.zeros((E2 - A * M * B, 128), f32)
    total = jnp.zeros((B, 128), f32)
    for c in range(A * M):
        hot = jnp.where(own[:, c : c + 1] == lane, 1.0, 0.0)
        oh[c * B : (c + 1) * B, :] = hot
        total = jnp.maximum(total, hot)
    land[0] = jnp.broadcast_to(jnp.max(total, axis=0, keepdims=True), (8, 128))

    def member(k):
        p = lax.rem(q + k, Q)
        return {"groups": lax.div(p, D), "state": lax.rem(p, D)}

    greet("state", [member(k) for k in range(1, Q)])
    copies = [
        pltpu.make_async_remote_copy(
            src_ref=land.at[0], dst_ref=land.at[k], send_sem=ssem.at[k], recv_sem=rsem.at[k],
            device_id=member(k), device_id_type=MESH,
        )
        for k in range(1, Q)
    ]
    for c in copies:
        c.start()

    seg = lax.div(lax.broadcasted_iota(jnp.int32, (1, 128), 1), B)
    b = lax.broadcasted_iota(jnp.int32, (1, 128), 1).astype(f32)

    def as_row(col):
        full = jnp.broadcast_to(col, (E2, 128))
        return jnp.concatenate(
            [jnp.transpose(full[k : k + 128, :])[0:1, :] for k in range(0, E2, 128)], axis=1
        )

    key_of = b + jnp.where(seg == z, 129.0, 1.0)
    key = jnp.sum(oh[...] * key_of, axis=1, keepdims=True)
    key = jnp.where(key == 0, 300.0, key)
    iq = lax.broadcasted_iota(jnp.int32, (E2, 1), 0)
    order = key * E2 + iq.astype(f32)
    order_row, key_row = as_row(order), as_row(key)
    pos = jnp.sum(jnp.where(order_row < order, 1.0, 0.0), axis=1, keepdims=True)
    less = jnp.sum(jnp.where(key_row < key, 1.0, 0.0), axis=1, keepdims=True)
    wide = lax.broadcasted_iota(jnp.int32, (E2, E2), 1).astype(f32)
    c = lax.div(iq, B)
    entry = ((lax.rem(iq, B) * A + lax.rem(c, A)) * M + lax.div(c, A)).astype(f32)
    move = jnp.where(pos == wide, 1.0, 0.0)
    put = lambda k, v: plan_ref.__setitem__((slice(k, k + 1), slice(0, v.shape[1])), v.astype(jnp.int32))
    plan_ref[...] = jnp.zeros(plan_ref.shape, jnp.int32)
    put(1, jnp.sum(move * entry, axis=0, keepdims=True))
    put(2, jnp.sum(move * jnp.where(pos == less, 0.0, pos), axis=0, keepdims=True))
    last = jnp.sum(jnp.where(key <= key_of, 1.0, 0.0), axis=0, keepdims=True)
    last = last * jnp.max(jnp.where(key == key_of, 1.0, 0.0), axis=0, keepdims=True)
    for k in copies:
        k.wait()

    half = D // 2
    rows, needs = [], []
    for u in range(Q // D):
        g = lax.rem(y + u, Q // D)
        need = [land[lax.rem(q - (g * D + r) + Q, Q)][0:1, :] for r in range(D)]
        end = jnp.where(seg < half, need[D - 1], need[0])
        gate = jnp.where(seg < half, need[half], need[half - 1]) * (1.0 - end)
        rows += [end, gate]
        if u == 0:
            needs = need
    peer = 2 * lax.div(z, 2) + 1 - lax.rem(z, 2)
    mine_need = sum(jnp.where(z == r, needs[r], 0.0) for r in range(D))
    peer_need = sum(jnp.where(peer == r, needs[r], 0.0) for r in range(D))
    at = len(rows)
    rows += [mine_need, peer_need]
    stack = jnp.concatenate(rows + [jnp.zeros((8 - len(rows), 128), f32)], axis=0)
    one = lax.broadcasted_iota(jnp.int32, (128, 128), 0)
    two = lax.broadcasted_iota(jnp.int32, (128, 128), 1)
    same = jnp.where(lax.div(one, B) == lax.div(two, B), 1.0, 0.0)
    below = jnp.where(one < two, same, 0.0)
    rank = jnp.dot(stack, below, preferred_element_type=f32)
    size = jnp.dot(stack, same, preferred_element_type=f32)
    far_any = rows[0] + rows[1]
    far_rank = jnp.where(rows[0] > 0, rank[0:1], size[0:1] + rank[1:2])
    most = size[0:1] + size[1:2]
    for u in range(1, Q // D):
        most = jnp.maximum(most, size[2 * u : 2 * u + 1] + size[2 * u + 1 : 2 * u + 2])
    near_rank, give_rank = rank[at : at + 1], rank[at + 1 : at + 2]
    first = (z * B).astype(f32)
    FX = 2 * cap
    row_of = 1.0 + jnp.where(
        seg == z,
        b - first,
        jnp.where(
            lax.div(seg, 2) == lax.div(z, 2), B + near_rank, B + cap + lax.rem(seg, 2).astype(f32) * FX + far_rank
        ),
    )

    row = jnp.sum(oh[...] * row_of, axis=1, keepdims=True)
    put(0, jnp.sum(jnp.where(entry == wide, row, 0.0), axis=0, keepdims=True))
    slot = lax.broadcasted_iota(jnp.int32, (16, 128), 0).astype(f32)
    here = jnp.where(seg == z, b - first, 0.0)
    mine_here = (seg == z) & (b - first == slot)
    goal = lax.broadcasted_iota(jnp.int32, (64, 128), 0).astype(f32)
    known = (mine_need > 0) | (seg == z)
    lists = [
        jnp.where((give_rank == slot) & (peer_need > 0), here, 0.0),
        jnp.where((far_rank == slot) & (far_any > 0), here, 0.0),
        jnp.where(mine_here & (peer_need > 0), give_rank + 1.0, 0.0),
        jnp.where(mine_here & (far_any > 0), far_rank + 1.0, 0.0),
        jnp.where((row_of - 1.0 == goal) & known, last, 0.0),
    ]
    column = jnp.concatenate([jnp.sum(v, axis=1, keepdims=True) for v in lists], axis=0)
    put(3, jnp.transpose(jnp.broadcast_to(column, (128, 128)))[0:1, :])
    widest = jnp.max(most)
    pick_ref[0] = sum(jnp.where(widest > f, 1, 0).astype(jnp.int32) for f in sizes[:-1])


def sweep_kernel(
    dims, plan, val, cot_hbm, tiles_hbm, util, taste, value_hbm, adj_hbm, retn, retf, gu_ref, gt_ref, *rest
):
    B, A, M, R, V, H, D, T, cap, FX, F, G, rows = dims
    f32, bf16 = jnp.float32, jnp.bfloat16
    E, C, CH = B * A * M, cap // 2, 2
    tables, rest = rest[:H], rest[H:]
    (own, stn, stx, tiles, cot, vout, scaled, P, bst, rel, adj, acc, fold, gacc, gtac, lu, lt,
     lsem, vsem, asem, sn, rn, sx, rx, sf, bsn, brn, bsx, brel, brx, usem, ursem, tsem, trsem) = rest
    z, t = lax.axis_index("state"), lax.axis_index("type")
    side = lax.div(z, 2)
    spot = lax.rem(z, 2)
    peer = 2 * side + 1 - spot
    gate_to = D // 2 - side
    is_gate = (z == D // 2 - 1) | (z == D // 2)
    is_end = jnp.logical_not(is_gate)
    far0 = 2 * (1 - side)
    tail = [C] if F > cap else []

    def span(c):
        return pl.ds(cap, F - cap) if isinstance(c, int) and c == C else pl.ds(c * CH, CH)

    def remote(src, dst, s, r, device):
        return pltpu.make_async_remote_copy(
            src_ref=src, dst_ref=dst, send_sem=s, recv_sem=r, device_id={"state": device}, device_id_type=MESH
        )

    def shift(c, base):
        s = span(c)
        return pl.ds(base + s.start, s.size)

    def fwd_near(h):
        return remote(stn.at[h], tables[h].at[pl.ds(B, cap)], sn.at[h], rn.at[h], peer)

    def fwd_far(h, c, x):
        return remote(
            stx.at[h, span(c)], tables[h].at[shift(c, B + cap + x * FX)], sx.at[h, c], rx.at[h, x, c], gate_to
        )

    def fwd_pass(h, x, c):
        part = tables[h].at[shift(c, B + cap + x * FX)]
        return remote(part, part, sf.at[h, x, c], rx.at[h, x, c], peer)

    def bwd_near(h):
        return remote(bst.at[h, pl.ds(0, cap)], retn.at[:, :, cols(h)], bsn.at[h], brn.at[h], peer)

    def bwd_far(h, x, c):
        return remote(
            bst.at[h, shift(c, cap + x * FX)], retf.at[span(c), :, cols(h)], bsx.at[h, x, c], brx.at[h, c], far0 + x
        )

    def bwd_end(h, x, c):
        return remote(
            bst.at[h, shift(c, cap + x * FX)], rel.at[h, x, span(c)], bsx.at[h, x, c], brel.at[h, x, c], peer
        )

    def cols(h):
        return pl.ds(h * V, V)

    own_copy = pltpu.make_async_copy(val, own, lsem.at[0])
    own_copy.start()
    fills = [
        pltpu.make_async_copy(val.at[:, :, cols(h)], tables[h].at[pl.ds(0, B)], lsem.at[1 + h]) for h in range(H)
    ]
    fills[0].start()
    tile_copy = pltpu.make_async_copy(tiles_hbm, tiles, lsem.at[1 + H])
    cot_copy = pltpu.make_async_copy(cot_hbm, cot, lsem.at[2 + H])
    greet(
        "state",
        [{"state": lax.rem(z + k, D)} for k in range(1, D)] + [{"type": lax.rem(t + k, T)} for k in range(1, T)],
    )
    own_copy.wait()
    for h in range(H):
        for s in range(F):
            stx[h, s] = own[plan[3, 16 + s], :, h * V : (h + 1) * V]
            if s >= 2 and s % CH == 1 and s - CH < cap:
                fwd_far(h, s // CH - 1, spot).start()
        for s in range(cap):
            stn[h, s] = own[plan[3, s], :, h * V : (h + 1) * V]
        if F <= cap + 1:
            fwd_far(h, C - 1, spot).start()
        for c in tail:
            fwd_far(h, c, spot).start()
        fwd_near(h).start()
        if h == 0:
            tile_copy.start()
            cot_copy.start()
            for f in fills[1:]:
                f.start()
    P[0] = jnp.zeros((R, V), f32)
    gtac[...] = jnp.zeros(gtac.shape, f32)

    def pass_on(h, c):
        @pl.when(is_gate)
        def _():
            for x in range(2):
                fwd_far(h, c, x).wait_recv()
                fwd_pass(h, x, c).start()

    def arrived(h):
        fwd_near(h).wait_recv()

        @pl.when(is_gate)
        def _():
            for x in range(2):
                for c in tail:
                    fwd_far(h, c, x).wait_recv()

        @pl.when(is_end)
        def _():
            for x in range(2):
                for c in range(C):
                    fwd_far(h, c, x).wait_recv()

    def value_out(h, k):
        part = pl.ds(k * G * R, G * R)
        return pltpu.make_async_copy(vout.at[lax.rem(k, 2)], value_hbm.at[part, cols(h)], vsem.at[lax.rem(k, 2)])

    def adj_out(h, k):
        part = pl.ds(k * G, G)
        return pltpu.make_async_copy(adj.at[lax.rem(k, 2)], adj_hbm.at[part, :, cols(h)], asem.at[lax.rem(k, 2)])

    def values(h, hook):
        t0, t1 = taste[0:1, h * V : (h + 1) * V], taste[1:2, h * V : (h + 1) * V]

        def step(k, carry):
            @pl.when(k >= 2)
            def _():
                value_out(h, k - 2).wait()

            for g in range(G):
                i = k * G + g
                for a in range(A):
                    weights, blocks = [], []
                    for n in range(M):
                        e = (i * A + a) * M + n
                        row = plan[0, e]
                        keep = jnp.where(row > 0, 1.0, 0.0).astype(f32)
                        tile = tiles[e]
                        weights.append(tile * jnp.full(tile.shape, keep, f32).astype(bf16))
                        blocks.append(tables[h][jnp.maximum(row - 1, 0)])
                    acc[g, a] = jnp.dot(
                        jnp.concatenate(weights, axis=1), jnp.concatenate(blocks, axis=0),
                        preferred_element_type=f32,
                    )
            for g in range(G):
                i = k * G + g
                lanes = pl.ds(pl.multiple_of(i * R, R), R)
                base = [jnp.transpose(jnp.broadcast_to(util[a : a + 1, lanes], (R, R))) for a in range(A)]
                g0 = g1 = 0.0
                for c in range(0, R, rows):
                    at = slice(c, c + rows)
                    here = pl.ds(pl.multiple_of(i * R + c, rows), rows)
                    q0 = base[0][at, 0:1] + t0 + 0.95 * acc[g, 0, at, :]
                    q1 = base[1][at, 0:1] + t1 + 0.95 * acc[g, 1, at, :]
                    gap = q1 - q0
                    small = jnp.exp(-jnp.abs(gap))
                    total = 1.0 + small
                    vout[lax.rem(k, 2), g * R + c : g * R + c + rows, :] = jnp.maximum(q0, q1) + jnp.log(total)
                    big = cot[here, h * V : (h + 1) * V].astype(f32) / total
                    little = big * small
                    first_wins = gap <= 0.0
                    h0 = jnp.where(first_wins, big, little)
                    h1 = jnp.where(first_wins, little, big)
                    scaled[i * A, at, :] = (0.95 * h0).astype(bf16)
                    scaled[i * A + 1, at, :] = (0.95 * h1).astype(bf16)
                    fold[0, at, :] = sum(h0[:, w : w + 128] for w in range(0, V, 128))
                    fold[1, at, :] = sum(h1[:, w : w + 128] for w in range(0, V, 128))
                    g0, g1 = g0 + h0, g1 + h1
                for a in range(A):
                    line = jnp.sum(jnp.transpose(fold[a]), axis=0, keepdims=True)
                    gacc[a : a + 1, lanes] = line if h == 0 else gacc[a : a + 1, lanes] + line
                gtac[0:1, h * V : (h + 1) * V] += jnp.sum(g0, axis=0, keepdims=True)
                gtac[1:2, h * V : (h + 1) * V] += jnp.sum(g1, axis=0, keepdims=True)
            value_out(h, k).start()
            hook(k)
            return carry

        lax.fori_loop(0, B // G, step, 0)
        for k in range(B // G - 2, B // G):
            value_out(h, k).wait()

    def back(lo, hi):
        def step(k, carry):
            for u in range(B):
                e = plan[1, k * B + u]
                P[k * B + u + 1] = P[plan[2, k * B + u]] + transposed_dot(tiles[e], scaled[lax.div(e, M)])
            return carry

        lax.fori_loop(lo, hi, step, 0)

    def stage(h, s):
        bst[h, s] = P[plan[3, 64 + B + s]].astype(bf16)

    def give(h):
        @pl.when(is_end)
        def _():
            for c in range(C):
                for x in range(2):
                    for s in range(c * CH, (c + 1) * CH):
                        stage(h, cap + x * FX + s)
                if c > 0:
                    for x in range(2):
                        bwd_end(h, x, c - 1).start()

        @pl.when(is_gate)
        def _():
            for x in range(2):
                for s in range(cap, F):
                    stage(h, cap + x * FX + s)

        for s in range(cap):
            stage(h, s)

        @pl.when(is_end)
        def _():
            for x in range(2):
                bwd_end(h, x, C - 1).start()

        @pl.when(is_gate)
        def _():
            for x in range(2):
                for c in tail:
                    bwd_far(h, x, c).start()

        bwd_near(h).start()

    def add_on(h, c):
        @pl.when(is_gate)
        def _():
            for x in range(2):
                bwd_end(h, x, c).wait_recv()
                for s in range(CH):
                    u = c * CH + s
                    term = P[plan[3, 64 + B + cap + x * FX + u]] + rel[h, x, u].astype(f32)
                    bst[h, cap + x * FX + u] = term.astype(bf16)
            for x in range(2):
                bwd_far(h, x, c).start()

    def keep(h):
        def step(k, carry):
            @pl.when(k >= 2)
            def _():
                adj_out(h, k - 2).wait()

            for g in range(G):
                adj[lax.rem(k, 2), g] = P[plan[3, 64 + k * G + g]]
            adj_out(h, k).start()
            return carry

        lax.fori_loop(0, B // G, step, 0)
        for k in range(B // G - 2, B // G):
            adj_out(h, k).wait()

    def sums():
        out = []
        for k in range(1, T):
            out.append(
                pltpu.make_async_remote_copy(
                    src_ref=gacc, dst_ref=lu.at[k], send_sem=usem.at[k], recv_sem=ursem.at[k],
                    device_id={"type": lax.rem(t + k, T)}, device_id_type=MESH,
                )
            )
        for k in range(1, D):
            out.append(remote(gtac, lt.at[k], tsem.at[k], trsem.at[k], lax.rem(z + k, D)))
        return out

    for c in range(C):
        pass_on(0, c)
    fills[0].wait()
    arrived(0)
    tile_copy.wait()
    cot_copy.wait()
    for h in range(H):
        steps = B // G

        def hook(k, h=h):
            @pl.when(k < C)
            def _():
                if h + 1 < H:
                    pass_on(h + 1, k)
                if h > 0:
                    add_on(h - 1, k)

        if h > 0:
            fills[h].wait()
            arrived(h)
        values(h, hook)
        back(0, 1)
        give(h)
        if h == H - 1:
            for c in sums():
                c.start()
        back(1, E // B)
        keep(h)
    for c in range(C):
        add_on(H - 1, c)
    for c in sums():
        c.wait()
    lu[0] = gacc[...]
    lt[0] = gtac[...]
    u = lu[lax.rem(t, T)]
    for j in range(1, T):
        u = u + lu[lax.rem(t - j + T, T)]
    w = lt[lax.rem(z, D)]
    for j in range(1, D):
        w = w + lt[lax.rem(z - j + D, D)]
    gu_ref[...] = u / (H * V * T)
    gt_ref[...] = w / (B * R * D)
    for h in range(H):
        fwd_near(h).wait_send()
        bwd_near(h).wait()
        for c in list(range(C)) + tail:
            fwd_far(h, c, spot).wait_send()
            bwd_far(h, 0, c).wait_recv()

        @pl.when(is_gate)
        def _(h=h):
            for x in range(2):
                for c in range(C):
                    fwd_pass(h, x, c).wait_send()
                for c in list(range(C)) + tail:
                    bwd_far(h, x, c).wait_send()

        @pl.when(is_end)
        def _(h=h):
            for x in range(2):
                for c in range(C):
                    bwd_end(h, x, c).wait_send()


def folded(value_in, cotangent, state_util, taste, tiles, dest_block, counts):
    B, A, M, R, _ = tiles.shape
    W = value_in.shape[1]
    D, T = lax.axis_size("state"), lax.axis_size("type")
    Q = lax.axis_size("groups") * D
    cap = (B + D - 2) // (D - 1)
    E, FX, H, G = B * A * M, 2 * cap, 2, 4
    V = W // H
    f32, bf16, i32 = jnp.float32, jnp.bfloat16, jnp.int32
    shape, DMA = jax.ShapeDtypeStruct, pltpu.SemaphoreType.DMA
    vmem = pl.BlockSpec(memory_space=VMEM)
    hbm = pl.BlockSpec(memory_space=pl.ANY)

    sizes = sorted({cap + (cap + 1) // 2, cap + (2 * cap + 2) // 3, FX})
    plan, pick = pl.pallas_call(
        functools.partial(meet_kernel, (B, A, M, D, cap, Q), sizes),
        out_shape=(shape((8, 256), i32), shape((1,), i32)),
        in_specs=[vmem] * 2,
        out_specs=[vmem, smem()],
        scratch_shapes=[VMEM((128, 128), f32), VMEM((Q, 8, 128), f32), VMEM((256, 128), f32), DMA((Q,)), DMA((Q,))],
        compiler_params=pltpu.CompilerParams(collective_id=0, has_side_effects=True),
        name="meet",
    )(dest_block.transpose(2, 1, 0), counts.T)

    def sweep(F, ident):
        dims = (B, A, M, R, V, H, D, T, cap, FX, F, G, 32)
        C = cap // 2
        return pl.pallas_call(
            functools.partial(sweep_kernel, dims),
            out_shape=(
                shape((B * R, W), f32), shape((B, R, W), f32), shape((cap, R, W), bf16), shape((FX, R, W), bf16),
                shape((A, B * R), f32), shape((A, W), f32),
            ),
            in_specs=[smem(), hbm, hbm, hbm, vmem, vmem],
            out_specs=[hbm, hbm, hbm, hbm, vmem, vmem],
            scratch_shapes=[VMEM((B + cap + 2 * FX, R, V), bf16)] * H
            + [
                VMEM((B, R, W), bf16), VMEM((H, cap, R, V), bf16), VMEM((H, FX, R, V), bf16),
                VMEM((E, R, R), bf16), VMEM((B * R, W), bf16), VMEM((2, G * R, V), f32),
                VMEM((B * A, R, V), bf16), VMEM((E + 1, R, V), f32), VMEM((H, cap + 2 * FX, R, V), bf16),
                VMEM((H, 2, cap, R, V), bf16), VMEM((2, G, R, V), f32), VMEM((G, A, R, V), f32),
                VMEM((A, R, 128), f32), VMEM((A, B * R), f32), VMEM((A, W), f32),
                VMEM((T, A, B * R), f32), VMEM((D, A, W), f32),
                DMA((3 + H,)), DMA((2,)), DMA((2,)), DMA((H,)), DMA((H,)),
                DMA((H, C + 1)), DMA((H, 2, C + 1)), DMA((H, 2, C)), DMA((H,)), DMA((H,)),
                DMA((H, 2, C + 1)), DMA((H, 2, C)), DMA((H, C + 1)),
                DMA((T,)), DMA((T,)), DMA((D,)), DMA((D,)),
            ],
            compiler_params=pltpu.CompilerParams(
                collective_id=ident, has_side_effects=True, vmem_limit_bytes=56_000_000
            ),
            cost_estimate=pl.CostEstimate(flops=4 * E * R * R * W, bytes_accessed=20 << 20, transcendentals=3 * B * R * W),
            name="sweep%d" % F,
        )

    held = lax.switch(
        pick.reshape(()), [sweep(f, 1 + k) for k, f in enumerate(sizes)],
        plan, value_in.reshape(B, R, W), cotangent, tiles.reshape(E, R, R), state_util, taste,
    )
    value, adjoint, grad_util, grad_taste = pl.pallas_call(
        functools.partial(finish_kernel, G),
        in_specs=[smem(), hbm, hbm, hbm, hbm, vmem, vmem],
        out_specs=[hbm, hbm, vmem, vmem],
        out_shape=[shape(held[k].shape, f32) for k in (0, 1, 4, 5)],
        scratch_shapes=[
            VMEM((cap, R, W), bf16), VMEM((FX, R, W), bf16), VMEM((B * R, W), f32), VMEM((B, R, W), f32),
            VMEM((B, R, W), f32), DMA((2,)), DMA((4, B // G)),
        ],
        name="finish",
    )(plan, *held)
    return value, adjoint.reshape(B * R, W), grad_util, grad_taste


def finish_kernel(
    G, plan, value_hbm, part_hbm, near_hbm, far_hbm, gu_ref, gt_ref, value, adjoint, gu, gt,
    near_ref, far_ref, held, part, total, rsem, sem
):
    f32 = jnp.float32
    B, R, _ = part.shape

    def piece(n, k):
        rows, blocks = pl.ds(k * G * R, G * R), pl.ds(k * G, G)
        src, dst, at = (
            (part_hbm, part, blocks), (value_hbm, held, rows), (total, adjoint, blocks), (held, value, rows)
        )[n]
        return pltpu.make_async_copy(src.at[at], dst.at[at], sem.at[n, k])

    near_copy = pltpu.make_async_copy(near_hbm, near_ref, rsem.at[0])
    far_copy = pltpu.make_async_copy(far_hbm, far_ref, rsem.at[1])
    steps = range(B // G)
    near_copy.start()
    far_copy.start()
    for k in steps:
        piece(1, k).start()
    for k in steps:
        piece(0, k).start()
    gu[...] = gu_ref[...]
    gt[...] = gt_ref[...]
    for k in steps:
        piece(1, k).wait()
        piece(3, k).start()
    near_copy.wait()
    far_copy.wait()
    for k in steps:
        piece(0, k).wait()
        for j in range(k * G, (k + 1) * G):
            near, far = plan[3, 32 + j], plan[3, 48 + j]
            add = jnp.where(near > 0, near_ref[jnp.maximum(near - 1, 0)].astype(f32), 0.0)
            total[j] = part[j] + add + jnp.where(far > 0, far_ref[jnp.maximum(far - 1, 0)].astype(f32), 0.0)
        piece(2, k).start()
    for k in steps:
        piece(3, k).wait()
        piece(2, k).wait()


def choose(*args):
    B, A, M, R, _ = args[4].shape
    D = lax.axis_size("state")
    cap = (B + D - 2) // (D - 1)
    fits = D * B <= 128 and 128 < B * A * M <= 256 and cap % 2 == 0 and B % 4 == 0 and R == 128
    if D == 4 and fits and args[0].shape[1] % 256 == 0:
        return folded(*args)
    return local(*args)


def solution(mesh):
    rows = ("groups", "state")
    return jax.shard_map(
        choose,
        mesh=mesh,
        in_specs=(
            P(rows, "type"),
            P(rows, "type"),
            P(None, rows),
            P(None, ("groups", "type")),
            P(rows, None, None, None, None),
            P(rows, None, None),
            P(rows, None),
        ),
        out_specs=(P(rows, "type"), P(rows, "type"), P(None, rows), P(None, ("groups", "type"))),
        check_vma=False,
    )
```

```python
import functools

import jax
import jax.numpy as jnp
from jax import lax
from jax.experimental import pallas as pl
from jax.experimental.pallas import tpu as pltpu
from jax.sharding import PartitionSpec as P

VMEM = pltpu.VMEM
SMEM = pltpu.SMEM
MESH = pl.DeviceIdType.MESH


def smem():
    return pl.BlockSpec(memory_space=SMEM)


def whole(shape):
    return pl.BlockSpec(shape, lambda *g: (0,) * len(shape))


def plan_kernel(dims, me_ref, dest_ref, count_ref, req_ref, look_ref, from_ref, fill):
    B, A, M, D, cap = dims
    me = me_ref[0]

    def clear(p, carry):
        fill[p] = 0
        for s in range(cap):
            req_ref[p, 0, s] = -1
            from_ref[p * cap + s] = 0
        return carry

    lax.fori_loop(0, D, clear, 0)

    def lists(i, carry):
        for a in range(A):
            count = count_ref[a, i]
            for n in range(M):
                e = (i * A + a) * M + n
                dest = dest_ref[n, a, i]
                owner = lax.div(dest, B)
                block = dest - owner * B
                used = n < count
                look_ref[e] = jnp.where(used & (owner == me), block, -1)

                @pl.when(used & (owner != me))
                def _():
                    s = fill[owner]
                    fill[owner] = s + 1
                    req_ref[owner, 0, s] = block
                    from_ref[owner * cap + s] = e
                    look_ref[e] = B + owner * cap + s

        return carry

    lax.fori_loop(0, B, lists, 0)


def greet(axis, others):
    barrier = pltpu.get_barrier_semaphore()
    for ids in others:
        pl.semaphore_signal(barrier, inc=1, device_id=ids, device_id_type=MESH)
    pl.semaphore_wait(barrier, len(others))


def request_kernel(D, req_ref, out_ref, land, send, recv):
    me = lax.axis_index("state")
    peers = [{"state": lax.rem(me + k, D)} for k in range(1, D)]
    greet("state", peers)
    copies = []
    for k in range(1, D):
        c = pltpu.make_async_remote_copy(
            src_ref=req_ref.at[lax.rem(me + k, D)],
            dst_ref=land.at[k],
            send_sem=send.at[k],
            recv_sem=recv.at[k],
            device_id={"state": lax.rem(me + k, D)},
            device_id_type=MESH,
        )
        c.start()
        copies.append(c)
    for c in copies:
        c.wait()
    out_ref[me] = req_ref[me]
    for k in range(1, D):
        out_ref[lax.rem(me - k + D, D)] = land[k]


def gather_kernel(D, cap, half, want_ref, val_ref, *rest):
    outs, sem = rest[:-1], rest[-1]

    def run(h, act):
        def peer(p, carry):
            for s in range(cap):
                w = jnp.maximum(want_ref[p, 0, s], 0)
                act(
                    pltpu.make_async_copy(
                        val_ref.at[w, :, pl.ds(h * half, half)],
                        outs[h].at[p * cap + s],
                        sem.at[h, p * cap + s],
                    )
                )
            return carry

        lax.fori_loop(0, D, peer, 0)

    for h in range(len(outs)):
        run(h, lambda c: c.start())
    for h in range(len(outs)):
        run(h, lambda c: c.wait())


def transposed_dot(tile, right):
    return lax.dot_general(tile, right, (((0,), (0,)), ((), ())), preferred_element_type=jnp.float32)


def continuation(M, first, look_ref, table, tiles):
    weights, values = [], []
    for n in range(M):
        row = look_ref[first + n]
        keep = jnp.where(row >= 0, 1.0, 0.0).astype(jnp.float32)
        tile = tiles(n)
        weights.append(tile * jnp.full(tile.shape, keep, jnp.float32).astype(jnp.bfloat16))
        values.append(table[jnp.maximum(row, 0)])
    return jnp.dot(
        jnp.concatenate(weights, axis=1), jnp.concatenate(values, axis=0), preferred_element_type=jnp.float32
    )


def fetch_value_kernel(G, rows, D, look_ref, from_ref, val_ref, *rest):
    H = (len(rest) - 14) // 2
    outs, rest = rest[:H], rest[H:]
    body, lands = rest[:9], rest[9 : 9 + H - 1]
    acc, table, kept, sem, send, recv = rest[9 + H - 1 :]
    step = pl.program_id(0)
    B, C, V = val_ref.shape[0], outs[0].shape[0], outs[0].shape[2]
    cap = C // D
    me = lax.axis_index("state")

    def copy(h, k):
        to = lax.rem(me + k, D)
        land = table.at[pl.ds(B + me * cap, cap)] if h == 0 else lands[h - 1].at[pl.ds(me * cap, cap)]
        return pltpu.make_async_remote_copy(
            src_ref=outs[h].at[pl.ds(to * cap, cap)],
            dst_ref=land,
            send_sem=send.at[h, k],
            recv_sem=recv.at[h, k],
            device_id={"state": to},
            device_id_type=MESH,
        )

    @pl.when(step == 0)
    def _():
        greet("state", [{"state": lax.rem(me + k, D)} for k in range(1, D)])
        for h in range(H):
            for k in range(1, D):
                copy(h, k).start()
        own = pltpu.make_async_copy(val_ref.at[:, :, pl.ds(0, V)], table.at[pl.ds(0, B)], sem.at[0])
        mine = pltpu.make_async_copy(
            outs[0].at[pl.ds(me * cap, cap)], table.at[pl.ds(B + me * cap, cap)], sem.at[1]
        )
        own.start()
        mine.start()
        own.wait()
        mine.wait()
        for k in range(1, D):
            copy(0, k).wait()

    work(G, rows, look_ref, from_ref, *body, acc, table, kept)

    @pl.when(step == pl.num_programs(0) - 1)
    def _():
        for h in range(1, H):
            for k in range(1, D):
                copy(h, k).wait()


def value_kernel(
    G, rows, col, look_ref, from_ref, val_ref, inc_ref, tiles_ref, cot_ref, util_ref, taste_ref, *rest
):
    before_ref = rest[0]
    value_ref, scaled_ref, out_ref, gu_ref, gt_ref, acc, table, kept, sem = rest[-9:]
    step = pl.program_id(0)
    B, C, V = val_ref.shape[0], inc_ref.shape[0], inc_ref.shape[2]

    @pl.when(step == 0)
    def _():
        own = pltpu.make_async_copy(val_ref.at[:, :, pl.ds(col, V)], table.at[pl.ds(0, B)], sem.at[0])
        far = pltpu.make_async_copy(inc_ref, table.at[pl.ds(B, C)], sem.at[1])
        own.start()
        far.start()
        own.wait()
        far.wait()

    value_ref[:, :col] = before_ref[...]
    work(
        G, rows, look_ref, from_ref, tiles_ref, cot_ref, util_ref, taste_ref,
        value_ref.at[:, col:], scaled_ref, out_ref, gu_ref, gt_ref, acc, table, kept,
    )


def work(
    G, rows, look_ref, from_ref, tiles_ref, cot_ref, util_ref, taste_ref,
    value_ref, scaled_ref, out_ref, gu_ref, gt_ref, acc, table, kept,
):
    step = pl.program_id(0)
    _, A, M, R, _ = tiles_ref.shape
    C = out_ref.shape[0]

    @pl.when(step == 0)
    def _():
        gt_ref[...] = jnp.zeros_like(gt_ref)

    t0, t1 = taste_ref[0:1, :], taste_ref[1:2, :]
    for g in range(G):
        i = step * G + g
        for a in range(A):
            acc[g, a] = continuation(M, (i * A + a) * M, look_ref, table, lambda n: tiles_ref[i, a, n])
    for g in range(G):
        g0 = g1 = 0.0
        cols = [
            jnp.transpose(jnp.broadcast_to(util_ref[a : a + 1, g * R : (g + 1) * R], (R, R))) for a in range(A)
        ]
        for c in range(0, R, rows):
            at = slice(c, c + rows)
            here = slice(g * R + c, g * R + c + rows)
            q0 = cols[0][at, 0:1] + t0 + 0.95 * acc[g, 0, at, :]
            q1 = cols[1][at, 0:1] + t1 + 0.95 * acc[g, 1, at, :]
            gap = q1 - q0
            small = jnp.exp(-jnp.abs(gap))
            total = 1.0 + small
            value_ref[here, :] = jnp.maximum(q0, q1) + jnp.log(total)
            big = cot_ref[here, :].astype(jnp.float32) / total
            little = big * small
            first_wins = gap <= 0.0
            h0 = jnp.where(first_wins, big, little)
            h1 = jnp.where(first_wins, little, big)
            scaled_ref[g, 0, at, :] = (0.95 * h0).astype(jnp.bfloat16)
            scaled_ref[g, 1, at, :] = (0.95 * h1).astype(jnp.bfloat16)
            gu_ref[g, at, 0:1] = jnp.sum(h0, axis=1, keepdims=True)
            gu_ref[g, at, 1:2] = jnp.sum(h1, axis=1, keepdims=True)
            g0, g1 = g0 + h0, g1 + h1
        gt_ref[0:1, :] += jnp.sum(g0, axis=0, keepdims=True)
        gt_ref[1:2, :] += jnp.sum(g1, axis=0, keepdims=True)
    kept[pl.ds(step * G, G)] = scaled_ref[...]

    @pl.when(step == pl.num_programs(0) - 1)
    def _():
        def back(q, carry):
            for u in range(2):
                slot = q * 2 + u
                e = from_ref[slot]
                pair = lax.div(e, M)
                i = lax.div(pair, A)
                a = pair - i * A
                out_ref[slot] = transposed_dot(tiles_ref[i, a, e - pair * M], kept[i, a]).astype(jnp.bfloat16)
            return carry

        lax.fori_loop(0, C // 2, back, 0)


def back_kernel(G, A, M, look_ref, tiles_ref, scaled_ref, adj_ref):
    spare = adj_ref.shape[0] - 1
    step = pl.program_id(0)

    @pl.when(step == 0)
    def _():
        adj_ref[...] = jnp.zeros_like(adj_ref)

    for g in range(G):
        i = step * G + g
        for a in range(A):
            for n in range(M):
                block = look_ref[(i * A + a) * M + n]
                here = jnp.where((block >= 0) & (block < spare), block, spare)
                adj_ref[here] += transposed_dot(tiles_ref[g, a, n], scaled_ref[g, a])


def sums_kernel(D, T, gu_ref, gt_ref, token_ref, after_ref, ou_ref, ot_ref, lu, lt, us, ur, ts, tr):
    ms, mt = lax.axis_index("state"), lax.axis_index("type")
    peers = [{"state": lax.rem(ms + k, D)} for k in range(1, D)]
    peers += [{"type": lax.rem(mt + k, T)} for k in range(1, T)]
    greet("state", peers)
    copies = []
    for k in range(1, T):
        copies.append(
            pltpu.make_async_remote_copy(
                src_ref=gu_ref, dst_ref=lu.at[k], send_sem=us.at[k], recv_sem=ur.at[k],
                device_id={"type": lax.rem(mt + k, T)}, device_id_type=MESH,
            )
        )
    for k in range(1, D):
        copies.append(
            pltpu.make_async_remote_copy(
                src_ref=gt_ref, dst_ref=lt.at[k], send_sem=ts.at[k], recv_sem=tr.at[k],
                device_id={"state": lax.rem(ms + k, D)}, device_id_type=MESH,
            )
        )
    for c in copies:
        c.start()
    for c in copies:
        c.wait()
    lu[0] = gu_ref[...]
    lt[0] = gt_ref[...]
    u = lu[lax.rem(mt, T)]
    for j in range(1, T):
        u = u + lu[lax.rem(mt - j + T, T)]
    t = lt[lax.rem(ms, D)]
    for j in range(1, D):
        t = t + lt[lax.rem(ms - j + D, D)]
    ou_ref[...] = u
    ot_ref[...] = t


def land_kernel(D, cap, want_ref, adj_ref, ret_ref, *rest):
    out_ref, done_ref = rest[-2:]
    done_ref[0] = 0
    out_ref[...] = adj_ref[...]

    def peer(p, carry):
        for s in range(cap):
            w = want_ref[p, 0, s]

            @pl.when(w >= 0)
            def _():
                out_ref[w] += ret_ref[p * cap + s].astype(jnp.float32)

        return carry

    lax.fori_loop(0, D, peer, 0)


def local(value_in, cotangent, state_util, taste, tiles, dest_block, counts):
    B, A, M, R, _ = tiles.shape
    W = value_in.shape[1]
    D = lax.axis_size("state")
    T = lax.axis_size("type")
    cap = max(2, (B + D - 2) // (D - 1))
    E, C = B * A * M, D * cap
    f32, bf16, i32 = jnp.float32, jnp.bfloat16, jnp.int32
    shape = jax.ShapeDtypeStruct
    values = value_in.reshape(B, R, W)

    req, look, origin = pl.pallas_call(
        functools.partial(plan_kernel, (B, A, M, D, cap)),
        out_shape=(shape((D, 1, 128), i32), shape((E,), i32), shape((C,), i32)),
        in_specs=[smem()] * 3,
        out_specs=[smem()] * 3,
        scratch_shapes=[SMEM((D,), i32)],
        name="plan",
    )(lax.axis_index("state").reshape(1).astype(i32), dest_block.transpose(2, 1, 0), counts.T)

    wanted = pl.pallas_call(
        functools.partial(request_kernel, D),
        out_shape=shape((D, 1, 128), i32),
        in_specs=[pl.BlockSpec(memory_space=VMEM)],
        out_specs=pl.BlockSpec(memory_space=VMEM),
        scratch_shapes=[VMEM((D, 1, 128), i32), pltpu.SemaphoreType.DMA((D,)), pltpu.SemaphoreType.DMA((D,))],
        compiler_params=pltpu.CompilerParams(collective_id=0, has_side_effects=True),
        name="request",
    )(req)

    H = 2 if W % 256 == 0 else 1
    V = W // H
    G = 4 if B % 4 == 0 else 1
    outgoing = pl.pallas_call(
        functools.partial(gather_kernel, D, cap, V),
        out_shape=tuple(shape((C, R, V), bf16) for h in range(H)),
        in_specs=[smem(), pl.BlockSpec(memory_space=VMEM)],
        out_specs=[pl.BlockSpec(memory_space=pl.ANY)] * H,
        scratch_shapes=[pltpu.SemaphoreType.DMA((H, C))],
        name="gather",
    )(wanted, values)

    def exchange(x):
        return lax.all_to_all(
            x.reshape(D, cap, R, V), "state", split_axis=0, concat_axis=0, tiled=True
        ).reshape(C, R, V)

    incoming = []

    flops = 2 * E * R * R * W
    value = None
    gus, gts, outbound, scaleds = [], [], [], []
    any_spec = pl.BlockSpec(memory_space=pl.ANY)
    for h in range(H):
        wide = V * (h + 1)
        ins = [
            whole((B, A, M, R, R)),
            pl.BlockSpec((G * R, V), lambda i, h=h: (i, h)),
            pl.BlockSpec((A, G * R), lambda i: (0, i)),
            pl.BlockSpec((A, V), lambda i, h=h: (0, h)),
        ]
        out_shape = [
            shape((B * R, wide), f32), shape((B, A, R, V), bf16), shape((C, R, V), bf16),
            shape((B, R, A), f32), shape((A, V), f32),
        ]
        out_specs = [
            pl.BlockSpec((G * R, wide), lambda i: (i, 0)),
            pl.BlockSpec((G, A, R, V), lambda i: (i, 0, 0, 0)),
            whole((C, R, V)),
            pl.BlockSpec((G, R, A), lambda i: (i, 0, 0)),
            whole((A, V)),
        ]
        scratch = [
            VMEM((G, A, R, V), f32), VMEM((B + C, R, V), bf16), VMEM((B, A, R, V), bf16),
            pltpu.SemaphoreType.DMA((2,)),
        ]
        cost = pl.CostEstimate(flops=flops // H, bytes_accessed=(24 << 20) // H, transcendentals=3 * B * R * V)
        if h == 0:
            value, scaled, out, gu, gt, *incoming = pl.pallas_call(
                functools.partial(fetch_value_kernel, G, 32, D),
                grid=(B // G,),
                out_shape=out_shape + [shape((C, R, V), bf16)] * (H - 1),
                in_specs=[smem(), smem(), any_spec] + [any_spec] * H + ins,
                out_specs=out_specs + [any_spec] * (H - 1),
                scratch_shapes=scratch + [pltpu.SemaphoreType.DMA((H, D)), pltpu.SemaphoreType.DMA((H, D))],
                compiler_params=pltpu.CompilerParams(collective_id=2, has_side_effects=True),
                cost_estimate=cost,
                name="fetch",
            )(look, origin, values, *outgoing, tiles, cotangent, state_util, taste)
        else:
            value, scaled, out, gu, gt = pl.pallas_call(
                functools.partial(value_kernel, G, 32, h * V),
                grid=(B // G,),
                out_shape=out_shape,
                in_specs=[smem(), smem(), any_spec, any_spec] + ins
                + [pl.BlockSpec((G * R, h * V), lambda i: (i, 0))],
                out_specs=out_specs,
                scratch_shapes=scratch,
                cost_estimate=cost,
                name="value",
            )(look, origin, values, incoming[h - 1], tiles, cotangent, state_util, taste, value)
        outbound.append(out)
        scaleds.append(scaled)
        gus.append(gu)
        gts.append(gt)

    adjs = [
        pl.pallas_call(
            functools.partial(back_kernel, G, A, M),
            grid=(B // G,),
            out_shape=shape((B + 1, R, V), f32),
            in_specs=[
                smem(),
                pl.BlockSpec((G, A, M, R, R), lambda i: (i, 0, 0, 0, 0)),
                pl.BlockSpec((G, A, R, V), lambda i: (i, 0, 0, 0)),
            ],
            out_specs=whole((B + 1, R, V)),
            cost_estimate=pl.CostEstimate(flops=flops // H, bytes_accessed=(14 << 20) // H, transcendentals=0),
            name="back",
        )(look, tiles, x)
        for x in scaleds
    ]

    returned = []
    for h in range(H):
        if h > 0:
            outbound[h], adjs[h - 1] = lax.optimization_barrier((outbound[h], adjs[h - 1]))
        returned.append(exchange(outbound[h]))

    adjoint, tokens = None, []
    gu_rows = sum(gus).transpose(2, 0, 1).reshape(A, B * R) / (W * T)
    for h in range(H):
        held = [] if h == 0 else [adjoint]
        adjoint, token = pl.pallas_call(
            functools.partial(land_kernel, D, cap),
            grid=(1,),
            out_shape=(shape((B, R, W), f32), shape((1,), i32)),
            in_specs=[smem(), whole((B, R, V)), whole((C, R, V))]
            + [pl.BlockSpec(memory_space=pl.ANY)] * len(held),
            out_specs=[pl.BlockSpec((B, R, V), lambda j, h=h: (0, 0, h)), smem()],
            input_output_aliases={3 + k: k for k in range(len(held))},
            name="land",
        )(wanted, adjs[h], returned[h], *held)
        tokens.append(token)
    grad_util, grad_taste = pl.pallas_call(
        functools.partial(sums_kernel, D, T),
        out_shape=(shape((A, B * R), f32), shape((A, W), f32)),
        in_specs=[pl.BlockSpec(memory_space=VMEM)] * 2 + [smem(), pl.BlockSpec(memory_space=pl.ANY)],
        out_specs=[pl.BlockSpec(memory_space=VMEM)] * 2,
        scratch_shapes=[
            VMEM((T, A, B * R), f32), VMEM((D, A, W), f32),
            pltpu.SemaphoreType.DMA((T,)), pltpu.SemaphoreType.DMA((T,)),
            pltpu.SemaphoreType.DMA((D,)), pltpu.SemaphoreType.DMA((D,)),
        ],
        compiler_params=pltpu.CompilerParams(collective_id=1, has_side_effects=True),
        cost_estimate=pl.CostEstimate(flops=0, bytes_accessed=8 << 20, transcendentals=0),
        name="sums",
    )(gu_rows, jnp.concatenate(gts, axis=1) / (B * R * D), tokens[0], adjs[-1])

    return value, adjoint.reshape(B * R, W), grad_util, grad_taste


def meet_kernel(dims, sizes, dest_ref, count_ref, plan_ref, pick_ref, mine, land, oh, ssem, rsem):
    B, A, M, D, cap, Q = dims
    f32 = jnp.float32
    y, z = lax.axis_index("groups"), lax.axis_index("state")
    q = y * D + z
    E2 = oh.shape[0]
    mine[...] = jnp.full(mine.shape, -1.0, f32)
    for n in range(M):
        mine[n * A : (n + 1) * A, 0:B] = jnp.where(n < count_ref[...], dest_ref[n], -1).astype(f32)
    own = jnp.transpose(mine[...])[0:B, :]
    lane = lax.broadcasted_iota(jnp.int32, (B, 128), 1).astype(f32)
    oh[A * M * B :, :] = jnp.zeros((E2 - A * M * B, 128), f32)
    total = jnp.zeros((B, 128), f32)
    for c in range(A * M):
        hot = jnp.where(own[:, c : c + 1] == lane, 1.0, 0.0)
        oh[c * B : (c + 1) * B, :] = hot
        total = jnp.maximum(total, hot)
    land[0] = jnp.broadcast_to(jnp.max(total, axis=0, keepdims=True), (8, 128))

    def member(k):
        p = lax.rem(q + k, Q)
        return {"groups": lax.div(p, D), "state": lax.rem(p, D)}

    greet("state", [member(k) for k in range(1, Q)])
    copies = [
        pltpu.make_async_remote_copy(
            src_ref=land.at[0], dst_ref=land.at[k], send_sem=ssem.at[k], recv_sem=rsem.at[k],
            device_id=member(k), device_id_type=MESH,
        )
        for k in range(1, Q)
    ]
    for c in copies:
        c.start()

    seg = lax.div(lax.broadcasted_iota(jnp.int32, (1, 128), 1), B)
    b = lax.broadcasted_iota(jnp.int32, (1, 128), 1).astype(f32)

    def as_row(col):
        full = jnp.broadcast_to(col, (E2, 128))
        return jnp.concatenate(
            [jnp.transpose(full[k : k + 128, :])[0:1, :] for k in range(0, E2, 128)], axis=1
        )

    key_of = b + jnp.where(seg == z, 129.0, 1.0)
    key = jnp.sum(oh[...] * key_of, axis=1, keepdims=True)
    key = jnp.where(key == 0, 300.0, key)
    iq = lax.broadcasted_iota(jnp.int32, (E2, 1), 0)
    order = key * E2 + iq.astype(f32)
    order_row, key_row = as_row(order), as_row(key)
    pos = jnp.sum(jnp.where(order_row < order, 1.0, 0.0), axis=1, keepdims=True)
    less = jnp.sum(jnp.where(key_row < key, 1.0, 0.0), axis=1, keepdims=True)
    wide = lax.broadcasted_iota(jnp.int32, (E2, E2), 1).astype(f32)
    c = lax.div(iq, B)
    entry = ((lax.rem(iq, B) * A + lax.rem(c, A)) * M + lax.div(c, A)).astype(f32)
    move = jnp.where(pos == wide, 1.0, 0.0)
    put = lambda k, v: plan_ref.__setitem__((slice(k, k + 1), slice(0, v.shape[1])), v.astype(jnp.int32))
    plan_ref[...] = jnp.zeros(plan_ref.shape, jnp.int32)
    put(1, jnp.sum(move * entry, axis=0, keepdims=True))
    put(2, jnp.sum(move * jnp.where(pos == less, 0.0, pos), axis=0, keepdims=True))
    last = jnp.sum(jnp.where(key <= key_of, 1.0, 0.0), axis=0, keepdims=True)
    last = last * jnp.max(jnp.where(key == key_of, 1.0, 0.0), axis=0, keepdims=True)
    for k in copies:
        k.wait()

    half = D // 2
    rows, needs = [], []
    for u in range(Q // D):
        g = lax.rem(y + u, Q // D)
        need = [land[lax.rem(q - (g * D + r) + Q, Q)][0:1, :] for r in range(D)]
        end = jnp.where(seg < half, need[D - 1], need[0])
        gate = jnp.where(seg < half, need[half], need[half - 1]) * (1.0 - end)
        rows += [end, gate]
        if u == 0:
            needs = need
    peer = 2 * lax.div(z, 2) + 1 - lax.rem(z, 2)
    mine_need = sum(jnp.where(z == r, needs[r], 0.0) for r in range(D))
    peer_need = sum(jnp.where(peer == r, needs[r], 0.0) for r in range(D))
    at = len(rows)
    rows += [mine_need, peer_need]
    stack = jnp.concatenate(rows + [jnp.zeros((8 - len(rows), 128), f32)], axis=0)
    one = lax.broadcasted_iota(jnp.int32, (128, 128), 0)
    two = lax.broadcasted_iota(jnp.int32, (128, 128), 1)
    same = jnp.where(lax.div(one, B) == lax.div(two, B), 1.0, 0.0)
    below = jnp.where(one < two, same, 0.0)
    rank = jnp.dot(stack, below, preferred_element_type=f32)
    size = jnp.dot(stack, same, preferred_element_type=f32)
    far_any = rows[0] + rows[1]
    far_rank = jnp.where(rows[0] > 0, rank[0:1], size[0:1] + rank[1:2])
    most = size[0:1] + size[1:2]
    for u in range(1, Q // D):
        most = jnp.maximum(most, size[2 * u : 2 * u + 1] + size[2 * u + 1 : 2 * u + 2])
    near_rank, give_rank = rank[at : at + 1], rank[at + 1 : at + 2]
    first = (z * B).astype(f32)
    FX = 2 * cap
    row_of = 1.0 + jnp.where(
        seg == z,
        b - first,
        jnp.where(
            lax.div(seg, 2) == lax.div(z, 2), B + near_rank, B + cap + lax.rem(seg, 2).astype(f32) * FX + far_rank
        ),
    )

    row = jnp.sum(oh[...] * row_of, axis=1, keepdims=True)
    put(0, jnp.sum(jnp.where(entry == wide, row, 0.0), axis=0, keepdims=True))
    slot = lax.broadcasted_iota(jnp.int32, (16, 128), 0).astype(f32)
    here = jnp.where(seg == z, b - first, 0.0)
    mine_here = (seg == z) & (b - first == slot)
    goal = lax.broadcasted_iota(jnp.int32, (64, 128), 0).astype(f32)
    known = (mine_need > 0) | (seg == z)
    lists = [
        jnp.where((give_rank == slot) & (peer_need > 0), here, 0.0),
        jnp.where((far_rank == slot) & (far_any > 0), here, 0.0),
        jnp.where(mine_here & (peer_need > 0), give_rank + 1.0, 0.0),
        jnp.where(mine_here & (far_any > 0), far_rank + 1.0, 0.0),
        jnp.where((row_of - 1.0 == goal) & known, last, 0.0),
    ]
    column = jnp.concatenate([jnp.sum(v, axis=1, keepdims=True) for v in lists], axis=0)
    put(3, jnp.transpose(jnp.broadcast_to(column, (128, 128)))[0:1, :])
    widest = jnp.max(most)
    pick_ref[0] = sum(jnp.where(widest > f, 1, 0).astype(jnp.int32) for f in sizes[:-1])


def sweep_kernel(
    dims, plan, val, cot_hbm, tiles_hbm, util, taste, value_ref, adj_ref, retn, retf, gu_ref, gt_ref, *rest
):
    B, A, M, R, V, H, D, T, cap, FX, F, G, rows = dims
    f32, bf16 = jnp.float32, jnp.bfloat16
    E, C, CH = B * A * M, cap // 2, 2
    tables, rest = rest[:H], rest[H:]
    (own, stn, stx, tiles, cot, scaled, P, bst, rel, acc, fold, gacc, gtac, lu, lt,
     lsem, sn, rn, sx, rx, sf, bsn, brn, bsx, brel, brx, usem, ursem, tsem, trsem) = rest
    z, t = lax.axis_index("state"), lax.axis_index("type")
    side = lax.div(z, 2)
    spot = lax.rem(z, 2)
    peer = 2 * side + 1 - spot
    gate_to = D // 2 - side
    is_gate = (z == D // 2 - 1) | (z == D // 2)
    is_end = jnp.logical_not(is_gate)
    far0 = 2 * (1 - side)
    tail = [C] if F > cap else []

    def span(c):
        return pl.ds(cap, F - cap) if isinstance(c, int) and c == C else pl.ds(c * CH, CH)

    def remote(src, dst, s, r, device):
        return pltpu.make_async_remote_copy(
            src_ref=src, dst_ref=dst, send_sem=s, recv_sem=r, device_id={"state": device}, device_id_type=MESH
        )

    def shift(c, base):
        s = span(c)
        return pl.ds(base + s.start, s.size)

    def fwd_near(h):
        return remote(stn.at[h], tables[h].at[pl.ds(B, cap)], sn.at[h], rn.at[h], peer)

    def fwd_far(h, c, x):
        return remote(
            stx.at[h, span(c)], tables[h].at[shift(c, B + cap + x * FX)], sx.at[h, c], rx.at[h, x, c], gate_to
        )

    def fwd_pass(h, x, c):
        part = tables[h].at[shift(c, B + cap + x * FX)]
        return remote(part, part, sf.at[h, x, c], rx.at[h, x, c], peer)

    def bwd_near(h):
        return remote(bst.at[h, pl.ds(0, cap)], retn.at[:, :, cols(h)], bsn.at[h], brn.at[h], peer)

    def bwd_far(h, x, c):
        return remote(
            bst.at[h, shift(c, cap + x * FX)], retf.at[span(c), :, cols(h)], bsx.at[h, x, c], brx.at[h, c], far0 + x
        )

    def bwd_end(h, x, c):
        return remote(
            bst.at[h, shift(c, cap + x * FX)], rel.at[h, x, span(c)], bsx.at[h, x, c], brel.at[h, x, c], peer
        )

    def cols(h):
        return pl.ds(h * V, V)

    own_copy = pltpu.make_async_copy(val, own, lsem.at[0])
    own_copy.start()
    fills = [
        pltpu.make_async_copy(val.at[:, :, cols(h)], tables[h].at[pl.ds(0, B)], lsem.at[1 + h]) for h in range(H)
    ]
    fills[0].start()
    tile_copy = pltpu.make_async_copy(tiles_hbm, tiles, lsem.at[1 + H])
    cot_copy = pltpu.make_async_copy(cot_hbm, cot, lsem.at[2 + H])
    barrier = pltpu.get_barrier_semaphore()
    for k in range(1, D):
        pl.semaphore_signal(barrier, inc=1, device_id={"state": lax.rem(z + k, D)}, device_id_type=MESH)
    for k in range(1, T):
        pl.semaphore_signal(barrier, inc=1, device_id={"type": lax.rem(t + k, T)}, device_id_type=MESH)
    own_copy.wait()
    for h in range(H):
        for s in range(F):
            stx[h, s] = own[plan[3, 16 + s], :, h * V : (h + 1) * V]
        for s in range(cap):
            stn[h, s] = own[plan[3, s], :, h * V : (h + 1) * V]
        if h == 0:
            pl.semaphore_wait(barrier, D - 1 + T - 1)
        for c in list(range(C)) + tail:
            fwd_far(h, c, spot).start()
        fwd_near(h).start()
        if h == 0:
            tile_copy.start()
            cot_copy.start()
            for f in fills[1:]:
                f.start()
    P[0] = jnp.zeros((R, V), f32)
    gtac[...] = jnp.zeros(gtac.shape, f32)

    def pass_on(h, c):
        @pl.when(is_gate)
        def _():
            for x in range(2):
                fwd_far(h, c, x).wait_recv()
                fwd_pass(h, x, c).start()

    def arrived(h):
        fwd_near(h).wait_recv()

        @pl.when(is_gate)
        def _():
            for x in range(2):
                for c in tail:
                    fwd_far(h, c, x).wait_recv()

        @pl.when(is_end)
        def _():
            for x in range(2):
                for c in range(C):
                    fwd_far(h, c, x).wait_recv()

    def values(h, hook):
        t0, t1 = taste[0:1, h * V : (h + 1) * V], taste[1:2, h * V : (h + 1) * V]

        def step(k, carry):
            for g in range(G):
                i = k * G + g
                for a in range(A):
                    weights, blocks = [], []
                    for n in range(M):
                        e = (i * A + a) * M + n
                        row = plan[0, e]
                        keep = jnp.where(row > 0, 1.0, 0.0).astype(f32)
                        tile = tiles[e]
                        weights.append(tile * jnp.full(tile.shape, keep, f32).astype(bf16))
                        blocks.append(tables[h][jnp.maximum(row - 1, 0)])
                    acc[g, a] = jnp.dot(
                        jnp.concatenate(weights, axis=1), jnp.concatenate(blocks, axis=0),
                        preferred_element_type=f32,
                    )
            for g in range(G):
                i = k * G + g
                lanes = pl.ds(pl.multiple_of(i * R, R), R)
                base = [jnp.transpose(jnp.broadcast_to(util[a : a + 1, lanes], (R, R))) for a in range(A)]
                g0 = g1 = 0.0
                for c in range(0, R, rows):
                    at = slice(c, c + rows)
                    here = pl.ds(pl.multiple_of(i * R + c, rows), rows)
                    q0 = base[0][at, 0:1] + t0 + 0.95 * acc[g, 0, at, :]
                    q1 = base[1][at, 0:1] + t1 + 0.95 * acc[g, 1, at, :]
                    gap = q1 - q0
                    small = jnp.exp(-jnp.abs(gap))
                    total = 1.0 + small
                    value_ref[here, h * V : (h + 1) * V] = jnp.maximum(q0, q1) + jnp.log(total)
                    big = cot[here, h * V : (h + 1) * V].astype(f32) / total
                    little = big * small
                    first_wins = gap <= 0.0
                    h0 = jnp.where(first_wins, big, little)
                    h1 = jnp.where(first_wins, little, big)
                    scaled[i * A, at, :] = (0.95 * h0).astype(bf16)
                    scaled[i * A + 1, at, :] = (0.95 * h1).astype(bf16)
                    fold[0, at, :] = sum(h0[:, w : w + 128] for w in range(0, V, 128))
                    fold[1, at, :] = sum(h1[:, w : w + 128] for w in range(0, V, 128))
                    g0, g1 = g0 + h0, g1 + h1
                for a in range(A):
                    line = jnp.sum(jnp.transpose(fold[a]), axis=0, keepdims=True)
                    gacc[a : a + 1, lanes] = line if h == 0 else gacc[a : a + 1, lanes] + line
                gtac[0:1, h * V : (h + 1) * V] += jnp.sum(g0, axis=0, keepdims=True)
                gtac[1:2, h * V : (h + 1) * V] += jnp.sum(g1, axis=0, keepdims=True)
            hook(k)
            return carry

        lax.fori_loop(0, B // G, step, 0)

    def back(lo, hi):
        def step(k, carry):
            for u in range(B):
                e = plan[1, k * B + u]
                P[k * B + u + 1] = P[plan[2, k * B + u]] + transposed_dot(tiles[e], scaled[lax.div(e, M)])
            return carry

        lax.fori_loop(lo, hi, step, 0)

    def stage(h, s):
        bst[h, s] = P[plan[3, 64 + B + s]].astype(bf16)

    def give(h):
        @pl.when(is_end)
        def _():
            for c in range(C):
                for x in range(2):
                    for s in range(c * CH, (c + 1) * CH):
                        stage(h, cap + x * FX + s)
                if c > 0:
                    for x in range(2):
                        bwd_end(h, x, c - 1).start()

        @pl.when(is_gate)
        def _():
            for x in range(2):
                for s in range(cap, F):
                    stage(h, cap + x * FX + s)

        for s in range(cap):
            stage(h, s)

        @pl.when(is_end)
        def _():
            for x in range(2):
                bwd_end(h, x, C - 1).start()

        @pl.when(is_gate)
        def _():
            for x in range(2):
                for c in tail:
                    bwd_far(h, x, c).start()

        bwd_near(h).start()

    def add_on(h, c):
        @pl.when(is_gate)
        def _():
            for x in range(2):
                bwd_end(h, x, c).wait_recv()
                for s in range(CH):
                    u = c * CH + s
                    term = P[plan[3, 64 + B + cap + x * FX + u]] + rel[h, x, u].astype(f32)
                    bst[h, cap + x * FX + u] = term.astype(bf16)
            for x in range(2):
                bwd_far(h, x, c).start()

    def keep(h):
        def step(k, carry):
            for g in range(G):
                adj_ref[k * G + g, :, h * V : (h + 1) * V] = P[plan[3, 64 + k * G + g]]
            return carry

        lax.fori_loop(0, B // G, step, 0)

    def sums():
        out = []
        for k in range(1, T):
            out.append(
                pltpu.make_async_remote_copy(
                    src_ref=gacc, dst_ref=lu.at[k], send_sem=usem.at[k], recv_sem=ursem.at[k],
                    device_id={"type": lax.rem(t + k, T)}, device_id_type=MESH,
                )
            )
        for k in range(1, D):
            out.append(remote(gtac, lt.at[k], tsem.at[k], trsem.at[k], lax.rem(z + k, D)))
        return out

    for c in range(C):
        pass_on(0, c)
    fills[0].wait()
    arrived(0)
    tile_copy.wait()
    cot_copy.wait()
    for h in range(H):
        steps = B // G

        def hook(k, h=h):
            @pl.when(k < C)
            def _():
                if h + 1 < H:
                    pass_on(h + 1, k)
                if h > 0:
                    add_on(h - 1, k)

        if h > 0:
            fills[h].wait()
            arrived(h)
        values(h, hook)
        back(0, 1)
        give(h)
        if h == H - 1:
            for c in sums():
                c.start()
        back(1, E // B)
        keep(h)
    for c in range(C):
        add_on(H - 1, c)
    for c in sums():
        c.wait()
    lu[0] = gacc[...]
    lt[0] = gtac[...]
    u = lu[lax.rem(t, T)]
    for j in range(1, T):
        u = u + lu[lax.rem(t - j + T, T)]
    w = lt[lax.rem(z, D)]
    for j in range(1, D):
        w = w + lt[lax.rem(z - j + D, D)]
    gu_ref[...] = u / (H * V * T)
    gt_ref[...] = w / (B * R * D)
    for h in range(H):
        fwd_near(h).wait_send()
        bwd_near(h).wait()
        for c in list(range(C)) + tail:
            fwd_far(h, c, spot).wait_send()
            bwd_far(h, 0, c).wait_recv()

        @pl.when(is_gate)
        def _(h=h):
            for x in range(2):
                for c in range(C):
                    fwd_pass(h, x, c).wait_send()
                for c in list(range(C)) + tail:
                    bwd_far(h, x, c).wait_send()

        @pl.when(is_end)
        def _(h=h):
            for x in range(2):
                for c in range(C):
                    bwd_end(h, x, c).wait_send()


def folded(value_in, cotangent, state_util, taste, tiles, dest_block, counts):
    B, A, M, R, _ = tiles.shape
    W = value_in.shape[1]
    D, T = lax.axis_size("state"), lax.axis_size("type")
    Q = lax.axis_size("groups") * D
    cap = (B + D - 2) // (D - 1)
    E, FX, H, G = B * A * M, 2 * cap, 2, 4
    V = W // H
    f32, bf16, i32 = jnp.float32, jnp.bfloat16, jnp.int32
    shape, DMA = jax.ShapeDtypeStruct, pltpu.SemaphoreType.DMA
    vmem = pl.BlockSpec(memory_space=VMEM)
    hbm = pl.BlockSpec(memory_space=pl.ANY)

    sizes = sorted({cap + (cap + 1) // 2, cap + (2 * cap + 2) // 3, FX})
    plan, pick = pl.pallas_call(
        functools.partial(meet_kernel, (B, A, M, D, cap, Q), sizes),
        out_shape=(shape((8, 256), i32), shape((1,), i32)),
        in_specs=[vmem] * 2,
        out_specs=[vmem, smem()],
        scratch_shapes=[VMEM((128, 128), f32), VMEM((Q, 8, 128), f32), VMEM((256, 128), f32), DMA((Q,)), DMA((Q,))],
        compiler_params=pltpu.CompilerParams(collective_id=0, has_side_effects=True),
        name="meet",
    )(dest_block.transpose(2, 1, 0), counts.T)

    def sweep(F, ident):
        dims = (B, A, M, R, V, H, D, T, cap, FX, F, G, 32)
        C = cap // 2
        return pl.pallas_call(
            functools.partial(sweep_kernel, dims),
            out_shape=(
                VMEM((B * R, W), f32), VMEM((B, R, W), f32), VMEM((cap, R, W), bf16), VMEM((FX, R, W), bf16),
                VMEM((A, B * R), f32), VMEM((A, W), f32),
            ),
            in_specs=[smem(), hbm, hbm, hbm, vmem, vmem],
            out_specs=[vmem] * 6,
            scratch_shapes=[VMEM((B + cap + 2 * FX, R, V), bf16)] * H
            + [
                VMEM((B, R, W), bf16), VMEM((H, cap, R, V), bf16), VMEM((H, FX, R, V), bf16),
                VMEM((E, R, R), bf16), VMEM((B * R, W), bf16),
                VMEM((B * A, R, V), bf16), VMEM((E + 1, R, V), f32), VMEM((H, cap + 2 * FX, R, V), bf16),
                VMEM((H, 2, cap, R, V), bf16), VMEM((G, A, R, V), f32),
                VMEM((A, R, 128), f32), VMEM((A, B * R), f32), VMEM((A, W), f32),
                VMEM((T, A, B * R), f32), VMEM((D, A, W), f32),
                DMA((3 + H,)), DMA((H,)), DMA((H,)),
                DMA((H, C + 1)), DMA((H, 2, C + 1)), DMA((H, 2, C)), DMA((H,)), DMA((H,)),
                DMA((H, 2, C + 1)), DMA((H, 2, C)), DMA((H, C + 1)),
                DMA((T,)), DMA((T,)), DMA((D,)), DMA((D,)),
            ],
            compiler_params=pltpu.CompilerParams(
                collective_id=ident, has_side_effects=True, vmem_limit_bytes=55_000_000
            ),
            cost_estimate=pl.CostEstimate(flops=4 * E * R * R * W, bytes_accessed=20 << 20, transcendentals=3 * B * R * W),
            name="sweep%d" % F,
        )

    def branch(F, ident):
        def run(plan, *args):
            held = sweep(F, ident)(plan, *args)
            held = [pltpu.with_memory_space_constraint(v, VMEM) for v in held]
            return pl.pallas_call(
                functools.partial(finish_kernel, G),
                in_specs=[smem()] + [vmem] * 6,
                out_specs=[hbm, hbm, vmem, vmem],
                out_shape=[shape(held[k].shape, f32) for k in (0, 1, 4, 5)],
                scratch_shapes=[VMEM((B, R, W), f32), DMA((B // G,)), DMA((B // G,))],
                compiler_params=pltpu.CompilerParams(vmem_limit_bytes=5 << 20),
                name="finish",
            )(plan, *held)

        return run

    value, adjoint, grad_util, grad_taste = lax.switch(
        pick.reshape(()), [branch(f, 1 + k) for k, f in enumerate(sizes)],
        plan, value_in.reshape(B, R, W), cotangent, tiles.reshape(E, R, R), state_util, taste,
    )
    return value, adjoint.reshape(B * R, W), grad_util, grad_taste


def finish_kernel(G, plan, held, part, near_ref, far_ref, gu_ref, gt_ref, value, adjoint, gu, gt, total, vsem, asem):
    f32 = jnp.float32
    B, R, _ = part.shape
    steps = range(B // G)
    outs = []
    for k in steps:
        rows = pl.ds(k * G * R, G * R)
        outs.append(pltpu.make_async_copy(held.at[rows], value.at[rows], vsem.at[k]))
        outs[-1].start()
    gu[...] = gu_ref[...]
    gt[...] = gt_ref[...]
    for k in steps:
        for j in range(k * G, (k + 1) * G):
            near, far = plan[3, 32 + j], plan[3, 48 + j]
            add = jnp.where(near > 0, near_ref[jnp.maximum(near - 1, 0)].astype(f32), 0.0)
            total[j] = part[j] + add + jnp.where(far > 0, far_ref[jnp.maximum(far - 1, 0)].astype(f32), 0.0)
        blocks = pl.ds(k * G, G)
        outs.append(pltpu.make_async_copy(total.at[blocks], adjoint.at[blocks], asem.at[k]))
        outs[-1].start()
    for c in outs:
        c.wait()


def choose(*args):
    B, A, M, R, _ = args[4].shape
    D = lax.axis_size("state")
    cap = (B + D - 2) // (D - 1)
    fits = D * B <= 128 and 128 < B * A * M <= 256 and cap % 2 == 0 and B % 4 == 0 and R == 128
    if D == 4 and fits and args[0].shape[1] % 256 == 0:
        return folded(*args)
    return local(*args)


def solution(mesh):
    rows = ("groups", "state")
    return jax.shard_map(
        choose,
        mesh=mesh,
        in_specs=(
            P(rows, "type"),
            P(rows, "type"),
            P(None, rows),
            P(None, ("groups", "type")),
            P(rows, None, None, None, None),
            P(rows, None, None),
            P(rows, None),
        ),
        out_specs=(P(rows, "type"), P(rows, "type"), P(None, rows), P(None, ("groups", "type"))),
        check_vma=False,
    )
```

```python
import functools

import jax
import jax.numpy as jnp
from jax import lax
from jax.experimental import pallas as pl
from jax.experimental.pallas import tpu as pltpu
from jax.sharding import PartitionSpec as P

VMEM = pltpu.VMEM
SMEM = pltpu.SMEM
MESH = pl.DeviceIdType.MESH


def smem():
    return pl.BlockSpec(memory_space=SMEM)


def whole(shape):
    return pl.BlockSpec(shape, lambda *g: (0,) * len(shape))


def plan_kernel(dims, me_ref, dest_ref, count_ref, req_ref, look_ref, from_ref, fill):
    B, A, M, D, cap = dims
    me = me_ref[0]

    def clear(p, carry):
        fill[p] = 0
        for s in range(cap):
            req_ref[p, 0, s] = -1
            from_ref[p * cap + s] = 0
        return carry

    lax.fori_loop(0, D, clear, 0)

    def lists(i, carry):
        for a in range(A):
            count = count_ref[a, i]
            for n in range(M):
                e = (i * A + a) * M + n
                dest = dest_ref[n, a, i]
                owner = lax.div(dest, B)
                block = dest - owner * B
                used = n < count
                look_ref[e] = jnp.where(used & (owner == me), block, -1)

                @pl.when(used & (owner != me))
                def _():
                    s = fill[owner]
                    fill[owner] = s + 1
                    req_ref[owner, 0, s] = block
                    from_ref[owner * cap + s] = e
                    look_ref[e] = B + owner * cap + s

        return carry

    lax.fori_loop(0, B, lists, 0)


def greet(axis, others):
    barrier = pltpu.get_barrier_semaphore()
    for ids in others:
        pl.semaphore_signal(barrier, inc=1, device_id=ids, device_id_type=MESH)
    pl.semaphore_wait(barrier, len(others))


def request_kernel(D, req_ref, out_ref, land, send, recv):
    me = lax.axis_index("state")
    peers = [{"state": lax.rem(me + k, D)} for k in range(1, D)]
    greet("state", peers)
    copies = []
    for k in range(1, D):
        c = pltpu.make_async_remote_copy(
            src_ref=req_ref.at[lax.rem(me + k, D)],
            dst_ref=land.at[k],
            send_sem=send.at[k],
            recv_sem=recv.at[k],
            device_id={"state": lax.rem(me + k, D)},
            device_id_type=MESH,
        )
        c.start()
        copies.append(c)
    for c in copies:
        c.wait()
    out_ref[me] = req_ref[me]
    for k in range(1, D):
        out_ref[lax.rem(me - k + D, D)] = land[k]


def gather_kernel(D, cap, half, want_ref, val_ref, *rest):
    outs, sem = rest[:-1], rest[-1]

    def run(h, act):
        def peer(p, carry):
            for s in range(cap):
                w = jnp.maximum(want_ref[p, 0, s], 0)
                act(
                    pltpu.make_async_copy(
                        val_ref.at[w, :, pl.ds(h * half, half)],
                        outs[h].at[p * cap + s],
                        sem.at[h, p * cap + s],
                    )
                )
            return carry

        lax.fori_loop(0, D, peer, 0)

    for h in range(len(outs)):
        run(h, lambda c: c.start())
    for h in range(len(outs)):
        run(h, lambda c: c.wait())


def transposed_dot(tile, right):
    return lax.dot_general(tile, right, (((0,), (0,)), ((), ())), preferred_element_type=jnp.float32)


def continuation(M, first, look_ref, table, tiles):
    weights, values = [], []
    for n in range(M):
        row = look_ref[first + n]
        keep = jnp.where(row >= 0, 1.0, 0.0).astype(jnp.float32)
        tile = tiles(n)
        weights.append(tile * jnp.full(tile.shape, keep, jnp.float32).astype(jnp.bfloat16))
        values.append(table[jnp.maximum(row, 0)])
    return jnp.dot(
        jnp.concatenate(weights, axis=1), jnp.concatenate(values, axis=0), preferred_element_type=jnp.float32
    )


def fetch_value_kernel(G, rows, D, look_ref, from_ref, val_ref, *rest):
    H = (len(rest) - 14) // 2
    outs, rest = rest[:H], rest[H:]
    body, lands = rest[:9], rest[9 : 9 + H - 1]
    acc, table, kept, sem, send, recv = rest[9 + H - 1 :]
    step = pl.program_id(0)
    B, C, V = val_ref.shape[0], outs[0].shape[0], outs[0].shape[2]
    cap = C // D
    me = lax.axis_index("state")

    def copy(h, k):
        to = lax.rem(me + k, D)
        land = table.at[pl.ds(B + me * cap, cap)] if h == 0 else lands[h - 1].at[pl.ds(me * cap, cap)]
        return pltpu.make_async_remote_copy(
            src_ref=outs[h].at[pl.ds(to * cap, cap)],
            dst_ref=land,
            send_sem=send.at[h, k],
            recv_sem=recv.at[h, k],
            device_id={"state": to},
            device_id_type=MESH,
        )

    @pl.when(step == 0)
    def _():
        greet("state", [{"state": lax.rem(me + k, D)} for k in range(1, D)])
        for h in range(H):
            for k in range(1, D):
                copy(h, k).start()
        own = pltpu.make_async_copy(val_ref.at[:, :, pl.ds(0, V)], table.at[pl.ds(0, B)], sem.at[0])
        mine = pltpu.make_async_copy(
            outs[0].at[pl.ds(me * cap, cap)], table.at[pl.ds(B + me * cap, cap)], sem.at[1]
        )
        own.start()
        mine.start()
        own.wait()
        mine.wait()
        for k in range(1, D):
            copy(0, k).wait()

    work(G, rows, look_ref, from_ref, *body, acc, table, kept)

    @pl.when(step == pl.num_programs(0) - 1)
    def _():
        for h in range(1, H):
            for k in range(1, D):
                copy(h, k).wait()


def value_kernel(
    G, rows, col, look_ref, from_ref, val_ref, inc_ref, tiles_ref, cot_ref, util_ref, taste_ref, *rest
):
    before_ref = rest[0]
    value_ref, scaled_ref, out_ref, gu_ref, gt_ref, acc, table, kept, sem = rest[-9:]
    step = pl.program_id(0)
    B, C, V = val_ref.shape[0], inc_ref.shape[0], inc_ref.shape[2]

    @pl.when(step == 0)
    def _():
        own = pltpu.make_async_copy(val_ref.at[:, :, pl.ds(col, V)], table.at[pl.ds(0, B)], sem.at[0])
        far = pltpu.make_async_copy(inc_ref, table.at[pl.ds(B, C)], sem.at[1])
        own.start()
        far.start()
        own.wait()
        far.wait()

    value_ref[:, :col] = before_ref[...]
    work(
        G, rows, look_ref, from_ref, tiles_ref, cot_ref, util_ref, taste_ref,
        value_ref.at[:, col:], scaled_ref, out_ref, gu_ref, gt_ref, acc, table, kept,
    )


def work(
    G, rows, look_ref, from_ref, tiles_ref, cot_ref, util_ref, taste_ref,
    value_ref, scaled_ref, out_ref, gu_ref, gt_ref, acc, table, kept,
):
    step = pl.program_id(0)
    _, A, M, R, _ = tiles_ref.shape
    C = out_ref.shape[0]

    @pl.when(step == 0)
    def _():
        gt_ref[...] = jnp.zeros_like(gt_ref)

    t0, t1 = taste_ref[0:1, :], taste_ref[1:2, :]
    for g in range(G):
        i = step * G + g
        for a in range(A):
            acc[g, a] = continuation(M, (i * A + a) * M, look_ref, table, lambda n: tiles_ref[i, a, n])
    for g in range(G):
        g0 = g1 = 0.0
        cols = [
            jnp.transpose(jnp.broadcast_to(util_ref[a : a + 1, g * R : (g + 1) * R], (R, R))) for a in range(A)
        ]
        for c in range(0, R, rows):
            at = slice(c, c + rows)
            here = slice(g * R + c, g * R + c + rows)
            q0 = cols[0][at, 0:1] + t0 + 0.95 * acc[g, 0, at, :]
            q1 = cols[1][at, 0:1] + t1 + 0.95 * acc[g, 1, at, :]
            gap = q1 - q0
            small = jnp.exp(-jnp.abs(gap))
            total = 1.0 + small
            value_ref[here, :] = jnp.maximum(q0, q1) + jnp.log(total)
            big = cot_ref[here, :].astype(jnp.float32) / total
            little = big * small
            first_wins = gap <= 0.0
            h0 = jnp.where(first_wins, big, little)
            h1 = jnp.where(first_wins, little, big)
            scaled_ref[g, 0, at, :] = (0.95 * h0).astype(jnp.bfloat16)
            scaled_ref[g, 1, at, :] = (0.95 * h1).astype(jnp.bfloat16)
            gu_ref[g, at, 0:1] = jnp.sum(h0, axis=1, keepdims=True)
            gu_ref[g, at, 1:2] = jnp.sum(h1, axis=1, keepdims=True)
            g0, g1 = g0 + h0, g1 + h1
        gt_ref[0:1, :] += jnp.sum(g0, axis=0, keepdims=True)
        gt_ref[1:2, :] += jnp.sum(g1, axis=0, keepdims=True)
    kept[pl.ds(step * G, G)] = scaled_ref[...]

    @pl.when(step == pl.num_programs(0) - 1)
    def _():
        def back(q, carry):
            for u in range(2):
                slot = q * 2 + u
                e = from_ref[slot]
                pair = lax.div(e, M)
                i = lax.div(pair, A)
                a = pair - i * A
                out_ref[slot] = transposed_dot(tiles_ref[i, a, e - pair * M], kept[i, a]).astype(jnp.bfloat16)
            return carry

        lax.fori_loop(0, C // 2, back, 0)


def back_kernel(G, A, M, look_ref, tiles_ref, scaled_ref, adj_ref):
    spare = adj_ref.shape[0] - 1
    step = pl.program_id(0)

    @pl.when(step == 0)
    def _():
        adj_ref[...] = jnp.zeros_like(adj_ref)

    for g in range(G):
        i = step * G + g
        for a in range(A):
            for n in range(M):
                block = look_ref[(i * A + a) * M + n]
                here = jnp.where((block >= 0) & (block < spare), block, spare)
                adj_ref[here] += transposed_dot(tiles_ref[g, a, n], scaled_ref[g, a])


def sums_kernel(D, T, gu_ref, gt_ref, token_ref, after_ref, ou_ref, ot_ref, lu, lt, us, ur, ts, tr):
    ms, mt = lax.axis_index("state"), lax.axis_index("type")
    peers = [{"state": lax.rem(ms + k, D)} for k in range(1, D)]
    peers += [{"type": lax.rem(mt + k, T)} for k in range(1, T)]
    greet("state", peers)
    copies = []
    for k in range(1, T):
        copies.append(
            pltpu.make_async_remote_copy(
                src_ref=gu_ref, dst_ref=lu.at[k], send_sem=us.at[k], recv_sem=ur.at[k],
                device_id={"type": lax.rem(mt + k, T)}, device_id_type=MESH,
            )
        )
    for k in range(1, D):
        copies.append(
            pltpu.make_async_remote_copy(
                src_ref=gt_ref, dst_ref=lt.at[k], send_sem=ts.at[k], recv_sem=tr.at[k],
                device_id={"state": lax.rem(ms + k, D)}, device_id_type=MESH,
            )
        )
    for c in copies:
        c.start()
    for c in copies:
        c.wait()
    lu[0] = gu_ref[...]
    lt[0] = gt_ref[...]
    u = lu[lax.rem(mt, T)]
    for j in range(1, T):
        u = u + lu[lax.rem(mt - j + T, T)]
    t = lt[lax.rem(ms, D)]
    for j in range(1, D):
        t = t + lt[lax.rem(ms - j + D, D)]
    ou_ref[...] = u
    ot_ref[...] = t


def land_kernel(D, cap, want_ref, adj_ref, ret_ref, *rest):
    out_ref, done_ref = rest[-2:]
    done_ref[0] = 0
    out_ref[...] = adj_ref[...]

    def peer(p, carry):
        for s in range(cap):
            w = want_ref[p, 0, s]

            @pl.when(w >= 0)
            def _():
                out_ref[w] += ret_ref[p * cap + s].astype(jnp.float32)

        return carry

    lax.fori_loop(0, D, peer, 0)


def local(value_in, cotangent, state_util, taste, tiles, dest_block, counts):
    B, A, M, R, _ = tiles.shape
    W = value_in.shape[1]
    D = lax.axis_size("state")
    T = lax.axis_size("type")
    cap = max(2, (B + D - 2) // (D - 1))
    E, C = B * A * M, D * cap
    f32, bf16, i32 = jnp.float32, jnp.bfloat16, jnp.int32
    shape = jax.ShapeDtypeStruct
    values = value_in.reshape(B, R, W)

    req, look, origin = pl.pallas_call(
        functools.partial(plan_kernel, (B, A, M, D, cap)),
        out_shape=(shape((D, 1, 128), i32), shape((E,), i32), shape((C,), i32)),
        in_specs=[smem()] * 3,
        out_specs=[smem()] * 3,
        scratch_shapes=[SMEM((D,), i32)],
        name="plan",
    )(lax.axis_index("state").reshape(1).astype(i32), dest_block.transpose(2, 1, 0), counts.T)

    wanted = pl.pallas_call(
        functools.partial(request_kernel, D),
        out_shape=shape((D, 1, 128), i32),
        in_specs=[pl.BlockSpec(memory_space=VMEM)],
        out_specs=pl.BlockSpec(memory_space=VMEM),
        scratch_shapes=[VMEM((D, 1, 128), i32), pltpu.SemaphoreType.DMA((D,)), pltpu.SemaphoreType.DMA((D,))],
        compiler_params=pltpu.CompilerParams(collective_id=0, has_side_effects=True),
        name="request",
    )(req)

    H = 2 if W % 256 == 0 else 1
    V = W // H
    G = 4 if B % 4 == 0 else 1
    outgoing = pl.pallas_call(
        functools.partial(gather_kernel, D, cap, V),
        out_shape=tuple(shape((C, R, V), bf16) for h in range(H)),
        in_specs=[smem(), pl.BlockSpec(memory_space=VMEM)],
        out_specs=[pl.BlockSpec(memory_space=pl.ANY)] * H,
        scratch_shapes=[pltpu.SemaphoreType.DMA((H, C))],
        name="gather",
    )(wanted, values)

    def exchange(x):
        return lax.all_to_all(
            x.reshape(D, cap, R, V), "state", split_axis=0, concat_axis=0, tiled=True
        ).reshape(C, R, V)

    incoming = []

    flops = 2 * E * R * R * W
    value = None
    gus, gts, outbound, scaleds = [], [], [], []
    any_spec = pl.BlockSpec(memory_space=pl.ANY)
    for h in range(H):
        wide = V * (h + 1)
        ins = [
            whole((B, A, M, R, R)),
            pl.BlockSpec((G * R, V), lambda i, h=h: (i, h)),
            pl.BlockSpec((A, G * R), lambda i: (0, i)),
            pl.BlockSpec((A, V), lambda i, h=h: (0, h)),
        ]
        out_shape = [
            shape((B * R, wide), f32), shape((B, A, R, V), bf16), shape((C, R, V), bf16),
            shape((B, R, A), f32), shape((A, V), f32),
        ]
        out_specs = [
            pl.BlockSpec((G * R, wide), lambda i: (i, 0)),
            pl.BlockSpec((G, A, R, V), lambda i: (i, 0, 0, 0)),
            whole((C, R, V)),
            pl.BlockSpec((G, R, A), lambda i: (i, 0, 0)),
            whole((A, V)),
        ]
        scratch = [
            VMEM((G, A, R, V), f32), VMEM((B + C, R, V), bf16), VMEM((B, A, R, V), bf16),
            pltpu.SemaphoreType.DMA((2,)),
        ]
        cost = pl.CostEstimate(flops=flops // H, bytes_accessed=(24 << 20) // H, transcendentals=3 * B * R * V)
        if h == 0:
            value, scaled, out, gu, gt, *incoming = pl.pallas_call(
                functools.partial(fetch_value_kernel, G, 32, D),
                grid=(B // G,),
                out_shape=out_shape + [shape((C, R, V), bf16)] * (H - 1),
                in_specs=[smem(), smem(), any_spec] + [any_spec] * H + ins,
                out_specs=out_specs + [any_spec] * (H - 1),
                scratch_shapes=scratch + [pltpu.SemaphoreType.DMA((H, D)), pltpu.SemaphoreType.DMA((H, D))],
                compiler_params=pltpu.CompilerParams(collective_id=2, has_side_effects=True),
                cost_estimate=cost,
                name="fetch",
            )(look, origin, values, *outgoing, tiles, cotangent, state_util, taste)
        else:
            value, scaled, out, gu, gt = pl.pallas_call(
                functools.partial(value_kernel, G, 32, h * V),
                grid=(B // G,),
                out_shape=out_shape,
                in_specs=[smem(), smem(), any_spec, any_spec] + ins
                + [pl.BlockSpec((G * R, h * V), lambda i: (i, 0))],
                out_specs=out_specs,
                scratch_shapes=scratch,
                cost_estimate=cost,
                name="value",
            )(look, origin, values, incoming[h - 1], tiles, cotangent, state_util, taste, value)
        outbound.append(out)
        scaleds.append(scaled)
        gus.append(gu)
        gts.append(gt)

    adjs = [
        pl.pallas_call(
            functools.partial(back_kernel, G, A, M),
            grid=(B // G,),
            out_shape=shape((B + 1, R, V), f32),
            in_specs=[
                smem(),
                pl.BlockSpec((G, A, M, R, R), lambda i: (i, 0, 0, 0, 0)),
                pl.BlockSpec((G, A, R, V), lambda i: (i, 0, 0, 0)),
            ],
            out_specs=whole((B + 1, R, V)),
            cost_estimate=pl.CostEstimate(flops=flops // H, bytes_accessed=(14 << 20) // H, transcendentals=0),
            name="back",
        )(look, tiles, x)
        for x in scaleds
    ]

    returned = []
    for h in range(H):
        if h > 0:
            outbound[h], adjs[h - 1] = lax.optimization_barrier((outbound[h], adjs[h - 1]))
        returned.append(exchange(outbound[h]))

    adjoint, tokens = None, []
    gu_rows = sum(gus).transpose(2, 0, 1).reshape(A, B * R) / (W * T)
    for h in range(H):
        held = [] if h == 0 else [adjoint]
        adjoint, token = pl.pallas_call(
            functools.partial(land_kernel, D, cap),
            grid=(1,),
            out_shape=(shape((B, R, W), f32), shape((1,), i32)),
            in_specs=[smem(), whole((B, R, V)), whole((C, R, V))]
            + [pl.BlockSpec(memory_space=pl.ANY)] * len(held),
            out_specs=[pl.BlockSpec((B, R, V), lambda j, h=h: (0, 0, h)), smem()],
            input_output_aliases={3 + k: k for k in range(len(held))},
            name="land",
        )(wanted, adjs[h], returned[h], *held)
        tokens.append(token)
    grad_util, grad_taste = pl.pallas_call(
        functools.partial(sums_kernel, D, T),
        out_shape=(shape((A, B * R), f32), shape((A, W), f32)),
        in_specs=[pl.BlockSpec(memory_space=VMEM)] * 2 + [smem(), pl.BlockSpec(memory_space=pl.ANY)],
        out_specs=[pl.BlockSpec(memory_space=VMEM)] * 2,
        scratch_shapes=[
            VMEM((T, A, B * R), f32), VMEM((D, A, W), f32),
            pltpu.SemaphoreType.DMA((T,)), pltpu.SemaphoreType.DMA((T,)),
            pltpu.SemaphoreType.DMA((D,)), pltpu.SemaphoreType.DMA((D,)),
        ],
        compiler_params=pltpu.CompilerParams(collective_id=1, has_side_effects=True),
        cost_estimate=pl.CostEstimate(flops=0, bytes_accessed=8 << 20, transcendentals=0),
        name="sums",
    )(gu_rows, jnp.concatenate(gts, axis=1) / (B * R * D), tokens[0], adjs[-1])

    return value, adjoint.reshape(B * R, W), grad_util, grad_taste


def meet_kernel(dims, sizes, dest_ref, count_ref, plan_ref, pick_ref, mine, land, oh, ssem, rsem):
    B, A, M, D, cap, Q = dims
    f32 = jnp.float32
    y, z = lax.axis_index("groups"), lax.axis_index("state")
    q = y * D + z
    E2 = oh.shape[0]
    mine[...] = jnp.full(mine.shape, -1.0, f32)
    for n in range(M):
        mine[n * A : (n + 1) * A, 0:B] = jnp.where(n < count_ref[...], dest_ref[n], -1).astype(f32)
    own = jnp.transpose(mine[...])[0:B, :]
    lane = lax.broadcasted_iota(jnp.int32, (B, 128), 1).astype(f32)
    oh[A * M * B :, :] = jnp.zeros((E2 - A * M * B, 128), f32)
    total = jnp.zeros((B, 128), f32)
    for c in range(A * M):
        hot = jnp.where(own[:, c : c + 1] == lane, 1.0, 0.0)
        oh[c * B : (c + 1) * B, :] = hot
        total = jnp.maximum(total, hot)
    land[0] = jnp.broadcast_to(jnp.max(total, axis=0, keepdims=True), (8, 128))

    def member(k):
        p = lax.rem(q + k, Q)
        return {"groups": lax.div(p, D), "state": lax.rem(p, D)}

    greet("state", [member(k) for k in range(1, Q)])
    copies = [
        pltpu.make_async_remote_copy(
            src_ref=land.at[0], dst_ref=land.at[k], send_sem=ssem.at[k], recv_sem=rsem.at[k],
            device_id=member(k), device_id_type=MESH,
        )
        for k in range(1, Q)
    ]
    for c in copies:
        c.start()

    seg = lax.div(lax.broadcasted_iota(jnp.int32, (1, 128), 1), B)
    b = lax.broadcasted_iota(jnp.int32, (1, 128), 1).astype(f32)

    def as_row(col):
        full = jnp.broadcast_to(col, (E2, 128))
        return jnp.concatenate(
            [jnp.transpose(full[k : k + 128, :])[0:1, :] for k in range(0, E2, 128)], axis=1
        )

    key_of = b + jnp.where(seg == z, 129.0, 1.0)
    key = jnp.sum(oh[...] * key_of, axis=1, keepdims=True)
    key = jnp.where(key == 0, 300.0, key)
    iq = lax.broadcasted_iota(jnp.int32, (E2, 1), 0)
    order = key * E2 + iq.astype(f32)
    order_row, key_row = as_row(order), as_row(key)
    pos = jnp.sum(jnp.where(order_row < order, 1.0, 0.0), axis=1, keepdims=True)
    less = jnp.sum(jnp.where(key_row < key, 1.0, 0.0), axis=1, keepdims=True)
    wide = lax.broadcasted_iota(jnp.int32, (E2, E2), 1).astype(f32)
    c = lax.div(iq, B)
    entry = ((lax.rem(iq, B) * A + lax.rem(c, A)) * M + lax.div(c, A)).astype(f32)
    move = jnp.where(pos == wide, 1.0, 0.0)
    put = lambda k, v: plan_ref.__setitem__((slice(k, k + 1), slice(0, v.shape[1])), v.astype(jnp.int32))
    plan_ref[...] = jnp.zeros(plan_ref.shape, jnp.int32)
    put(1, jnp.sum(move * entry, axis=0, keepdims=True))
    put(2, jnp.sum(move * jnp.where(pos == less, 0.0, pos), axis=0, keepdims=True))
    last = jnp.sum(jnp.where(key <= key_of, 1.0, 0.0), axis=0, keepdims=True)
    last = last * jnp.max(jnp.where(key == key_of, 1.0, 0.0), axis=0, keepdims=True)
    for k in copies:
        k.wait()

    half = D // 2
    rows, needs = [], []
    for u in range(Q // D):
        g = lax.rem(y + u, Q // D)
        need = [land[lax.rem(q - (g * D + r) + Q, Q)][0:1, :] for r in range(D)]
        end = jnp.where(seg < half, need[D - 1], need[0])
        gate = jnp.where(seg < half, need[half], need[half - 1]) * (1.0 - end)
        rows += [end, gate]
        if u == 0:
            needs = need
    peer = 2 * lax.div(z, 2) + 1 - lax.rem(z, 2)
    mine_need = sum(jnp.where(z == r, needs[r], 0.0) for r in range(D))
    peer_need = sum(jnp.where(peer == r, needs[r], 0.0) for r in range(D))
    at = len(rows)
    rows += [mine_need, peer_need]
    stack = jnp.concatenate(rows + [jnp.zeros((8 - len(rows), 128), f32)], axis=0)
    one = lax.broadcasted_iota(jnp.int32, (128, 128), 0)
    two = lax.broadcasted_iota(jnp.int32, (128, 128), 1)
    same = jnp.where(lax.div(one, B) == lax.div(two, B), 1.0, 0.0)
    below = jnp.where(one < two, same, 0.0)
    rank = jnp.dot(stack, below, preferred_element_type=f32)
    size = jnp.dot(stack, same, preferred_element_type=f32)
    far_any = rows[0] + rows[1]
    far_rank = jnp.where(rows[0] > 0, rank[0:1], size[0:1] + rank[1:2])
    most = size[0:1] + size[1:2]
    for u in range(1, Q // D):
        most = jnp.maximum(most, size[2 * u : 2 * u + 1] + size[2 * u + 1 : 2 * u + 2])
    near_rank, give_rank = rank[at : at + 1], rank[at + 1 : at + 2]
    first = (z * B).astype(f32)
    FX = 2 * cap
    row_of = 1.0 + jnp.where(
        seg == z,
        b - first,
        jnp.where(
            lax.div(seg, 2) == lax.div(z, 2), B + near_rank, B + cap + lax.rem(seg, 2).astype(f32) * FX + far_rank
        ),
    )

    row = jnp.sum(oh[...] * row_of, axis=1, keepdims=True)
    put(0, jnp.sum(jnp.where(entry == wide, row, 0.0), axis=0, keepdims=True))
    slot = lax.broadcasted_iota(jnp.int32, (16, 128), 0).astype(f32)
    here = jnp.where(seg == z, b - first, 0.0)
    mine_here = (seg == z) & (b - first == slot)
    goal = lax.broadcasted_iota(jnp.int32, (64, 128), 0).astype(f32)
    known = (mine_need > 0) | (seg == z)
    lists = [
        jnp.where((give_rank == slot) & (peer_need > 0), here, 0.0),
        jnp.where((far_rank == slot) & (far_any > 0), here, 0.0),
        jnp.where(mine_here & (peer_need > 0), give_rank + 1.0, 0.0),
        jnp.where(mine_here & (far_any > 0), far_rank + 1.0, 0.0),
        jnp.where((row_of - 1.0 == goal) & known, last, 0.0),
    ]
    column = jnp.concatenate([jnp.sum(v, axis=1, keepdims=True) for v in lists], axis=0)
    put(3, jnp.transpose(jnp.broadcast_to(column, (128, 128)))[0:1, :])
    widest = jnp.max(most)
    pick_ref[0] = sum(jnp.where(widest > f, 1, 0).astype(jnp.int32) for f in sizes[:-1])


def sweep_kernel(
    dims, plan, val, cot_hbm, tiles_hbm, util, taste, value_ref, adj_ref, retn, retf, gu_ref, gt_ref, *rest
):
    B, A, M, R, V, H, D, T, cap, FX, F, G, rows = dims
    f32, bf16 = jnp.float32, jnp.bfloat16
    E, C, CH = B * A * M, cap // 2, 2
    tables, rest = rest[:H], rest[H:]
    (own, stn, stx, tiles, cot, scaled, P, bst, rel, acc, fold, gacc, gtac, lu, lt,
     lsem, sn, rn, sx, rx, sf, bsn, brn, bsx, brel, brx, usem, ursem, tsem, trsem) = rest
    z, t = lax.axis_index("state"), lax.axis_index("type")
    side = lax.div(z, 2)
    spot = lax.rem(z, 2)
    peer = 2 * side + 1 - spot
    gate_to = D // 2 - side
    is_gate = (z == D // 2 - 1) | (z == D // 2)
    is_end = jnp.logical_not(is_gate)
    far0 = 2 * (1 - side)
    tail = [C] if F > cap else []

    def span(c):
        return pl.ds(cap, F - cap) if isinstance(c, int) and c == C else pl.ds(c * CH, CH)

    def remote(src, dst, s, r, device):
        return pltpu.make_async_remote_copy(
            src_ref=src, dst_ref=dst, send_sem=s, recv_sem=r, device_id={"state": device}, device_id_type=MESH
        )

    def shift(c, base):
        s = span(c)
        return pl.ds(base + s.start, s.size)

    def fwd_near(h):
        return remote(stn.at[h], tables[h].at[pl.ds(B, cap)], sn.at[h], rn.at[h], peer)

    def fwd_far(h, c, x):
        return remote(
            stx.at[h, span(c)], tables[h].at[shift(c, B + cap + x * FX)], sx.at[h, c], rx.at[h, x, c], gate_to
        )

    def fwd_pass(h, x, c):
        part = tables[h].at[shift(c, B + cap + x * FX)]
        return remote(part, part, sf.at[h, x, c], rx.at[h, x, c], peer)

    def bwd_near(h):
        return remote(bst.at[h, pl.ds(0, cap)], retn.at[:, :, cols(h)], bsn.at[h], brn.at[h], peer)

    def bwd_far(h, x, c):
        return remote(
            bst.at[h, shift(c, cap + x * FX)], retf.at[span(c), :, cols(h)], bsx.at[h, x, c], brx.at[h, c], far0 + x
        )

    def bwd_end(h, x, c):
        return remote(
            bst.at[h, shift(c, cap + x * FX)], rel.at[h, x, span(c)], bsx.at[h, x, c], brel.at[h, x, c], peer
        )

    def cols(h):
        return pl.ds(h * V, V)

    own_copy = pltpu.make_async_copy(val, own, lsem.at[0])
    own_copy.start()
    fills = [
        pltpu.make_async_copy(val.at[:, :, cols(h)], tables[h].at[pl.ds(0, B)], lsem.at[1 + h]) for h in range(H)
    ]
    fills[0].start()
    tile_copy = pltpu.make_async_copy(tiles_hbm, tiles, lsem.at[1 + H])
    cot_copy = pltpu.make_async_copy(cot_hbm, cot, lsem.at[2 + H])
    barrier = pltpu.get_barrier_semaphore()
    for k in range(1, D):
        pl.semaphore_signal(barrier, inc=1, device_id={"state": lax.rem(z + k, D)}, device_id_type=MESH)
    for k in range(1, T):
        pl.semaphore_signal(barrier, inc=1, device_id={"type": lax.rem(t + k, T)}, device_id_type=MESH)
    own_copy.wait()
    for h in range(H):
        for s in range(F):
            stx[h, s] = own[plan[3, 16 + s], :, h * V : (h + 1) * V]
        for s in range(cap):
            stn[h, s] = own[plan[3, s], :, h * V : (h + 1) * V]
        if h == 0:
            pl.semaphore_wait(barrier, D - 1 + T - 1)
        for c in list(range(C)) + tail:
            fwd_far(h, c, spot).start()
        fwd_near(h).start()
        if h == 0:
            tile_copy.start()
            cot_copy.start()
            for f in fills[1:]:
                f.start()
    P[0] = jnp.zeros((R, V), f32)
    gtac[...] = jnp.zeros(gtac.shape, f32)

    def pass_on(h, c):
        @pl.when(is_gate)
        def _():
            for x in range(2):
                fwd_far(h, c, x).wait_recv()
                fwd_pass(h, x, c).start()

    def arrived(h):
        fwd_near(h).wait_recv()

        @pl.when(is_gate)
        def _():
            for x in range(2):
                for c in tail:
                    fwd_far(h, c, x).wait_recv()

        @pl.when(is_end)
        def _():
            for x in range(2):
                for c in range(C):
                    fwd_far(h, c, x).wait_recv()

    def values(h, hook):
        t0, t1 = taste[0:1, h * V : (h + 1) * V], taste[1:2, h * V : (h + 1) * V]

        def step(k, carry):
            for g in range(G):
                i = k * G + g
                for a in range(A):
                    weights, blocks = [], []
                    for n in range(M):
                        e = (i * A + a) * M + n
                        row = plan[0, e]
                        keep = jnp.where(row > 0, 1.0, 0.0).astype(f32)
                        tile = tiles[e]
                        weights.append(tile * jnp.full(tile.shape, keep, f32).astype(bf16))
                        blocks.append(tables[h][jnp.maximum(row - 1, 0)])
                    acc[g, a] = jnp.dot(
                        jnp.concatenate(weights, axis=1), jnp.concatenate(blocks, axis=0),
                        preferred_element_type=f32,
                    )
            for g in range(G):
                i = k * G + g
                lanes = pl.ds(pl.multiple_of(i * R, R), R)
                base = [jnp.transpose(jnp.broadcast_to(util[a : a + 1, lanes], (R, R))) for a in range(A)]
                g0 = g1 = 0.0
                for c in range(0, R, rows):
                    at = slice(c, c + rows)
                    here = pl.ds(pl.multiple_of(i * R + c, rows), rows)
                    q0 = base[0][at, 0:1] + t0 + 0.95 * acc[g, 0, at, :]
                    q1 = base[1][at, 0:1] + t1 + 0.95 * acc[g, 1, at, :]
                    gap = q1 - q0
                    small = jnp.exp(-jnp.abs(gap))
                    total = 1.0 + small
                    value_ref[here, h * V : (h + 1) * V] = jnp.maximum(q0, q1) + jnp.log(total)
                    big = cot[here, h * V : (h + 1) * V].astype(f32) / total
                    little = big * small
                    first_wins = gap <= 0.0
                    h0 = jnp.where(first_wins, big, little)
                    h1 = jnp.where(first_wins, little, big)
                    scaled[i * A, at, :] = (0.95 * h0).astype(bf16)
                    scaled[i * A + 1, at, :] = (0.95 * h1).astype(bf16)
                    fold[0, at, :] = sum(h0[:, w : w + 128] for w in range(0, V, 128))
                    fold[1, at, :] = sum(h1[:, w : w + 128] for w in range(0, V, 128))
                    g0, g1 = g0 + h0, g1 + h1
                for a in range(A):
                    line = jnp.sum(jnp.transpose(fold[a]), axis=0, keepdims=True)
                    gacc[a : a + 1, lanes] = line if h == 0 else gacc[a : a + 1, lanes] + line
                gtac[0:1, h * V : (h + 1) * V] += jnp.sum(g0, axis=0, keepdims=True)
                gtac[1:2, h * V : (h + 1) * V] += jnp.sum(g1, axis=0, keepdims=True)
            hook(k)
            return carry

        lax.fori_loop(0, B // G, step, 0)

    def back(lo, hi):
        def step(k, carry):
            for u in range(B):
                e = plan[1, k * B + u]
                P[k * B + u + 1] = P[plan[2, k * B + u]] + transposed_dot(tiles[e], scaled[lax.div(e, M)])
            return carry

        lax.fori_loop(lo, hi, step, 0)

    def stage(h, s):
        bst[h, s] = P[plan[3, 64 + B + s]].astype(bf16)

    def give(h):
        @pl.when(is_end)
        def _():
            for c in range(C):
                for x in range(2):
                    for s in range(c * CH, (c + 1) * CH):
                        stage(h, cap + x * FX + s)
                if c > 0:
                    for x in range(2):
                        bwd_end(h, x, c - 1).start()

        @pl.when(is_gate)
        def _():
            for x in range(2):
                for s in range(cap, F):
                    stage(h, cap + x * FX + s)

        for s in range(cap):
            stage(h, s)

        @pl.when(is_end)
        def _():
            for x in range(2):
                bwd_end(h, x, C - 1).start()

        @pl.when(is_gate)
        def _():
            for x in range(2):
                for c in tail:
                    bwd_far(h, x, c).start()

        bwd_near(h).start()

    def add_on(h, c):
        @pl.when(is_gate)
        def _():
            for x in range(2):
                bwd_end(h, x, c).wait_recv()
                for s in range(CH):
                    u = c * CH + s
                    term = P[plan[3, 64 + B + cap + x * FX + u]] + rel[h, x, u].astype(f32)
                    bst[h, cap + x * FX + u] = term.astype(bf16)
            for x in range(2):
                bwd_far(h, x, c).start()

    def keep(h):
        def step(k, carry):
            for g in range(G):
                adj_ref[k * G + g, :, h * V : (h + 1) * V] = P[plan[3, 64 + k * G + g]]
            return carry

        lax.fori_loop(0, B // G, step, 0)

    def sums():
        out = []
        for k in range(1, T):
            out.append(
                pltpu.make_async_remote_copy(
                    src_ref=gacc, dst_ref=lu.at[k], send_sem=usem.at[k], recv_sem=ursem.at[k],
                    device_id={"type": lax.rem(t + k, T)}, device_id_type=MESH,
                )
            )
        for k in range(1, D):
            out.append(remote(gtac, lt.at[k], tsem.at[k], trsem.at[k], lax.rem(z + k, D)))
        return out

    for c in range(C):
        pass_on(0, c)
    fills[0].wait()
    arrived(0)
    tile_copy.wait()
    cot_copy.wait()
    for h in range(H):
        steps = B // G

        def hook(k, h=h):
            @pl.when(k < C)
            def _():
                if h + 1 < H:
                    pass_on(h + 1, k)
                if h > 0:
                    add_on(h - 1, k)

        if h > 0:
            fills[h].wait()
            arrived(h)
        values(h, hook)
        back(0, 1)
        give(h)
        if h == H - 1:
            for c in sums():
                c.start()
        back(1, E // B)
        keep(h)
    for c in range(C):
        add_on(H - 1, c)
    for c in sums():
        c.wait()
    lu[0] = gacc[...]
    lt[0] = gtac[...]
    u = lu[lax.rem(t, T)]
    for j in range(1, T):
        u = u + lu[lax.rem(t - j + T, T)]
    w = lt[lax.rem(z, D)]
    for j in range(1, D):
        w = w + lt[lax.rem(z - j + D, D)]
    gu_ref[...] = u / (H * V * T)
    gt_ref[...] = w / (B * R * D)
    for h in range(H):
        fwd_near(h).wait_send()
        bwd_near(h).wait()
        for c in list(range(C)) + tail:
            fwd_far(h, c, spot).wait_send()
            bwd_far(h, 0, c).wait_recv()

        @pl.when(is_gate)
        def _(h=h):
            for x in range(2):
                for c in range(C):
                    fwd_pass(h, x, c).wait_send()
                for c in list(range(C)) + tail:
                    bwd_far(h, x, c).wait_send()

        @pl.when(is_end)
        def _(h=h):
            for x in range(2):
                for c in range(C):
                    bwd_end(h, x, c).wait_send()


def folded(value_in, cotangent, state_util, taste, tiles, dest_block, counts):
    B, A, M, R, _ = tiles.shape
    W = value_in.shape[1]
    D, T = lax.axis_size("state"), lax.axis_size("type")
    Q = lax.axis_size("groups") * D
    cap = (B + D - 2) // (D - 1)
    E, FX, H, G = B * A * M, 2 * cap, 2, 4
    V = W // H
    f32, bf16, i32 = jnp.float32, jnp.bfloat16, jnp.int32
    shape, DMA = jax.ShapeDtypeStruct, pltpu.SemaphoreType.DMA
    vmem = pl.BlockSpec(memory_space=VMEM)
    hbm = pl.BlockSpec(memory_space=pl.ANY)

    sizes = sorted({cap + (cap + 1) // 2, cap + (2 * cap + 2) // 3, FX - 1, FX})
    plan, pick = pl.pallas_call(
        functools.partial(meet_kernel, (B, A, M, D, cap, Q), sizes),
        out_shape=(shape((8, 256), i32), shape((1,), i32)),
        in_specs=[vmem] * 2,
        out_specs=[vmem, smem()],
        scratch_shapes=[VMEM((128, 128), f32), VMEM((Q, 8, 128), f32), VMEM((256, 128), f32), DMA((Q,)), DMA((Q,))],
        compiler_params=pltpu.CompilerParams(collective_id=0, has_side_effects=True),
        name="meet",
    )(dest_block.transpose(2, 1, 0), counts.T)

    def sweep(F, ident):
        dims = (B, A, M, R, V, H, D, T, cap, FX, F, G, 32)
        C = cap // 2
        return pl.pallas_call(
            functools.partial(sweep_kernel, dims),
            out_shape=(
                VMEM((B * R, W), f32), VMEM((B, R, W), f32), VMEM((cap, R, W), bf16), VMEM((FX, R, W), bf16),
                VMEM((A, B * R), f32), VMEM((A, W), f32),
            ),
            in_specs=[smem(), hbm, hbm, hbm, vmem, vmem],
            out_specs=[vmem] * 6,
            scratch_shapes=[VMEM((B + cap + 2 * FX, R, V), bf16)] * H
            + [
                VMEM((B, R, W), bf16), VMEM((H, cap, R, V), bf16), VMEM((H, FX, R, V), bf16),
                VMEM((E, R, R), bf16), VMEM((B * R, W), bf16),
                VMEM((B * A, R, V), bf16), VMEM((E + 1, R, V), f32), VMEM((H, cap + 2 * FX, R, V), bf16),
                VMEM((H, 2, cap, R, V), bf16), VMEM((G, A, R, V), f32),
                VMEM((A, R, 128), f32), VMEM((A, B * R), f32), VMEM((A, W), f32),
                VMEM((T, A, B * R), f32), VMEM((D, A, W), f32),
                DMA((3 + H,)), DMA((H,)), DMA((H,)),
                DMA((H, C + 1)), DMA((H, 2, C + 1)), DMA((H, 2, C)), DMA((H,)), DMA((H,)),
                DMA((H, 2, C + 1)), DMA((H, 2, C)), DMA((H, C + 1)),
                DMA((T,)), DMA((T,)), DMA((D,)), DMA((D,)),
            ],
            compiler_params=pltpu.CompilerParams(
                collective_id=ident, has_side_effects=True, vmem_limit_bytes=55_000_000
            ),
            cost_estimate=pl.CostEstimate(flops=4 * E * R * R * W, bytes_accessed=20 << 20, transcendentals=3 * B * R * W),
            name="sweep%d" % F,
        )

    def branch(F, ident):
        def run(plan, *args):
            held = sweep(F, ident)(plan, *args)
            held = [pltpu.with_memory_space_constraint(v, VMEM) for v in held]
            return pl.pallas_call(
                functools.partial(finish_kernel, G),
                in_specs=[smem()] + [vmem] * 6,
                out_specs=[hbm, hbm, vmem, vmem],
                out_shape=[shape(held[k].shape, f32) for k in (0, 1, 4, 5)],
                scratch_shapes=[VMEM((B, R, W), f32), DMA((B // G,)), DMA((B // G,))],
                compiler_params=pltpu.CompilerParams(vmem_limit_bytes=5 << 20),
                name="finish",
            )(plan, *held)

        return run

    value, adjoint, grad_util, grad_taste = lax.switch(
        pick.reshape(()), [branch(f, 1 + k) for k, f in enumerate(sizes)],
        plan, value_in.reshape(B, R, W), cotangent, tiles.reshape(E, R, R), state_util, taste,
    )
    return value, adjoint.reshape(B * R, W), grad_util, grad_taste


def finish_kernel(G, plan, held, part, near_ref, far_ref, gu_ref, gt_ref, value, adjoint, gu, gt, total, vsem, asem):
    f32 = jnp.float32
    B, R, _ = part.shape
    steps = range(B // G)
    outs = []
    for k in steps:
        rows = pl.ds(k * G * R, G * R)
        outs.append(pltpu.make_async_copy(held.at[rows], value.at[rows], vsem.at[k]))
        outs[-1].start()
    gu[...] = gu_ref[...]
    gt[...] = gt_ref[...]
    for k in steps:
        for j in range(k * G, (k + 1) * G):
            near, far = plan[3, 32 + j], plan[3, 48 + j]
            add = jnp.where(near > 0, near_ref[jnp.maximum(near - 1, 0)].astype(f32), 0.0)
            total[j] = part[j] + add + jnp.where(far > 0, far_ref[jnp.maximum(far - 1, 0)].astype(f32), 0.0)
        blocks = pl.ds(k * G, G)
        outs.append(pltpu.make_async_copy(total.at[blocks], adjoint.at[blocks], asem.at[k]))
        outs[-1].start()
    for c in outs:
        c.wait()


def choose(*args):
    B, A, M, R, _ = args[4].shape
    D = lax.axis_size("state")
    cap = (B + D - 2) // (D - 1)
    fits = D * B <= 128 and 128 < B * A * M <= 256 and cap % 2 == 0 and B % 4 == 0 and R == 128
    if D == 4 and fits and args[0].shape[1] % 256 == 0:
        return folded(*args)
    return local(*args)


def solution(mesh):
    rows = ("groups", "state")
    return jax.shard_map(
        choose,
        mesh=mesh,
        in_specs=(
            P(rows, "type"),
            P(rows, "type"),
            P(None, rows),
            P(None, ("groups", "type")),
            P(rows, None, None, None, None),
            P(rows, None, None),
            P(rows, None),
        ),
        out_specs=(P(rows, "type"), P(rows, "type"), P(None, rows), P(None, ("groups", "type"))),
        check_vma=False,
    )
```
